32 devices in a mesh: seq: 8 (over z, y), head: 4 (over x, core).
Axes of the slice: x: 2, y: 2, z: 4, core: 2. Of those that a mesh axis runs over, the one named last changes fastest.
Arguments:
- inputs: bfloat16 [2, 1024, 768], P(None, 'seq'), may hold values from -6 to 6
- cotangent: float32 [2, 1024, 768], P(None, 'seq'), may hold values from -6 to 6
- lengths: int32 [2], replicated, may hold values from 256 to 1024, as said below
- ln1_gain: float32 [768], replicated, may hold values from 0.5 to 1.5
- ln1_bias: float32 [768], replicated, may hold values from -3 to 3
- query_key_value_weight: bfloat16 [3, 768, 768], P(None, None, 'head'), may hold values from -0.21875 to 0.21875
- b_qkv: float32 [3, 768], P(None, 'head'), may hold values from -3 to 3
- shift_taps: float32 [64, 768], P(None, 'head'), may hold values from -2.5 to 2.5
- shift_skip: float32 [768], P('head'), may hold values from -4 to 4
- ssm_a: float32 [768, 64], P('head'), as said below
- ssm_b: float32 [768, 64], P('head'), may hold values from -4 to 4
- ssm_c: float32 [768, 64], P('head'), may hold values from -0.75 to 0.75
- ssm_skip: float32 [768], P('head'), may hold values from -3 to 3
- ssm_step: float32 [768], P('head'), may hold values from 0.5 to 2
- output_weight: bfloat16 [768, 768], P('head'), may hold values from -0.21875 to 0.21875
- b_out: float32 [768], replicated, may hold values from -3 to 3
- ln2_gain: float32 [768], replicated, may hold values from 0.5 to 1.5
- ln2_bias: float32 [768], replicated, may hold values from -3 to 3
- up_weight: bfloat16 [768, 3072], P(None, 'head'), may hold values from -0.21875 to 0.21875
- up_bias: float32 [3072], P('head'), may hold values from -3 to 3
- down_weight: bfloat16 [3072, 768], P('head'), may hold values from -0.109375 to 0.109375
- b_down: float32 [768], replicated, may hold values from -3 to 3
Outputs:
- layer_out: float32 [2, 1024, 768], P(None, 'seq')
- grad_inputs: float32 [2, 1024, 768], P(None, 'seq')
- grad_ln1_gain: float32 [768], replicated
- grad_ln1_bias: float32 [768], replicated
- grad_w_qkv: float32 [3, 768, 768], P(None, None, 'head')
- grad_b_qkv: float32 [3, 768], P(None, 'head')
- grad_shift_taps: float32 [64, 768], P(None, 'head')
- grad_shift_skip: float32 [768], P('head')
- grad_ssm_a: float32 [768, 64], P('head')
- grad_ssm_b: float32 [768, 64], P('head')
- grad_ssm_c: float32 [768, 64], P('head')
- grad_ssm_skip: float32 [768], P('head')
- grad_ssm_step: float32 [768], P('head')
- grad_w_out: float32 [768, 768], P('head')
- grad_b_out: float32 [768], replicated
- grad_ln2_gain: float32 [768], replicated
- grad_ln2_bias: float32 [768], replicated
- up_weight_gradient: float32 [768, 3072], P(None, 'head')
- grad_b_up: float32 [3072], P('head')
- grad_w_down: float32 [3072, 768], P('head')
- grad_b_down: float32 [768], replicated
The draws below stay inside these ranges and needn't reach their ends.
Inputs may be any that keep to these rules, and one draw needn't show every extreme that they name: `lengths`: every slot's valid tokens come first; one slot in every draw has all 1024 tokens valid. `ssm_a`: positive.
All inputs are finite; a program needn't handle non-finite values.
Results may differ from the reference program's by a relative error of at most 0.02.
Values may be sent and summed in bfloat16 or wider, within the bound.
No kernel may reach another device: no remote copies, remote signals or barrier semaphores. Data moves between devices by JAX's collectives and lax.ppermute only.
A program may use at most 128 MiB of HBM per device.

```python
import math
import jax
import jax.numpy as jnp
from jax import lax

D = 768
FF = 3072
NST = 64
SHIFT = 64
SLOTS = 2
TOK_DEV = 128
LEN = 1024
N_SEQ = 8
N_HEAD = 4


def draw_lengths(key, part):
    key_lengths, key_longest = jax.random.split(jax.random.fold_in(key, 11))
    picked = jax.random.randint(key_lengths, (SLOTS,), LEN // 4, LEN)
    longest = jax.random.randint(key_longest, (), 0, SLOTS)
    return jnp.where(jnp.arange(SLOTS) == longest, LEN, picked).astype(jnp.int32)


def draw_ssm_a(key, part):
    lowest = math.log(0.05 / LEN)
    upper = math.log(1.0 / 32.0)
    fraction = jax.random.uniform(jax.random.fold_in(key, 23), (D, NST), jnp.float32)
    return jnp.exp(lowest + (upper - lowest) * fraction).astype(jnp.float32)


def block_levels(key, extent, cuts, low, high):
    def one(dim, shards_of):
        steps = jax.random.uniform(jax.random.fold_in(jax.random.fold_in(key, 6), dim), (shards_of,), jnp.float32, low / len(cuts), high / len(cuts))
        return jnp.repeat(jnp.exp(steps), extent[dim] // shards_of).reshape((-1,) + (1,) * (len(extent) - dim - 1))

    factor_of = one(*cuts[0])
    for cut in cuts[1:]:
        factor_of = factor_of * one(*cut)
    return factor_of


def bell_draw(key, shape, width, bound, cuts=(), held_as=jnp.bfloat16):
    factor_of = block_levels(key, shape, cuts, -0.22, 0.18) if cuts else 1.0
    values = jax.random.normal(key, shape, jnp.float32) * width * factor_of
    return jnp.minimum(jnp.maximum(values, -bound), bound).astype(held_as)


def setup_inputs(seed: int = 0) -> dict:
    arg_keys = jax.random.split(jax.random.key(seed), 23)
    return {
        "inputs": bell_draw(arg_keys[0], (SLOTS, LEN, D), 1.0, 6.0, ((1, 8),)),
        "cotangent": bell_draw(arg_keys[1], (SLOTS, LEN, D), 1.0, 6.0, ((1, 8),), jnp.float32),
        "lengths": draw_lengths(jax.random.fold_in(arg_keys[22], 71), 0),
        "ln1_gain": jnp.clip(1.0 + 0.1 * jax.random.normal(arg_keys[3], (D,), jnp.float32), 0.5, 1.5),
        "ln1_bias": bell_draw(arg_keys[4], (D,), 0.3, 3.0, (), jnp.float32),
        "query_key_value_weight": bell_draw(arg_keys[5], (3, D, D), D ** -0.5, 0.21875, ((2, 4),)),
        "b_qkv": bell_draw(arg_keys[6], (3, D), 0.3, 3.0, ((1, 4),), jnp.float32),
        "shift_taps": bell_draw(arg_keys[7], (SHIFT, D), 0.4, 2.5, ((1, 4),), jnp.float32),
        "shift_skip": bell_draw(arg_keys[8], (D,), 1.0, 4.0, ((0, 4),), jnp.float32),
        "ssm_a": draw_ssm_a(jax.random.fold_in(arg_keys[22], 71), 0),
        "ssm_b": bell_draw(arg_keys[10], (D, NST), 1.0, 4.0, ((0, 4),), jnp.float32),
        "ssm_c": bell_draw(arg_keys[11], (D, NST), NST ** -0.5, 0.75, ((0, 4),), jnp.float32),
        "ssm_skip": bell_draw(arg_keys[12], (D,), 0.5, 3.0, ((0, 4),), jnp.float32),
        "ssm_step": jnp.clip(jnp.exp(math.log(2.0) - 1.3862944 * jax.random.uniform(arg_keys[13], (D,), jnp.float32) ** block_levels(arg_keys[13], (D,), ((0, 4),), -0.2, 0.2)), 0.5, 2.0),
        "output_weight": bell_draw(arg_keys[14], (D, D), D ** -0.5, 0.21875, ((0, 4),)),
        "b_out": bell_draw(arg_keys[15], (D,), 0.3, 3.0, (), jnp.float32),
        "ln2_gain": jnp.clip(1.0 + 0.1 * jax.random.normal(arg_keys[16], (D,), jnp.float32), 0.5, 1.5),
        "ln2_bias": bell_draw(arg_keys[17], (D,), 0.3, 3.0, (), jnp.float32),
        "up_weight": bell_draw(arg_keys[18], (D, FF), D ** -0.5, 0.21875, ((1, 4),)),
        "up_bias": bell_draw(arg_keys[19], (FF,), 0.3, 3.0, ((0, 4),), jnp.float32),
        "down_weight": bell_draw(arg_keys[20], (FF, D), FF ** -0.5, 0.109375, ((0, 4),)),
        "b_down": bell_draw(arg_keys[21], (D,), 0.3, 3.0, (), jnp.float32),
    }


highest = lax.Precision.HIGHEST
norm_epsilon = 1e-05

@jax.custom_vjp
def low(v):
    return lax.optimization_barrier(v.astype(jnp.bfloat16)).astype(jnp.float32)

@jax.custom_vjp
def low_back(v):
    return v

def low_keep(v):
    return (low(v), None)

def low_pass(kept, grad):
    return (grad,)

def back_keep(v):
    return (v, None)

def back_low(kept, grad):
    return (low(grad),)
low.defvjp(low_keep, low_pass)
low_back.defvjp(back_keep, back_low)

def layer_norm(rows_in, norm_gain, norm_bias):
    mean_val = lax.optimization_barrier(jnp.mean(rows_in, axis=-1, keepdims=True))
    centred = rows_in - mean_val
    spread = lax.optimization_barrier(jnp.mean(centred * centred, axis=-1, keepdims=True))
    return centred * lax.rsqrt(spread + norm_epsilon) * norm_gain + norm_bias

def shift_mix(extended, values, shift_taps, shift_skip):
    filters = jnp.concatenate([shift_taps[::-1], shift_skip[None]], axis=0)[:, None, :]
    shifted = lax.conv_general_dilated(extended, filters, (1,), 'VALID', dimension_numbers=('NWC', 'WIO', 'NWC'), feature_group_count=extended.shape[2], precision=highest)
    return shifted * values

def ssm_kernel(decay_rate, weight_c):
    starts = jnp.arange(N_SEQ, dtype=jnp.int32) * TOK_DEV

    def one_block(start):
        offsets = (start + jnp.arange(TOK_DEV, dtype=jnp.int32)).astype(jnp.float32)
        powers = jnp.exp(-offsets[:, None, None] * decay_rate[None])
        return lax.optimization_barrier(jnp.sum(powers * weight_c[None], axis=-1))
    blocks = lax.map(jax.checkpoint(one_block), starts)
    return blocks.reshape(LEN, D)

def long_conv(series, kernel):
    length_two = 2 * LEN
    spectrum = jnp.fft.rfft(series, n=length_two, axis=1) * jnp.fft.rfft(kernel, n=length_two, axis=0)[None]
    return jnp.fft.irfft(spectrum, n=length_two, axis=1)[:, :LEN]

def forward(inputs, ln1_gain, ln1_bias, query_key_value_weight, b_qkv, shift_taps, shift_skip, ssm_a, ssm_b, ssm_c, ssm_skip, ssm_step, output_weight, b_out, ln2_gain, ln2_bias, up_weight, up_bias, down_weight, b_down, valid_rows):
    group_width = D // N_HEAD
    hidden_cols = FF // N_HEAD
    normed = low(layer_norm(inputs, ln1_gain, ln1_bias))
    copies = low_back(jnp.broadcast_to(normed[None], (N_HEAD,) + normed.shape))
    grouped = query_key_value_weight.reshape(3, D, N_HEAD, group_width)
    projected = jnp.einsum('gsld,jdgc->jslgc', copies, grouped, precision=highest).reshape(3, SLOTS, LEN, D)
    projected = low_back(projected + b_qkv[:, None, None, :])
    queries = projected[0]
    keys_low = low(projected[1])
    values = projected[2]
    extended = jnp.pad(keys_low, ((0, 0), (SHIFT, 0), (0, 0)))
    mixed_u = shift_mix(extended, values, shift_taps, shift_skip)
    decay_rate = ssm_step[:, None] * ssm_a
    weight_c = ssm_c * jnp.sqrt(-jnp.expm1(-2.0 * decay_rate)) * ssm_b
    kernel = ssm_kernel(decay_rate, weight_c)
    ssm_out = long_conv(mixed_u, kernel) + ssm_skip * mixed_u
    gated_mixture = low(queries * ssm_out)
    partials = jnp.einsum('slgc,gcd->gsld', gated_mixture.reshape(SLOTS, LEN, N_HEAD, group_width), output_weight.reshape(N_HEAD, group_width, D), precision=highest)
    attended = low_back(lax.optimization_barrier(jnp.sum(low(partials), axis=0))) + b_out
    middle = inputs + attended
    normed_two = low(layer_norm(middle, ln2_gain, ln2_bias))
    copies_two = low_back(jnp.broadcast_to(normed_two[None], (N_HEAD,) + normed_two.shape))
    up_projected = jnp.einsum('gsld,dgf->slgf', copies_two, up_weight.reshape(D, N_HEAD, hidden_cols), precision=highest).reshape(SLOTS, LEN, FF)
    up_projected = low_back(up_projected + up_bias)
    hidden_activations = low(jax.nn.gelu(up_projected, approximate=True))
    partials_two = jnp.einsum('slgf,gfd->gsld', hidden_activations.reshape(SLOTS, LEN, N_HEAD, hidden_cols), down_weight.reshape(N_HEAD, hidden_cols, D), precision=highest)
    feed_out = low_back(lax.optimization_barrier(jnp.sum(low(partials_two), axis=0))) + b_down
    return valid_rows * (middle + feed_out)

def reference(inputs, cotangent, lengths, ln1_gain, ln1_bias, query_key_value_weight, b_qkv, shift_taps, shift_skip, ssm_a, ssm_b, ssm_c, ssm_skip, ssm_step, output_weight, b_out, ln2_gain, ln2_bias, up_weight, up_bias, down_weight, b_down):
    places = jnp.arange(LEN, dtype=jnp.int32)
    valid_rows = (places[None, :] < lengths[:, None]).astype(jnp.float32)[:, :, None]
    floats = [inputs.astype(jnp.float32), ln1_gain, ln1_bias, query_key_value_weight.astype(jnp.float32), b_qkv, shift_taps, shift_skip, ssm_a, ssm_b, ssm_c, ssm_skip, ssm_step, output_weight.astype(jnp.float32), b_out, ln2_gain, ln2_bias, up_weight.astype(jnp.float32), up_bias, down_weight.astype(jnp.float32), b_down]

    def closed(*params):
        return forward(*params, valid_rows)
    layer_out, undo = jax.vjp(closed, *floats)
    grads = undo(cotangent)
    return (layer_out, grads[0], grads[1], grads[2], grads[3], grads[4], grads[5], grads[6], grads[7], grads[8], grads[9], grads[10], grads[11], grads[12], grads[13], grads[14], grads[15], grads[16], grads[17], grads[18], grads[19])
```

```python
import functools

import jax
import jax.numpy as jnp
from jax import lax
from jax.experimental import pallas as pl
from jax.experimental.pallas import tpu as pltpu
from jax.sharding import PartitionSpec as P

highest = lax.Precision.HIGHEST
norm_epsilon = 1e-05


f32 = jnp.float32
bf16 = jnp.bfloat16
LANES = 128
SUBS = 8


def shifted(shard, axis, by):
    peers = lax.axis_size(axis)
    return lax.ppermute(shard, axis, [(i, i + by) for i in range(peers) if 0 <= i + by < peers])


def swapped(shard, axis, mask):
    return lax.ppermute(shard, axis, [(i, i ^ mask) for i in range(lax.axis_size(axis))])


def pick(pair, index):
    return lax.dynamic_index_in_dim(pair, index, 0, False)


def head_sum(part, axis="head"):
    peers = lax.axis_size(axis)
    if peers & (peers - 1) or peers < 2 or part.shape[0] % 2:
        return lax.psum(part.astype(f32), axis)
    place = lax.axis_index(axis)
    low_bit = place % 2
    halves = part.reshape((2, part.shape[0] // 2) + part.shape[1:])
    total = pick(halves, low_bit).astype(f32) + swapped(pick(halves, 1 - low_bit), axis, 1).astype(f32)
    mask = 2
    while mask < peers:
        total = total + swapped(total.astype(bf16), axis, mask).astype(f32)
        mask *= 2
    own = total.astype(bf16)
    other = swapped(own, axis, 1)
    first = jnp.where(low_bit == 0, own, other)
    second = jnp.where(low_bit == 0, other, own)
    return jnp.concatenate([first, second], axis=0).astype(f32)


def halving_sum(block, axis, masks):
    place = lax.axis_index(axis)
    for mask in masks:
        bit = (place // mask) % 2
        halves = block.reshape((2, block.shape[0] // 2) + block.shape[1:])
        got = swapped(pick(halves, 1 - bit), axis, mask)
        block = (pick(halves, bit).astype(f32) + got.astype(f32)).astype(bf16)
    for mask in masks[::-1]:
        bit = (place // mask) % 2
        got = swapped(block, axis, mask)
        first = jnp.where(bit == 0, block, got)
        second = jnp.where(bit == 0, got, block)
        block = jnp.concatenate([first, second], axis=0)
    return block


def seq_sums(first, second, axis="seq"):
    peers = lax.axis_size(axis)
    masks = []
    while 2 ** len(masks) < peers:
        masks.append(2 ** len(masks))
    other = masks[1::-1] + masks[2:] if len(masks) > 1 else masks
    return halving_sum(first, axis, masks), halving_sum(second, axis, other)


def carried_state(ends, whole, axis, ahead):
    peers = lax.axis_size(axis)
    way = -1 if ahead else 1
    if peers % 2 or peers > 8:
        state = shifted(ends.astype(bf16), axis, way).astype(f32)
        power, step = whole, 1
        while step < peers:
            state = state + power * shifted(state.astype(bf16), axis, way * step).astype(f32)
            power, step = power * power, step * 2
        return state
    inner = lax.axis_index(axis) % 2
    is_near = inner == (0 if ahead else 1)
    mate = swapped(ends.astype(bf16), axis, 1).astype(f32)
    far, near = jnp.where(is_near, mate, ends), jnp.where(is_near, ends, mate)
    pair = (near + whole * far).astype(bf16)
    square = whole * whole
    power = jnp.ones_like(whole)
    state = jnp.zeros_like(ends)
    for step in range(2, peers, 2):
        state = state + power * shifted(pair, axis, way * step).astype(f32)
        power = power * square
    return jnp.where(is_near, mate + whole * state, state)


def layer_norm(rows_in, norm_gain, norm_bias):
    mean_val = jnp.mean(rows_in, axis=-1, keepdims=True)
    centred = rows_in - mean_val
    spread = jnp.mean(centred * centred, axis=-1, keepdims=True)
    return centred * lax.rsqrt(spread + norm_epsilon) * norm_gain + norm_bias


def smooth_gate(values_in):
    return jax.nn.gelu(values_in, approximate=True)


def shift_mix(extended, values, shift_taps, shift_skip):
    filters = jnp.concatenate([shift_taps[::-1], shift_skip[None]], axis=0)[:, None, :]
    shifted = lax.conv_general_dilated(
        extended,
        filters,
        (1,),
        "VALID",
        dimension_numbers=("NWC", "WIO", "NWC"),
        feature_group_count=extended.shape[2],
        precision=highest,
    )
    return shifted * values


def lane_tiles(width):
    return [slice(i, i + LANES) for i in range(0, width, LANES)]


def folded(product):
    states, lanes = product.shape
    return jnp.sum(product.reshape(states // SUBS, SUBS, lanes), axis=0)


def end_kernel(reverse, series_ref, decay_ref, end_ref):
    rows = series_ref.shape[0]
    blocks = rows // SUBS
    for lanes in lane_tiles(series_ref.shape[1]):
        decay = decay_ref[:, lanes]

        def one(lap, state, lanes=lanes, decay=decay):
            place = blocks - 1 - lap if reverse else lap
            tile = series_ref[pl.ds(pl.multiple_of(place * SUBS, SUBS), SUBS), lanes]
            for r in range(SUBS):
                r = SUBS - 1 - r if reverse else r
                state = decay * state + tile[r : r + 1, :]
            return state

        end_ref[:, lanes] = lax.fori_loop(0, blocks, one, jnp.zeros_like(decay))


def forward_kernel(series_ref, decay_ref, weight_ref, start_ref, out_ref, part_ref):
    rows = series_ref.shape[0]
    blocks = rows // SUBS
    for lanes in lane_tiles(series_ref.shape[1]):
        decay = decay_ref[:, lanes]
        weight = weight_ref[:, lanes]

        def one(lap, state, lanes=lanes, decay=decay, weight=weight):
            tile = series_ref[pl.ds(pl.multiple_of(lap * SUBS, SUBS), SUBS), lanes]
            base = pl.multiple_of(lap * SUBS * SUBS, SUBS)
            for r in range(SUBS):
                state = decay * state + tile[r : r + 1, :]
                part_ref[pl.ds(base + r * SUBS, SUBS), :] = folded(weight * state)
            return state

        lax.fori_loop(0, blocks, one, start_ref[:, lanes])
        total = part_ref[pl.ds(0, rows, stride=SUBS), :]
        for r in range(1, SUBS):
            total = total + part_ref[pl.ds(r, rows, stride=SUBS), :]
        out_ref[:, lanes] = total


def backward_kernel(
    series_ref, grad_ref, decay_ref, weight_ref, start_ref, end_ref,
    out_ref, gain_ref, power_ref, part_ref, past_ref,
):
    rows = series_ref.shape[0]
    blocks = rows // SUBS
    states = decay_ref.shape[0]
    for lanes in lane_tiles(series_ref.shape[1]):
        decay = decay_ref[:, lanes]
        weight = weight_ref[:, lanes]

        def rise(lap, state, lanes=lanes, decay=decay):
            tile = series_ref[pl.ds(pl.multiple_of(lap * SUBS, SUBS), SUBS), lanes]
            base = pl.multiple_of(lap * SUBS * states, SUBS)
            for r in range(SUBS):
                past_ref[pl.ds(base + r * states, states), :] = state
                state = decay * state + tile[r : r + 1, :]
            return state

        lax.fori_loop(0, blocks, rise, start_ref[:, lanes])

        def fall(lap, carry, lanes=lanes, decay=decay, weight=weight):
            adjoint, gain, power = carry
            place = blocks - 1 - lap
            at = pl.ds(pl.multiple_of(place * SUBS, SUBS), SUBS)
            tile, grads = series_ref[at, lanes], grad_ref[at, lanes]
            base = pl.multiple_of(place * SUBS * SUBS, SUBS)
            far = pl.multiple_of(place * SUBS * states, SUBS)
            for r in range(SUBS - 1, -1, -1):
                adjoint = decay * adjoint + grads[r : r + 1, :]
                part_ref[pl.ds(base + r * SUBS, SUBS), :] = folded(weight * adjoint)
                gain = gain + adjoint * tile[r : r + 1, :]
                power = power + adjoint * past_ref[pl.ds(far + r * states, states), :]
            return adjoint, gain, power

        zero = jnp.zeros_like(decay)
        _, gain, power = lax.fori_loop(0, blocks, fall, (end_ref[:, lanes], zero, zero))
        gain_ref[:, lanes] = gain
        power_ref[:, lanes] = power
        total = part_ref[pl.ds(0, rows, stride=SUBS), :]
        for r in range(1, SUBS):
            total = total + part_ref[pl.ds(r, rows, stride=SUBS), :]
        out_ref[:, lanes] = total


def cost(flops, *arrays):
    size = sum(a.size * a.dtype.itemsize for a in arrays)
    return pl.CostEstimate(flops=flops, bytes_accessed=size, transcendentals=0)


def ssm_end(series, decay, reverse):
    rows, width = series.shape
    return pl.pallas_call(
        functools.partial(end_kernel, reverse),
        out_shape=jax.ShapeDtypeStruct(decay.shape, f32),
        compiler_params=pltpu.CompilerParams(vmem_limit_bytes=16 << 20),
        cost_estimate=cost(2 * rows * decay.size, series, decay),
    )(series, decay)


def ssm_forward(series, decay, weight, start):
    rows, width = series.shape
    return pl.pallas_call(
        forward_kernel,
        out_shape=jax.ShapeDtypeStruct(series.shape, f32),
        scratch_shapes=[pltpu.VMEM((rows * SUBS, LANES), f32)],
        compiler_params=pltpu.CompilerParams(vmem_limit_bytes=16 << 20),
        cost_estimate=cost(4 * rows * decay.size, series, decay, weight, start),
    )(series, decay, weight, start)


def ssm_backward(series, grads, decay, weight, start, end):
    rows, width = series.shape
    states = decay.shape[0]
    return pl.pallas_call(
        backward_kernel,
        out_shape=(
            jax.ShapeDtypeStruct(series.shape, f32),
            jax.ShapeDtypeStruct(decay.shape, f32),
            jax.ShapeDtypeStruct(decay.shape, f32),
        ),
        scratch_shapes=[
            pltpu.VMEM((rows * SUBS, LANES), f32),
            pltpu.VMEM((rows * states, LANES), f32),
        ],
        compiler_params=pltpu.CompilerParams(vmem_limit_bytes=24 << 20),
        cost_estimate=cost(10 * rows * decay.size, series, grads, decay, weight, start, end),
    )(series, grads, decay, weight, start, end)


def packed(array):
    return jnp.concatenate([array[s] for s in range(array.shape[0])], axis=-1)


def unpacked(array, slots):
    return jnp.stack(jnp.split(array, slots, axis=-1))


def shards(
    inputs,
    cotangent,
    lengths,
    ln1_gain,
    ln1_bias,
    query_key_value_weight,
    b_qkv,
    shift_taps,
    shift_skip,
    ssm_a,
    ssm_b,
    ssm_c,
    ssm_skip,
    ssm_step,
    output_weight,
    b_out,
    ln2_gain,
    ln2_bias,
    up_weight,
    up_bias,
    down_weight,
    b_down,
):
    slot_count, row_count, width_all = inputs.shape
    tap_count, chan_count = shift_taps.shape
    state_count = ssm_a.shape[1]
    places = lax.axis_index("seq") * row_count + jnp.arange(row_count, dtype=jnp.int32)
    valid_rows = (places[None, :] < lengths[:, None]).astype(jnp.float32)[:, :, None]
    residual_in = inputs.astype(jnp.float32)

    def repeated(array):
        return jnp.concatenate([array] * slot_count, axis=-1)

    rate = (ssm_step[:, None] * ssm_a).T
    decay = jnp.exp(-rate)
    gain_root = jnp.sqrt(-jnp.expm1(-2.0 * rate))
    in_weight = gain_root * ssm_b.T
    out_weight = ssm_c.T
    decay_wide = repeated(decay)
    whole_wide = repeated(jnp.exp(-rate * row_count))
    weight_wide = repeated(out_weight * in_weight)
    skip_wide = repeated(ssm_skip)

    normed_one, undo_one = jax.vjp(layer_norm, residual_in, ln1_gain, ln1_bias)
    first_activation = normed_one.astype(jnp.bfloat16)
    projected = (
        jnp.einsum(
            "vbg,tgi->tvbi",
            first_activation,
            query_key_value_weight,
            preferred_element_type=jnp.float32,
        )
        + b_qkv[:, None, None, :]
    )
    queries = projected[0]
    keys_low = projected[1].astype(jnp.bfloat16)
    values = projected[2]
    edge_rows = shifted(keys_low[:, row_count - tap_count :, :], "seq", 1)
    extended = jnp.concatenate([edge_rows, keys_low], axis=1).astype(jnp.float32)
    mixed_u, shift_undo = jax.vjp(shift_mix, extended, values, shift_taps, shift_skip)
    series = packed(mixed_u)
    end_local = ssm_end(series, decay_wide, False)
    start_state = carried_state(end_local, whole_wide, "seq", False)
    ssm_out = unpacked(
        ssm_forward(series, decay_wide, weight_wide, start_state) + skip_wide * series, slot_count
    )
    gated_mixture = (queries * ssm_out).astype(jnp.bfloat16)
    attention_terms = jnp.einsum(
        "upm,mq->upq", gated_mixture, output_weight, preferred_element_type=jnp.float32
    )
    attended = head_sum(attention_terms.astype(jnp.bfloat16)) + b_out
    middle = residual_in + attended
    normed_two, undo_two = jax.vjp(layer_norm, middle, ln2_gain, ln2_bias)
    second_activation = normed_two.astype(jnp.bfloat16)
    up_projected = (
        jnp.einsum("pwu,uj->pwj", second_activation, up_weight, preferred_element_type=jnp.float32)
        + up_bias
    )
    hidden_full, gelu_undo = jax.vjp(smooth_gate, up_projected)
    hidden_activations = hidden_full.astype(jnp.bfloat16)
    down_projection_terms = jnp.einsum(
        "jiq,qx->jix", hidden_activations, down_weight, preferred_element_type=jnp.float32
    )
    feed_out = head_sum(down_projection_terms.astype(jnp.bfloat16)) + b_down
    layer_out = valid_rows * (middle + feed_out)
    grad_out = cotangent * valid_rows
    grad_b_down = jnp.sum(grad_out, axis=(0, 1))
    output_lower_gradient = grad_out.astype(jnp.bfloat16)
    grad_w_down = jnp.einsum(
        "iqe,iqy->ey", hidden_activations, output_lower_gradient, preferred_element_type=jnp.float32
    )
    grad_hidden = jnp.einsum(
        "apo,io->api", output_lower_gradient, down_weight, preferred_element_type=jnp.float32
    )
    up_gradient = gelu_undo(grad_hidden)[0].astype(jnp.bfloat16)
    grad_b_up = jnp.sum(up_gradient.astype(jnp.float32), axis=(0, 1))
    up_weight_gradient = jnp.einsum(
        "bar,bak->rk", second_activation, up_gradient, preferred_element_type=jnp.float32
    )
    second_activation_terms = jnp.einsum(
        "hxe,ge->hxg", up_gradient, up_weight, preferred_element_type=jnp.float32
    )
    grad_act_two = head_sum(second_activation_terms.astype(jnp.bfloat16))
    grad_mid_norm, grad_ln2_gain, grad_ln2_bias = undo_two(grad_act_two)
    grad_middle = grad_out + grad_mid_norm
    sum_up, sum_down = seq_sums(up_weight_gradient.astype(bf16), grad_w_down.astype(bf16))
    grad_b_out = jnp.sum(grad_middle, axis=(0, 1))
    middle_lower_gradient = grad_middle.astype(jnp.bfloat16)
    grad_w_out = jnp.einsum(
        "hxq,hxe->qe", gated_mixture, middle_lower_gradient, preferred_element_type=jnp.float32
    )
    gated_gradient = jnp.einsum(
        "ihq,zq->ihz", middle_lower_gradient, output_weight, preferred_element_type=jnp.float32
    )
    grad_queries = gated_gradient * ssm_out
    grad_ssm = packed(gated_gradient * queries)
    front_local = ssm_end(grad_ssm, decay_wide, True)
    end_adjoint = carried_state(front_local, whole_wide, "seq", True)
    grad_series, gain_sum, power_sum = ssm_backward(
        series, grad_ssm, decay_wide, weight_wide, start_state, end_adjoint
    )
    grad_mixed_u = unpacked(grad_series + skip_wide * grad_ssm, slot_count)
    gain_sum = jnp.sum(gain_sum.reshape(state_count, slot_count, chan_count), axis=1)
    power_sum = jnp.sum(power_sum.reshape(state_count, slot_count, chan_count), axis=1)
    grad_ssm_c = in_weight * gain_sum
    grad_in_weight = out_weight * gain_sum
    grad_ssm_b = grad_in_weight * gain_root
    grad_rate = (
        grad_in_weight * ssm_b.T * jnp.exp(-2.0 * rate) / gain_root
        - decay * out_weight * in_weight * power_sum
    )
    grad_ssm_a = grad_rate * ssm_step
    grad_ssm_step = jnp.sum(grad_rate * ssm_a.T, axis=0)
    grad_ssm_skip = jnp.sum(
        jnp.sum(grad_ssm * series, axis=0).reshape(slot_count, chan_count), axis=0
    )
    grad_ext, grad_values, grad_shift_taps, grad_shift_skip = shift_undo(grad_mixed_u)
    received = shifted(grad_ext[:, :tap_count, :].astype(jnp.bfloat16), "seq", -1).astype(
        jnp.float32
    )
    grad_keys = grad_ext[:, tap_count:, :] + jnp.pad(
        received, ((0, 0), (row_count - tap_count, 0), (0, 0))
    )
    projected_gradient = jnp.stack([grad_queries, grad_keys, grad_values]).astype(jnp.bfloat16)
    grad_b_qkv = jnp.sum(projected_gradient.astype(jnp.float32), axis=(1, 2))
    grad_w_qkv = jnp.einsum(
        "quf,gquv->gvf", first_activation, projected_gradient, preferred_element_type=jnp.float32
    )
    act_one_terms = jnp.einsum(
        "znpu,zru->npr",
        projected_gradient,
        query_key_value_weight,
        preferred_element_type=jnp.float32,
    )
    grad_act_one = head_sum(act_one_terms.astype(jnp.bfloat16))
    grad_in_norm, grad_ln1_gain, grad_ln1_bias = undo_one(grad_act_one)
    grad_inputs = grad_middle + grad_in_norm

    small = [
        grad_ln1_gain,
        grad_ln1_bias,
        grad_b_qkv,
        grad_shift_taps,
        grad_shift_skip,
        grad_ssm_a,
        grad_ssm_b,
        grad_ssm_c,
        grad_ssm_skip,
        grad_ssm_step,
        grad_b_out,
        grad_ln2_gain,
        grad_ln2_bias,
        grad_b_up,
        grad_b_down,
    ]
    flat = jnp.concatenate([a.reshape(-1) for a in small])
    pieces = [grad_w_qkv.reshape(3 * chan_count, width_all), grad_w_out]
    rows_big = 4 * chan_count
    unit = 2 * lax.axis_size("seq") * SUBS
    rows_all = -(-(rows_big * width_all + flat.size) // (width_all * unit)) * unit
    flat = jnp.pad(flat, (0, (rows_all - rows_big) * width_all - flat.size))
    pieces.append(flat.reshape(rows_all - rows_big, width_all))
    whole_buffer = jnp.concatenate(pieces, axis=0).astype(bf16)
    half = rows_all // 2
    summed = jnp.concatenate(seq_sums(whole_buffer[:half], whole_buffer[half:]), axis=0)
    sum_qkv = jnp.transpose(summed[: 3 * chan_count].reshape(3, chan_count, width_all), (0, 2, 1))
    sum_out = summed[3 * chan_count : rows_big]
    flat = summed[rows_big:].reshape(-1).astype(f32)
    sums, offset = [], 0
    for a in small:
        sums.append(flat[offset : offset + a.size].reshape(a.shape))
        offset += a.size
    return (
        layer_out,
        grad_inputs,
        sums[0],
        sums[1],
        sum_qkv.astype(f32),
        sums[2],
        sums[3],
        sums[4],
        sums[5].T,
        sums[6].T,
        sums[7].T,
        sums[8],
        sums[9],
        sum_out.astype(f32),
        sums[10],
        sums[11],
        sums[12],
        sum_up.astype(f32),
        sums[13],
        sum_down.astype(f32),
        sums[14],
    )


def solution(mesh):
    in_specs = (
        P(None, "seq", None),
        P(None, "seq", None),
        P(),
        P(),
        P(),
        P(None, None, "head"),
        P(None, "head"),
        P(None, "head"),
        P("head"),
        P("head", None),
        P("head", None),
        P("head", None),
        P("head"),
        P("head"),
        P("head", None),
        P(),
        P(),
        P(),
        P(None, "head"),
        P("head"),
        P("head", None),
        P(),
    )
    out_specs = (
        P(None, "seq", None),
        P(None, "seq", None),
        P(),
        P(),
        P(None, None, "head"),
        P(None, "head"),
        P(None, "head"),
        P("head"),
        P("head", None),
        P("head", None),
        P("head", None),
        P("head"),
        P("head"),
        P("head", None),
        P(),
        P(),
        P(),
        P(None, "head"),
        P("head"),
        P("head", None),
        P(),
    )
    return jax.shard_map(shards, mesh=mesh, in_specs=in_specs, out_specs=out_specs, check_vma=False)
```

```python
import functools

import jax
import jax.numpy as jnp
from jax import lax
from jax.experimental import pallas as pl
from jax.experimental.pallas import tpu as pltpu
from jax.sharding import PartitionSpec as P

norm_epsilon = 1e-05
f32 = jnp.float32
bf16 = jnp.bfloat16
LANES = 128
FLOPS_PER_US = 0.5e9
SUBS = 8


def shifted(shard, axis, by):
    peers = lax.axis_size(axis)
    return lax.ppermute(shard, axis, [(i, i + by) for i in range(peers) if 0 <= i + by < peers])


def swapped(shard, axis, mask):
    return lax.ppermute(shard, axis, [(i, i ^ mask) for i in range(lax.axis_size(axis))])


class Steps:
    def __init__(self, steps):
        self.steps, self.value, self.ended = steps, None, False
        self.step()

    def step(self):
        try:
            if not self.ended:
                next(self.steps)
        except StopIteration as end:
            self.value, self.ended = end.value, True

    def result(self):
        while not self.ended:
            self.step()
        return self.value


def stepped(work):
    return lambda *args: Steps(work(*args))


@stepped
def halving_steps(call, groups, orders, spot, axis):
    keeps, sends = [g[0] for g in groups], [g[1] for g in groups]
    count = len(orders[0])
    for stage in range(count):
        gots = [swapped(send, axis, order[stage]) for send, order in zip(sends, orders)]
        yield
        operands = [a for pair in zip(keeps, gots) for a in pair]
        if stage + 1 < count:
            after = tuple(order[stage + 1] for order in orders)
            shapes = [like((k.shape[0] // 2, k.shape[1]), bf16) for k in keeps for _ in range(2)]
            parts = call(
                functools.partial(halve_kernel, after), shapes, [spot, *operands], limit=8, scalars=1
            )
            keeps, sends = parts[0::2], parts[1::2]
        else:
            owns = call(add_kernel, [like(k.shape, bf16) for k in keeps], operands, limit=8)
    for stage in range(count - 1, -1, -1):
        gots = [swapped(own, axis, order[stage]) for own, order in zip(owns, orders)]
        operands = [a for pair in zip(owns, gots) for a in pair]
        if stage:
            yield
            shapes = [like((2 * own.shape[0], own.shape[1]), bf16) for own in owns]
            owns = call(
                functools.partial(double_kernel, tuple(order[stage] for order in orders)),
                shapes, [spot, *operands], limit=8, scalars=1,
            )
    return operands


@stepped
def head_steps(call, keep, send, axis="head"):
    got = swapped(send, axis, 1)
    mask = 2
    while True:
        yield
        total, low = call(
            join_kernel, [like(keep.shape), like(keep.shape, bf16)], [keep, got], limit=8
        )
        if mask >= lax.axis_size(axis):
            return low, swapped(low, axis, 1)
        keep, got = total, swapped(low, axis, mask)
        mask *= 2


@stepped
def carry_steps(call, total, low, whole, spot, axis, ahead):
    carry = jnp.zeros_like(total)
    mask = 1
    while True:
        got = swapped(low, axis, mask)
        if 2 * mask >= lax.axis_size(axis):
            return carry, got
        yield
        total, low, carry = call(
            functools.partial(merge_kernel, mask, ahead),
            [like(total.shape), like(total.shape, bf16), like(total.shape)],
            [spot, whole, total, got, carry],
            limit=8,
            scalars=1,
        )
        mask *= 2


@stepped
def sum_steps(call, rows, axis):
    mask = 1
    while mask < lax.axis_size(axis):
        got = swapped(rows, axis, mask)
        yield
        (rows,) = call(plain_add_kernel, [like(rows.shape)], [rows, got], limit=4)
        mask *= 2
    return rows


def lane_tiles(width):
    return [slice(i, i + LANES) for i in range(0, width, LANES)]


def folded(product):
    states, lanes = product.shape
    return jnp.sum(product.reshape(states // SUBS, SUBS, lanes), axis=0)


def rows_at(start, size):
    return pl.ds(pl.multiple_of(start, SUBS), size)


def centred_rows(rows):
    centred = rows - jnp.mean(rows, axis=-1, keepdims=True)
    spread = jnp.mean(centred * centred, axis=-1, keepdims=True)
    return centred, lax.rsqrt(spread + norm_epsilon)


def row(vector_ref):
    return vector_ref[...].reshape(1, vector_ref.shape[0])


def wide(array, slots):
    return jnp.concatenate([array] * slots, axis=-1)


def slot_of(array, slot, width):
    return array[:, slot * width : (slot + 1) * width]


def contract(left, right, left_dim, right_dim):
    return lax.dot_general(
        left, right, (((left_dim,), (right_dim,)), ((), ())), preferred_element_type=f32
    )


def run_scan(series_ref, decay_ref, out_ref, reverse):
    blocks = series_ref.shape[0] // SUBS
    for lanes in lane_tiles(series_ref.shape[1]):
        decay = decay_ref[:, lanes]

        def one(lap, state, lanes=lanes, decay=decay):
            place = blocks - 1 - lap if reverse else lap
            tile = series_ref[rows_at(place * SUBS, SUBS), lanes]
            for r in range(SUBS):
                r = SUBS - 1 - r if reverse else r
                state = decay * state + tile[r : r + 1, :]
            return state

        out_ref[:, lanes] = lax.fori_loop(0, blocks, one, jnp.zeros_like(decay))


def part_total(part_ref, rows):
    total = part_ref[pl.ds(0, rows, stride=SUBS), :]
    for r in range(1, SUBS):
        total = total + part_ref[pl.ds(r, rows, stride=SUBS), :]
    return total


def power_of(whole, exponent, mask):
    power, bit = jnp.ones_like(whole), 1
    while bit < mask:
        power = jnp.where((exponent // bit) % 2 == 1, power * whole, power)
        whole = whole * whole
        bit *= 2
    return power, whole


def merged(mask, ahead, place, whole, got, carry):
    inner = place % mask
    far = (place // mask) % 2
    if ahead:
        inner, far = mask - 1 - inner, 1 - far
    power, step = power_of(whole, inner, mask)
    return jnp.where(far == 1, carry + power * got, carry), far, step


def merge_kernel(mask, ahead, spot_ref, whole_ref, total_ref, got_ref, carry_ref, sum_ref, low_ref, out_ref):
    got = got_ref[...].astype(f32)
    total = total_ref[...]
    out_ref[...], far, step = merged(
        mask, ahead, spot_ref[0], whole_ref[...], got, carry_ref[...]
    )
    total = jnp.where(far == 1, step * got + total, step * total + got)
    sum_ref[...] = total
    low_ref[...] = total.astype(bf16)


def bit_of(spot, mask):
    return (spot[0] // mask) % 2


def halve_kernel(after, spot_ref, *refs):
    ins, outs = refs[: 2 * len(after)], refs[2 * len(after) :]
    for k, mask in enumerate(after):
        total = ins[2 * k][...].astype(f32) + ins[2 * k + 1][...].astype(f32)
        half = total.shape[0] // 2
        put_halves(bit_of(spot_ref, mask), total[:half], total[half:], outs[2 * k], outs[2 * k + 1])


def plain_add_kernel(own_ref, got_ref, out_ref):
    out_ref[...] = own_ref[...] + got_ref[...]


def add_kernel(*refs):
    count = len(refs) // 3
    for k, out_ref in enumerate(refs[2 * count :]):
        total = refs[2 * k][...].astype(f32) + refs[2 * k + 1][...].astype(f32)
        out_ref[...] = total.astype(bf16)


def double_kernel(masks, spot_ref, *refs):
    for k, mask in enumerate(masks):
        out_ref = refs[2 * len(masks) + k]
        half = out_ref.shape[0] // 2
        first, second = halves_of(bit_of(spot_ref, mask), refs[2 * k], refs[2 * k + 1])
        out_ref[0:half, :] = first.astype(bf16)
        out_ref[half:, :] = second.astype(bf16)


def join_kernel(keep_ref, got_ref, total_ref, low_ref):
    total = keep_ref[...].astype(f32) + got_ref[...].astype(f32)
    total_ref[...] = total
    low_ref[...] = total.astype(bf16)


def ordered(bit, own, other):
    return jnp.where(bit == 0, own, other), jnp.where(bit == 0, other, own)


def halves_of(bit, own_ref, other_ref):
    return ordered(bit, own_ref[...].astype(f32), other_ref[...].astype(f32))


def put_halves(bit, first, second, keep_ref, send_ref):
    keep, send = ordered(bit, first, second)
    keep_ref[...] = keep.astype(bf16)
    send_ref[...] = send.astype(bf16)


def project_kernel(
    spot_ref, x_hbm, gain_hbm, bias_hbm, w_hbm, wb_hbm, act_ref, q_ref, k_ref, v_ref,
    x_ref, gain_ref, bias_ref, w_ref, wb_ref, sems,
):
    pairs = ((x_hbm, x_ref), (gain_hbm, gain_ref), (bias_hbm, bias_ref), (w_hbm, w_ref), (wb_hbm, wb_ref))
    copies = [pltpu.make_async_copy(a, b, sems.at[i]) for i, (a, b) in enumerate(pairs)]
    for copy in copies:
        copy.start()
    for copy in copies:
        copy.wait()
    slots, rows, _ = x_ref.shape
    gain, bias = row(gain_ref), row(bias_ref)
    kept = [[], [], []]
    for s in range(slots):
        centred, root = centred_rows(x_ref[s].astype(f32))
        act = (centred * root * gain + bias).astype(bf16)
        act_ref[s * rows : (s + 1) * rows, :] = act
        for j in range(3):
            kept[j].append(contract(act, w_ref[j], 1, 1) + wb_ref[j : j + 1, :])
    q_ref[...] = jnp.concatenate(kept[0], axis=-1)
    k_ref[...] = jnp.concatenate(kept[1], axis=-1).astype(bf16)
    v_ref[...] = jnp.concatenate(kept[2], axis=-1)


def masked_kernel(spot_ref, lengths_ref, cotangent_ref, low_ref, sum_ref):
    slots, rows, model = cotangent_ref.shape
    spot = spot_ref[0] * rows + lax.broadcasted_iota(jnp.int32, (rows, model), 0)
    total = 0.0
    for s in range(slots):
        grads = jnp.where(spot < lengths_ref[s], cotangent_ref[s], 0.0)
        low_ref[s * rows : (s + 1) * rows, :] = grads.astype(bf16)
        total = total + jnp.sum(grads, axis=0, keepdims=True)
    sum_ref[...] = total


def mix_kernel(
    edge_ref, k_ref, v_ref, taps_ref, skip_ref, decay_ref,
    shifted_ref, u_ref, end_ref, low_ref, ext_ref, wide_ref,
):
    taps, width = edge_ref.shape
    rows = k_ref.shape[0]
    slots = width // taps_ref.shape[1]
    ext_ref[0:taps, :] = edge_ref[...].astype(f32)
    ext_ref[taps : taps + rows, :] = k_ref[...].astype(f32)
    wide_ref[0:taps, :] = wide(taps_ref[...], slots)
    wide_ref[taps : taps + 1, :] = wide(row(skip_ref), slots)
    for lanes in lane_tiles(width):
        total = wide_ref[taps : taps + 1, lanes] * ext_ref[taps : taps + rows, lanes]
        for r in range(SUBS):
            if r:
                block = ext_ref[SUBS - r : taps + rows - r, lanes]
            else:
                block = ext_ref[0 : taps + rows - SUBS, lanes]
            for q in range(taps // SUBS):
                i = SUBS * q + (r if r else SUBS)
                start = taps - SUBS - SUBS * q
                total = total + wide_ref[i - 1 : i, lanes] * block[start : start + rows, :]
        shifted_ref[:, lanes] = total
        u_ref[:, lanes] = total * v_ref[:, lanes]
    run_scan(u_ref, decay_ref, end_ref, False)
    low_ref[...] = end_ref[...].astype(bf16)


def attend_kernel(
    mask, spot_ref, u_ref, decay_ref, weight_ref, whole_ref, got_ref, carry_ref, skip_ref,
    q_ref, w_ref, ssm_ref, gated_ref, start_ref, keep_ref, send_ref, part_ref,
):
    rows, width = u_ref.shape
    chans = w_ref.shape[0]
    slots = width // chans
    blocks = rows // SUBS
    skip = wide(row(skip_ref), slots)
    start_ref[...], _, _ = merged(
        mask, False, spot_ref[0], whole_ref[...], got_ref[...].astype(f32), carry_ref[...]
    )
    for lanes in lane_tiles(width):
        decay = decay_ref[:, lanes]
        weight = weight_ref[:, lanes]

        def one(lap, state, lanes=lanes, decay=decay, weight=weight):
            tile = u_ref[rows_at(lap * SUBS, SUBS), lanes]
            for r in range(SUBS):
                state = decay * state + tile[r : r + 1, :]
                part_ref[rows_at(lap * SUBS * SUBS + r * SUBS, SUBS), :] = folded(weight * state)
            return state

        lax.fori_loop(0, blocks, one, start_ref[:, lanes])
        ssm_ref[:, lanes] = part_total(part_ref, rows) + skip[:, lanes] * u_ref[:, lanes]
    mixture = q_ref[...] * ssm_ref[...]
    terms = []
    for s in range(slots):
        gated = slot_of(mixture, s, chans).astype(bf16)
        gated_ref[s * rows : (s + 1) * rows, :] = gated
        terms.append(contract(gated, w_ref[...], 1, 0))
    half = slots // 2
    put_halves(
        spot_ref[1],
        jnp.concatenate(terms[:half], axis=0),
        jnp.concatenate(terms[half:], axis=0),
        keep_ref,
        send_ref,
    )


def gelu_parts(x):
    root = 0.7978845608028654
    square = x * x
    bend = jnp.tanh(root * (x + 0.044715 * (square * x)))
    value = 0.5 * x * (1.0 + bend)
    slope = 0.5 * (1.0 + bend) + 0.5 * x * (1.0 - bend * bend) * root * (1.0 + 0.134145 * square)
    return value, slope


def feed_kernel(
    mask_one, mask_two, spot_ref, own_ref, other_ref, x_ref, b_out_ref, gain_ref, bias_ref, up_ref, up_bias_ref, down_ref,
    gout_ref, mid_ref, keep_ref, send_ref, out_keep_ref, out_send_ref,
    bias_sum_ref, w_up_ref, w_up_send_ref, w_down_ref, w_down_send_ref, act_ref, hidden_ref, grad_ref,
):
    bias_sum = 0.0
    backs, outs = [], []
    rows = own_ref.shape[0]
    for half, attended in enumerate(halves_of(spot_ref[1], own_ref, other_ref)):
        at = slice(half * rows, (half + 1) * rows)
        middle = x_ref[at, :].astype(f32) + attended + row(b_out_ref)
        mid_ref[at, :] = middle
        centred, root = centred_rows(middle)
        act = (centred * root * row(gain_ref) + row(bias_ref)).astype(bf16)
        act_ref[at, :] = act
        value, slope = gelu_parts(contract(act, up_ref[...], 1, 0) + row(up_bias_ref))
        hidden = value.astype(bf16)
        hidden_ref[at, :] = hidden
        grads = (contract(gout_ref[at, :], down_ref[...], 1, 1) * slope).astype(bf16)
        grad_ref[at, :] = grads
        bias_sum = bias_sum + jnp.sum(grads.astype(f32), axis=0, keepdims=True)
        backs.append(contract(grads, up_ref[...], 1, 1))
        outs.append(contract(hidden, down_ref[...], 1, 0))
    bias_sum_ref[...] = bias_sum
    put_halves(spot_ref[1], backs[0], backs[1], keep_ref, send_ref)
    put_halves(spot_ref[1], outs[0], outs[1], out_keep_ref, out_send_ref)
    sums = contract(act_ref[...], grad_ref[...], 0, 0)
    half = sums.shape[0] // 2
    put_halves(bit_of(spot_ref, mask_one), sums[:half], sums[half:], w_up_ref, w_up_send_ref)
    sums = contract(hidden_ref[...], gout_ref[...], 0, 0)
    half = sums.shape[0] // 2
    put_halves(bit_of(spot_ref, mask_two), sums[:half], sums[half:], w_down_ref, w_down_send_ref)


def result_kernel(spot_ref, lengths_ref, own_ref, other_ref, mid_ref, b_down_ref, out_ref):
    slots, rows, model = out_ref.shape
    halves = halves_of(spot_ref[1], own_ref, other_ref)
    per = slots // 2
    spot = spot_ref[0] * rows + lax.broadcasted_iota(jnp.int32, (rows, model), 0)
    for s in range(slots):
        half = halves[s // per]
        feed = half[(s % per) * rows : (s % per + 1) * rows, :] + row(b_down_ref)
        total = mid_ref[s * rows : (s + 1) * rows, :] + feed
        out_ref[s] = jnp.where(spot < lengths_ref[s], total, 0.0)


def norm_grad(grad, hat, root, gain):
    scaled = grad * gain
    inner = jnp.mean(scaled * hat, axis=-1, keepdims=True)
    return root * (scaled - jnp.mean(scaled, axis=-1, keepdims=True) - hat * inner)


def entry_kernel(spot_ref, own_ref, other_ref, x_ref, gain_ref, gmid_ref, out_ref, rows_ref):
    rows = own_ref.shape[0]
    gain_rows = bias_rows = 0.0
    for half, grad in enumerate(halves_of(spot_ref[1], own_ref, other_ref)):
        at = slice(half * rows, (half + 1) * rows)
        centred, root = centred_rows(x_ref[at, :].astype(f32))
        hat = centred * root
        out_ref[at, :] = gmid_ref[at, :] + norm_grad(grad, hat, root, row(gain_ref))
        gain_rows = gain_rows + jnp.sum(grad * hat, axis=0, keepdims=True)
        bias_rows = bias_rows + jnp.sum(grad, axis=0, keepdims=True)
    rows_ref[...] = jnp.concatenate(
        [gain_rows, bias_rows, jnp.zeros((SUBS - 2, gain_rows.shape[1]), f32)], axis=0
    )


def middle_kernel(
    spot_ref, lengths_ref, own_ref, other_ref, mid_ref, cotangent_ref, gain_ref, w_ref, ssm_ref, q_ref, decay_ref,
    gmid_ref, low_ref, gq_ref, gs_ref, front_ref, front_low_ref, rows_ref,
):
    rows, width = ssm_ref.shape
    chans = w_ref.shape[0]
    gain = row(gain_ref)
    gain_rows = bias_rows = mid_rows = 0.0
    kept = []
    half = own_ref.shape[0]
    first, second = halves_of(spot_ref[1], own_ref, other_ref)
    for s in range(width // chans):
        at = slice(s * rows, (s + 1) * rows)
        inside = slice(s * rows % half, s * rows % half + rows)
        grad = (first if s * rows < half else second)[inside, :]
        centred, root = centred_rows(mid_ref[at, :])
        hat = centred * root
        spot = spot_ref[0] * rows + lax.broadcasted_iota(jnp.int32, hat.shape, 0)
        held = jnp.where(spot < lengths_ref[s], cotangent_ref[s], 0.0)
        grad_mid = held + norm_grad(grad, hat, root, gain)
        gmid_ref[at, :] = grad_mid
        low = grad_mid.astype(bf16)
        low_ref[at, :] = low
        gain_rows = gain_rows + jnp.sum(grad * hat, axis=0, keepdims=True)
        bias_rows = bias_rows + jnp.sum(grad, axis=0, keepdims=True)
        mid_rows = mid_rows + jnp.sum(grad_mid, axis=0, keepdims=True)
        kept.append(contract(low, w_ref[...], 1, 1))
    gated = jnp.concatenate(kept, axis=-1)
    gq_ref[...] = (gated * ssm_ref[...]).astype(bf16)
    gs_ref[...] = gated * q_ref[...]
    rows_ref[...] = jnp.zeros_like(rows_ref)
    rows_ref[0:1, :] = gain_rows
    rows_ref[1:2, :] = bias_rows
    rows_ref[2:3, :] = mid_rows
    run_scan(gs_ref, decay_ref, front_ref, True)
    front_low_ref[...] = front_ref[...].astype(bf16)


def local_kernel(
    u_ref, gs_ref, decay_ref, weight_ref, start_ref,
    out_ref, gain_ref, power_ref, reach_ref, part_ref, past_ref,
):
    rows = u_ref.shape[0]
    blocks = rows // SUBS
    states = decay_ref.shape[0]
    for lanes in lane_tiles(u_ref.shape[1]):
        decay = decay_ref[:, lanes]
        weight = weight_ref[:, lanes]

        def rise(lap, carry, lanes=lanes, decay=decay):
            state, reach = carry
            tile = u_ref[rows_at(lap * SUBS, SUBS), lanes]
            for r in range(SUBS):
                past_ref[rows_at(lap * SUBS * states + r * states, states), :] = state
                reach = decay * (reach + state)
                state = decay * state + tile[r : r + 1, :]
            return state, reach

        zero = jnp.zeros_like(decay)
        _, reach = lax.fori_loop(0, blocks, rise, (start_ref[:, lanes], zero))
        reach_ref[:, lanes] = reach

        def fall(lap, carry, lanes=lanes, decay=decay, weight=weight):
            adjoint, gain, power = carry
            place = blocks - 1 - lap
            tile = u_ref[rows_at(place * SUBS, SUBS), lanes]
            grads = gs_ref[rows_at(place * SUBS, SUBS), lanes]
            for r in range(SUBS - 1, -1, -1):
                adjoint = decay * adjoint + grads[r : r + 1, :]
                part_ref[rows_at(place * SUBS * SUBS + r * SUBS, SUBS), :] = folded(weight * adjoint)
                gain = gain + adjoint * tile[r : r + 1, :]
                power = power + adjoint * past_ref[
                    rows_at(place * SUBS * states + r * states, states), :
                ]
            return adjoint, gain, power

        _, gain, power = lax.fori_loop(0, blocks, fall, (zero, zero, zero))
        gain_ref[:, lanes] = gain
        power_ref[:, lanes] = power
        out_ref[:, lanes] = part_total(part_ref, rows)


def unmix_kernel(
    mask, spot_ref, gloc_ref, gs_ref, u_ref, decay_ref, weight_ref, whole_ref, got_ref, carry_ref, gain_ref, power_ref, reach_ref,
    end_ref, v_ref, shifted_ref, edge_ref, k_ref, taps_ref, shift_skip_ref, ssm_skip_ref,
    in_ref, out_ref, root_ref, slope_ref, fall_ref, a_ref, step_ref,
    gk_ref, halo_ref, gv_ref, small_ref, misc_ref,
    part_ref, ext_ref, pad_ref, wide_ref, sums_ref, tap_ref, behind_ref,
):
    rows, width = u_ref.shape
    blocks = rows // SUBS
    taps, chans = taps_ref.shape
    states = decay_ref.shape[0]
    slots = width // chans
    skip = wide(row(ssm_skip_ref), slots)
    behind_ref[...], _, _ = merged(
        mask, True, spot_ref[0], whole_ref[...], got_ref[...].astype(f32), carry_ref[...]
    )
    ext_ref[0:taps, :] = edge_ref[...].astype(f32)
    ext_ref[taps : taps + rows, :] = k_ref[...].astype(f32)
    pad_ref[0:taps, :] = jnp.zeros((taps, width), f32)
    pad_ref[taps + rows : 2 * taps + rows, :] = jnp.zeros((taps, width), f32)
    wide_ref[0:taps, :] = wide(taps_ref[...], slots)
    wide_ref[taps : taps + 1, :] = wide(row(shift_skip_ref), slots)
    for lanes in lane_tiles(width):
        decay = decay_ref[:, lanes]
        weight = weight_ref[:, lanes]

        def one(lap, state, decay=decay, weight=weight):
            place = blocks - 1 - lap
            for r in range(SUBS - 1, -1, -1):
                state = decay * state
                part_ref[rows_at(place * SUBS * SUBS + r * SUBS, SUBS), :] = folded(weight * state)
            return state

        lax.fori_loop(0, blocks, one, behind_ref[:, lanes])
        grad_u = (
            gloc_ref[:, lanes] + part_total(part_ref, rows) + skip[:, lanes] * gs_ref[:, lanes]
        )
        gv_ref[:, lanes] = (grad_u * shifted_ref[:, lanes]).astype(bf16)
        pad_ref[taps : taps + rows, lanes] = grad_u * v_ref[:, lanes]
        total = wide_ref[taps : taps + 1, lanes] * pad_ref[taps : taps + rows, lanes]
        borrowed = jnp.zeros((taps, LANES), f32)
        for r in range(SUBS):
            block = pad_ref[r : 2 * taps + rows - SUBS + r, lanes]
            for q in range(taps // SUBS + 1):
                i = SUBS * q + r
                if i < 1 or i > taps:
                    continue
                tap = wide_ref[i - 1 : i, lanes]
                start = taps + SUBS * q
                if start + rows <= block.shape[0]:
                    total = total + tap * block[start : start + rows, :]
                else:
                    live = block.shape[0] - start
                    total = total + tap * jnp.concatenate(
                        [block[start:, :], jnp.zeros((rows - live, LANES), f32)], axis=0
                    )
                borrowed = borrowed + tap * block[SUBS * q : SUBS * q + taps, :]
        gk_ref[:, lanes] = total
        halo_ref[:, lanes] = borrowed.astype(bf16)
        grad_shifted = pad_ref[taps : taps + rows, lanes]
        for r in range(SUBS):
            block = ext_ref[r : taps + rows - SUBS + r, lanes] if r else ext_ref[:, lanes]
            for q in range(taps // SUBS + 1):
                start = SUBS * q
                i = taps - start - r
                if i < 0:
                    continue
                product = grad_shifted * block[start : start + rows, :]
                sums_ref[SUBS * i : SUBS * (i + 1), :] = folded(product)
        tap_ref[0 : taps + 1, lanes] = part_total(sums_ref, taps + 1)
    gain = gain_ref[...] + behind_ref[...] * decay_ref[...] * end_ref[...]
    power = power_ref[...] + behind_ref[...] * reach_ref[...]

    def slots_total(array):
        total = slot_of(array, 0, chans)
        for s in range(1, slots):
            total = total + slot_of(array, s, chans)
        return total

    gain, power = slots_total(gain), slots_total(power)
    grad_in = out_ref[...] * gain
    grad_rate = grad_in * slope_ref[...] - fall_ref[...] * power
    tap_sums = slots_total(tap_ref[0 : taps + 1, :])
    small_ref[...] = jnp.concatenate(
        [
            tap_sums[1 : taps + 1, :],
            grad_rate * row(step_ref),
            grad_in * root_ref[...],
            in_ref[...] * gain,
        ],
        axis=-1,
    )
    misc_ref[...] = jnp.zeros_like(misc_ref)
    skip_sums = slots_total(jnp.sum(gs_ref[...] * u_ref[...], axis=0, keepdims=True))
    step_sums = jnp.sum(grad_rate * a_ref[...], axis=0, keepdims=True)
    misc_ref[0:1, :] = jnp.concatenate(
        [tap_sums[0:1, :], skip_sums, step_sums, jnp.zeros_like(skip_sums)], axis=-1
    )


def weights_kernel(gq_ref, act_ref, gated_ref, low_ref, out_ref):
    rows, width = gq_ref.shape
    chans = gated_ref.shape[1]
    query = 0.0
    for s in range(width // chans):
        grads = slot_of(gq_ref[...].astype(f32), s, chans).astype(bf16)
        query = query + contract(grads, act_ref[s * rows : (s + 1) * rows, :], 0, 0)
    out_ref[0:chans, :] = query.astype(bf16)
    out_ref[chans : 2 * chans, :] = contract(gated_ref[...], low_ref[...], 0, 0).astype(bf16)


def last_kernel(
    mask_one, mask_two, spot_ref, gq_ref, gk_ref, received_ref, gv_ref, act_ref, w_ref, early_ref, small_ref, misc_ref,
    rows_ref, up_ref, down_ref, keep_ref, send_ref, one_ref, one_send_ref, two_ref,
    two_send_ref, all_ref,
):
    rows, width = gk_ref.shape
    taps = received_ref.shape[0]
    chans = w_ref.shape[1]
    slots = width // chans
    grad_k = jnp.concatenate(
        [
            gk_ref[0 : rows - taps, :],
            gk_ref[rows - taps : rows, :] + received_ref[...].astype(f32),
        ],
        axis=0,
    ).astype(bf16)
    parts = [gq_ref[...].astype(f32), grad_k.astype(f32), gv_ref[...].astype(f32)]
    sums = [0.0, 0.0, 0.0]
    terms, biases = [], []
    for s in range(slots):
        act = act_ref[s * rows : (s + 1) * rows, :]
        term = 0.0
        for j in range(3):
            grads = slot_of(parts[j], s, chans).astype(bf16)
            term = term + contract(grads, w_ref[j], 1, 0)
            if j:
                sums[j] = sums[j] + contract(grads, act, 0, 0)
        terms.append(term)
    half = slots // 2
    put_halves(
        spot_ref[1],
        jnp.concatenate(terms[:half], axis=0),
        jnp.concatenate(terms[half:], axis=0),
        keep_ref,
        send_ref,
    )
    for j in range(3):
        total = jnp.sum(parts[j], axis=0, keepdims=True)
        bias = slot_of(total, 0, chans)
        for s in range(1, slots):
            bias = bias + slot_of(total, s, chans)
        biases.append(bias)
    place = 0

    def put(block):
        nonlocal place
        all_ref[place : place + block.shape[0], :] = block.astype(f32)
        place += block.shape[0]

    put(early_ref[...])
    put(sums[1])
    put(sums[2])
    put(small_ref[...])
    put(
        jnp.concatenate(
            [
                misc_ref[0:1, :],
                jnp.concatenate(biases + [jnp.zeros_like(biases[0])], axis=-1),
                rows_ref[0:3, :],
                up_ref[...],
                down_ref[...],
                jnp.zeros((2 * SUBS - 7, misc_ref.shape[1]), f32),
            ],
            axis=0,
        )
    )
    put(jnp.zeros((all_ref.shape[0] - place, misc_ref.shape[1]), f32))
    count = all_ref.shape[0] // 4
    quarters = [all_ref[k * count : (k + 1) * count, :] for k in range(4)]
    put_halves(bit_of(spot_ref, mask_one), quarters[0], quarters[1], one_ref, one_send_ref)
    put_halves(bit_of(spot_ref, mask_two), quarters[2], quarters[3], two_ref, two_send_ref)


def widen_kernel(mask_one, mask_two, spot_ref, up_ref, up_got_ref, down_ref, down_got_ref, one_ref, two_ref):
    for mask, own_ref, got_ref, out_ref in (
        (mask_one, up_ref, up_got_ref, one_ref),
        (mask_two, down_ref, down_got_ref, two_ref),
    ):
        half = own_ref.shape[0]
        first, second = halves_of(bit_of(spot_ref, mask), own_ref, got_ref)
        out_ref[0:half, :] = first
        out_ref[half:, :] = second


def spread_kernel(
    chans, taps, mask_one, mask_two, spot_ref, one_ref, one_got_ref, two_ref, two_got_ref,
    qkv_ref, bias_ref, tap_ref, shift_skip_ref, a_ref, b_ref, c_ref, ssm_skip_ref, step_ref, out_ref,
    gain_ref, norm_bias_ref, out_bias_ref, up_ref, down_ref, all_ref,
):
    quarter = one_ref.shape[0]
    pieces = halves_of(bit_of(spot_ref, mask_one), one_ref, one_got_ref)
    pieces += halves_of(bit_of(spot_ref, mask_two), two_ref, two_got_ref)
    for place, piece in enumerate(pieces):
        all_ref[place * quarter : (place + 1) * quarter, :] = piece
    for j, place in enumerate((0, 2, 3)):
        qkv_ref[j] = all_ref[place * chans : (place + 1) * chans, :]
    out_ref[...] = all_ref[chans : 2 * chans, :]
    base = 4 * chans
    small = all_ref[base : base + taps, :]
    for slot, ref in enumerate((tap_ref, a_ref, b_ref, c_ref)):
        ref[...] = slot_of(small, slot, chans)
    base = base + taps
    misc = all_ref[base : base + SUBS, :]
    for slot, ref in enumerate((shift_skip_ref, ssm_skip_ref, step_ref)):
        ref[...] = slot_of(misc[0:1, :], slot, chans).reshape(chans)
    bias_ref[...] = jnp.concatenate([slot_of(misc[1:2, :], j, chans) for j in range(3)], axis=0)
    for place, ref in enumerate((gain_ref, norm_bias_ref, out_bias_ref, up_ref, down_ref)):
        ref[...] = misc[2 + place : 3 + place, :].reshape(misc.shape[1])


def ordered_calls():
    held = [jnp.zeros((SUBS, LANES), f32)]

    def call(kernel, outs, args, scratch=(), us=0.5, limit=24, scalars=0, place=pltpu.VMEM):
        inputs = len(args)

        def body(*refs):
            given, rest = refs[:inputs], refs[inputs + 1 :]
            rest[len(outs)][...] = refs[inputs][...]
            kernel(*given, *rest[: len(outs)], *rest[len(outs) + 1 :])

        size = sum(a.size * a.dtype.itemsize for a in list(args) + list(outs))
        specs = [pl.BlockSpec(memory_space=pltpu.SMEM)] * scalars
        specs += [pl.BlockSpec(memory_space=place)] * (inputs - scalars)
        specs += [pl.BlockSpec(memory_space=pltpu.VMEM)]
        results = pl.pallas_call(
            body,
            in_specs=specs,
            out_shape=tuple(outs) + (like((SUBS, LANES)),),
            scratch_shapes=list(scratch),
            compiler_params=pltpu.CompilerParams(vmem_limit_bytes=limit << 20),
            cost_estimate=pl.CostEstimate(
                flops=int(us * FLOPS_PER_US), bytes_accessed=0, transcendentals=0
            ),
        )(*args, held[0])
        held[0] = results[-1]
        return results[:-1]

    return call


def like(shape, dtype=f32):
    return jax.ShapeDtypeStruct(shape, dtype)


def shards(
    inputs,
    cotangent,
    lengths,
    ln1_gain,
    ln1_bias,
    query_key_value_weight,
    b_qkv,
    shift_taps,
    shift_skip,
    ssm_a,
    ssm_b,
    ssm_c,
    ssm_skip,
    ssm_step,
    output_weight,
    b_out,
    ln2_gain,
    ln2_bias,
    up_weight,
    up_bias,
    down_weight,
    b_down,
):
    slots, rows, model = inputs.shape
    taps, chans = shift_taps.shape
    states = ssm_a.shape[1]
    width = slots * chans
    tokens = slots * rows
    spot = jnp.stack([lax.axis_index("seq"), lax.axis_index("head") % 2]).astype(jnp.int32)
    peers = lax.axis_size("seq")
    last_mask = peers // 2
    half_tokens = tokens // 2
    half_like = like((half_tokens, model), bf16)
    projections = jnp.swapaxes(query_key_value_weight, 1, 2)
    flat_inputs = inputs.reshape(tokens, model)
    hidden_count = up_bias.shape[0]
    masks = [2**k for k in range(peers.bit_length() - 1)]
    orders = (masks, masks[1::-1] + masks[2:])
    ends = tuple(order[0] for order in orders)
    call = ordered_calls()

    rate = (ssm_step[:, None] * ssm_a).T
    decay = jnp.exp(-rate)
    gain_root = jnp.sqrt(-jnp.expm1(-2.0 * rate))
    turned_b, turned_c = ssm_b.T, ssm_c.T
    in_weight = gain_root * turned_b
    decay_wide = wide(decay, slots)
    whole_wide = wide(jnp.exp(-rate * rows), slots)
    weight_wide = wide(turned_c * in_weight, slots)
    slope = turned_b * jnp.exp(-2.0 * rate) / gain_root
    fall = decay * turned_c * in_weight

    act_one, queries, keys, values = call(
        project_kernel,
        [like((tokens, model), bf16), like((rows, width)), like((rows, width), bf16), like((rows, width))],
        [spot] + [
            pltpu.with_memory_space_constraint(a, pltpu.HBM)
            for a in (inputs, ln1_gain, ln1_bias, projections, b_qkv)
        ],
        [
            pltpu.VMEM(inputs.shape, inputs.dtype),
            pltpu.VMEM(ln1_gain.shape, f32),
            pltpu.VMEM(ln1_bias.shape, f32),
            pltpu.VMEM(projections.shape, projections.dtype),
            pltpu.VMEM(b_qkv.shape, f32),
            pltpu.SemaphoreType.DMA((5,)),
        ],
        us=2.0,
        scalars=1,
        place=pltpu.HBM,
        limit=24,
    )
    edge = shifted(keys[rows - taps :, :], "seq", 1)
    shifted_keys, series, end_local, end_low = call(
        mix_kernel,
        [like((rows, width)), like((rows, width)), like((states, width)), like((states, width), bf16)],
        [edge, keys, values, shift_taps, shift_skip, decay_wide],
        [pltpu.VMEM((taps + rows, width), f32), pltpu.VMEM((taps + SUBS, width), f32)],
        us=2.9,
    )
    steps = carry_steps(call, end_local, end_low, whole_wide, spot, "seq", False)
    low_out, grad_b_down = call(
        masked_kernel,
        [like((tokens, model), bf16), like((1, model))],
        [spot, lengths, cotangent],
        us=0.8,
        scalars=2,
    )
    carry, got = steps.result()
    ssm_out, gated, start_state, keep, send = call(
        functools.partial(attend_kernel, last_mask),
        [like((rows, width)), like((tokens, chans), bf16), like((states, width)), half_like, half_like],
        [
            spot, series, decay_wide, weight_wide, whole_wide, got, carry, ssm_skip, queries,
            output_weight,
        ],
        [pltpu.VMEM((rows * SUBS, LANES), f32)],
        us=2.9,
        scalars=1,
    )
    own, other = head_steps(call, keep, send).result()
    middle, keep, send, out_keep, out_send, grad_b_up, up_keep, up_send, down_keep, down_send = call(
        functools.partial(feed_kernel, *ends),
        [
            like((tokens, model)),
            half_like,
            half_like,
            half_like,
            half_like,
            like((1, hidden_count)),
            like((model // 2, hidden_count), bf16),
            like((model // 2, hidden_count), bf16),
            like((hidden_count // 2, model), bf16),
            like((hidden_count // 2, model), bf16),
        ],
        [
            spot, own, other, flat_inputs, b_out, ln2_gain, ln2_bias, up_weight, up_bias, down_weight,
            low_out,
        ],
        [
            pltpu.VMEM((tokens, model), bf16),
            pltpu.VMEM((tokens, hidden_count), bf16),
            pltpu.VMEM((tokens, hidden_count), bf16),
        ],
        us=5.0,
        scalars=1,
        limit=32,
    )
    feed_sums = halving_steps(
        call, [(up_keep, up_send), (down_keep, down_send)], orders, spot, "seq"
    )
    steps = head_steps(call, keep, send)
    own, other = steps.result()
    grad_middle, low_middle, grad_queries, grad_ssm, front_local, front_low, norm_rows = call(
        middle_kernel,
        [
            like((tokens, model)),
            like((tokens, model), bf16),
            like((rows, width), bf16),
            like((rows, width)),
            like((states, width)),
            like((states, width), bf16),
            like((SUBS, model)),
        ],
        [
            spot, lengths, own, other, middle, cotangent, ln2_gain, output_weight, ssm_out, queries,
            decay_wide,
        ],
        us=2.5,
        scalars=2,
    )
    steps = carry_steps(call, front_local, front_low, whole_wide, spot, "seq", True)
    (early,) = call(
        weights_kernel,
        [like((2 * chans, model), bf16)],
        [grad_queries, act_one, gated, low_middle],
        us=0.5,
    )
    feed_sums.step()
    steps.step()
    carry, got = steps.result()
    grad_local, gain_local, power_local, reach = call(
        local_kernel,
        [like((rows, width)), like((states, width)), like((states, width)), like((states, width))],
        [series, grad_ssm, decay_wide, weight_wide, start_state],
        [pltpu.VMEM((rows * SUBS, LANES), f32), pltpu.VMEM((rows * states, LANES), f32)],
        us=5.8,
    )
    feed_sums.step()
    grad_keys, halo, grad_values, small, misc = call(
        functools.partial(unmix_kernel, last_mask),
        [
            like((rows, width)),
            like((taps, width), bf16),
            like((rows, width), bf16),
            like((states, 4 * chans)),
            like((SUBS, 4 * chans)),
        ],
        [
            spot, grad_local, grad_ssm, series, decay_wide, weight_wide, whole_wide, got, carry,
            gain_local, power_local, reach, end_local, values, shifted_keys, edge, keys, shift_taps,
            shift_skip, ssm_skip, in_weight, turned_c, gain_root, slope, fall, ssm_a.T, ssm_step,
        ],
        [
            pltpu.VMEM((rows * SUBS, LANES), f32),
            pltpu.VMEM((taps + rows, width), f32),
            pltpu.VMEM((2 * taps + rows, width), f32),
            pltpu.VMEM((taps + SUBS, width), f32),
            pltpu.VMEM(((taps + 1) * SUBS, LANES), f32),
            pltpu.VMEM((taps + SUBS, width), f32),
            pltpu.VMEM((states, width), f32),
        ],
        us=6.0,
        scalars=1,
    )
    received = shifted(halo, "seq", -1)
    feed_sums.step()
    unit = 2 * peers * SUBS
    last_rows = -(-(4 * chans + states + 2 * SUBS) // unit) * unit
    quarter = like((last_rows // 4, model), bf16)
    keep, send, one, one_send, two, two_send = call(
        functools.partial(last_kernel, *ends),
        [half_like, half_like, quarter, quarter, quarter, quarter],
        [
            spot, grad_queries, grad_keys, received, grad_values, act_one, projections, early, small,
            misc, norm_rows, grad_b_up, grad_b_down,
        ],
        [pltpu.VMEM((last_rows, model), f32)],
        us=1.5,
        scalars=1,
    )
    back = head_steps(call, keep, send)
    last_sums = halving_steps(call, [(one, one_send), (two, two_send)], orders, spot, "seq")
    back.step()
    feed_sums.step()
    own, other = back.result()
    last_sums.step()
    grad_inputs, ln1_rows = call(
        entry_kernel,
        [like((tokens, model)), like((SUBS, model))],
        [spot, own, other, flat_inputs, ln1_gain, grad_middle],
        scalars=1,
        us=2.0,
    )
    ln1 = sum_steps(call, ln1_rows, "seq")
    feed_joined = feed_sums.result()
    last_sums.step()
    feed = head_steps(call, out_keep, out_send)
    ln1.step()
    last_sums.step()
    feed.step()
    ln1.step()
    last_sums.step()
    sum_up, sum_down = call(
        functools.partial(widen_kernel, *ends),
        [like((model, hidden_count)), like((hidden_count, model))],
        [spot, *feed_joined],
        scalars=1,
        us=2.5,
    )
    own, other = feed.result()
    last_sums.step()
    (layer_out,) = call(
        result_kernel,
        [like(inputs.shape)],
        [spot, lengths, own, other, middle, b_down],
        scalars=2,
        us=1.5,
    )
    ln1_rows = ln1.result()
    joined = last_sums.result()
    spread = call(
        functools.partial(spread_kernel, chans, taps, *ends),
        [
            like((3, chans, model)),
            like((3, chans)),
            like((taps, chans)),
            like((chans,)),
            like((states, chans)),
            like((states, chans)),
            like((states, chans)),
            like((chans,)),
            like((chans,)),
            like((chans, model)),
            like((model,)),
            like((model,)),
            like((model,)),
            like(up_bias.shape),
            like((model,)),
        ],
        [spot, *joined],
        [pltpu.VMEM((last_rows, model), f32)],
        scalars=1,
        us=2.0,
    )
    (
        sum_qkv, sum_b_qkv, sum_taps, sum_shift_skip, sum_a, sum_b, sum_c, sum_ssm_skip, sum_step,
        sum_out, sum_ln2_gain, sum_ln2_bias, sum_b_out, sum_b_up, sum_b_down,
    ) = spread
    return (
        layer_out,
        grad_inputs.reshape(inputs.shape),
        ln1_rows[0],
        ln1_rows[1],
        jnp.swapaxes(sum_qkv, 1, 2),
        sum_b_qkv,
        sum_taps,
        sum_shift_skip,
        sum_a.T,
        sum_b.T,
        sum_c.T,
        sum_ssm_skip,
        sum_step,
        sum_out,
        sum_b_out,
        sum_ln2_gain,
        sum_ln2_bias,
        sum_up,
        sum_b_up,
        sum_down,
        sum_b_down,
    )


def solution(mesh):
    in_specs = (
        P(None, "seq", None),
        P(None, "seq", None),
        P(),
        P(),
        P(),
        P(None, None, "head"),
        P(None, "head"),
        P(None, "head"),
        P("head"),
        P("head", None),
        P("head", None),
        P("head", None),
        P("head"),
        P("head"),
        P("head", None),
        P(),
        P(),
        P(),
        P(None, "head"),
        P("head"),
        P("head", None),
        P(),
    )
    out_specs = (
        P(None, "seq", None),
        P(None, "seq", None),
        P(),
        P(),
        P(None, None, "head"),
        P(None, "head"),
        P(None, "head"),
        P("head"),
        P("head", None),
        P("head", None),
        P("head", None),
        P("head"),
        P("head"),
        P("head", None),
        P(),
        P(),
        P(),
        P(None, "head"),
        P("head"),
        P("head", None),
        P(),
    )
    return jax.shard_map(shards, mesh=mesh, in_specs=in_specs, out_specs=out_specs, check_vma=False)
```

```python
import functools

import jax
import jax.numpy as jnp
from jax import lax
from jax.experimental import pallas as pl
from jax.experimental.pallas import tpu as pltpu
from jax.sharding import PartitionSpec as P

norm_epsilon = 1e-05
f32 = jnp.float32
bf16 = jnp.bfloat16
LANES = 128
ORDER = "mmmmEMmmMmMmmMmLmLNMLLNLN"
FLOPS_PER_US = 0.5e9
SUBS = 8


def shifted(shard, axis, by):
    peers = lax.axis_size(axis)
    return lax.ppermute(shard, axis, [(i, i + by) for i in range(peers) if 0 <= i + by < peers])


def swapped(shard, axis, mask):
    return lax.ppermute(shard, axis, [(i, i ^ mask) for i in range(lax.axis_size(axis))])


def halving_steps(call, groups, orders, spot, axis):
    keeps, sends = [g[0] for g in groups], [g[1] for g in groups]
    count = len(orders[0])
    joint = [k > 0 and len({order[k] for order in orders}) == 1 for k in range(count)]

    def shapes(rows, stage):
        rows = [sum(rows)] if joint[stage] else rows
        return [like((r, keeps[0].shape[1]), bf16) for r in rows]

    def trade(blocks, stage):
        return [swapped(block, axis, order[stage]) for block, order in zip(blocks, orders)]

    for stage in range(count):
        gots = trade(sends, stage)
        yield
        rows = [k.shape[0] for k in keeps]
        if stage + 1 < count:
            half = [r // 2 for r in rows]
            masks = tuple(order[stage + 1] for order in orders)
            results = call(
                functools.partial(halve_kernel, masks),
                [like((r, keeps[0].shape[1]), bf16) for r in half] + shapes(half, stage + 1),
                [spot, *keeps, *gots], limit=8, scalars=1,
            )
            keeps, sends = results[: len(half)], results[len(half) :]
        else:
            owns = call(
                functools.partial(sum_kernel, len(keeps)), shapes(rows, stage), [*keeps, *gots], limit=8
            )
    for stage in range(count - 1, -1, -1):
        gots = trade(owns, stage)
        yield
        if not stage:
            return [a for pair in zip(owns, gots) for a in pair]
        masks = tuple(order[stage] for order in orders)
        owns = call(
            functools.partial(double_kernel, joint[stage], masks),
            shapes([2 * r for r in rows], stage - 1),
            [spot, *owns, *gots], limit=8, scalars=1,
        )
        rows = [2 * r for r in rows]


def head_steps(call, keep, send, axis="head"):
    got = swapped(send, axis, 1)
    mask = 2
    while True:
        yield
        if mask >= lax.axis_size(axis):
            (low,) = call(
                functools.partial(sum_kernel, 1), [like(keep.shape, bf16)], [keep, got], limit=8
            )
            return low, swapped(low, axis, 1)
        keep, low = call(
            join_kernel, [like(keep.shape), like(keep.shape, bf16)], [keep, got], limit=8
        )
        got = swapped(low, axis, mask)
        mask *= 2


def carry_steps(call, total, low, whole, spot, axis, ahead):
    carry = jnp.zeros_like(total)
    mask = 1
    while True:
        got = swapped(low, axis, mask)
        if 2 * mask >= lax.axis_size(axis):
            return carry, got
        yield
        more = 4 * mask < lax.axis_size(axis)
        low, carry, *kept = call(
            functools.partial(merge_kernel, mask, ahead),
            [like(total.shape, bf16), like(total.shape)] + [like(total.shape)] * more,
            [spot, whole, total, got, carry],
            limit=8,
            scalars=1,
        )
        total = kept[0] if kept else total
        mask *= 2


def sum_steps(call, rows, axis):
    mask = 1
    while True:
        got = swapped(rows, axis, mask)
        yield
        mask *= 2
        if mask >= lax.axis_size(axis):
            return rows, got
        (rows,) = call(plain_add_kernel, [like(rows.shape)], [rows, got], limit=4)


def ran(steps):
    while True:
        try:
            next(steps)
        except StopIteration as end:
            return end.value


def lane_tiles(width):
    return [slice(i, i + LANES) for i in range(0, width, LANES)]


def folded(product):
    states, lanes = product.shape
    return jnp.sum(product.reshape(states // SUBS, SUBS, lanes), axis=0)


def rows_at(start, size):
    return pl.ds(pl.multiple_of(start, SUBS), size)


def centred_rows(rows):
    centred = rows - jnp.mean(rows, axis=-1, keepdims=True)
    spread = jnp.mean(centred * centred, axis=-1, keepdims=True)
    return centred, lax.rsqrt(spread + norm_epsilon)


def row(vector_ref):
    return vector_ref[...].reshape(1, vector_ref.shape[0])


def wide(array, slots):
    return jnp.concatenate([array] * slots, axis=-1)


def slot_of(array, slot, width):
    return array[:, slot * width : (slot + 1) * width]


def contract(left, right, left_dim, right_dim):
    return lax.dot_general(
        left, right, (((left_dim,), (right_dim,)), ((), ())), preferred_element_type=f32
    )


def run_scan(series_ref, decay_ref, out_ref, reverse):
    blocks = series_ref.shape[0] // SUBS
    tiles = lane_tiles(series_ref.shape[1])
    decays = [decay_ref[:, lanes] for lanes in tiles]

    def one(lap, states):
        place = blocks - 1 - lap if reverse else lap
        at = rows_at(place * SUBS, SUBS)
        blocks_in = [series_ref[at, lanes] for lanes in tiles]
        for r in range(SUBS):
            r = SUBS - 1 - r if reverse else r
            states = [d * s + b[r : r + 1, :] for d, s, b in zip(decays, states, blocks_in)]
        return states

    states = lax.fori_loop(0, blocks, one, [jnp.zeros_like(d) for d in decays])
    for lanes, state in zip(tiles, states):
        out_ref[:, lanes] = state


def part_total(part_ref, rows, base=0):
    total = part_ref[pl.ds(base, rows, stride=SUBS), :]
    for r in range(1, SUBS):
        total = total + part_ref[pl.ds(base + r, rows, stride=SUBS), :]
    return total


def power_of(whole, exponent, mask):
    power, bit = jnp.ones_like(whole), 1
    while bit < mask:
        power = jnp.where((exponent // bit) % 2 == 1, power * whole, power)
        whole = whole * whole
        bit *= 2
    return power, whole


def merged(mask, ahead, place, whole, got, carry):
    inner = place % mask
    far = (place // mask) % 2
    if ahead:
        inner, far = mask - 1 - inner, 1 - far
    power, step = power_of(whole, inner, mask)
    return jnp.where(far == 1, carry + power * got, carry), far, step


def merge_kernel(mask, ahead, spot_ref, whole_ref, total_ref, got_ref, carry_ref, low_ref, out_ref, *sums):
    got = got_ref[...].astype(f32)
    total = total_ref[...]
    out_ref[...], far, step = merged(
        mask, ahead, spot_ref[0], whole_ref[...], got, carry_ref[...]
    )
    total = jnp.where(far == 1, step * got + total, step * total + got)
    for sum_ref in sums:
        sum_ref[...] = total
    low_ref[...] = total.astype(bf16)


def bit_of(spot, mask):
    return (spot[0] // mask) % 2


def split_blocks(refs, rows):
    if len(refs) == len(rows):
        return [ref[...].astype(f32) for ref in refs]
    whole, starts = refs[0][...].astype(f32), [sum(rows[:k]) for k in range(len(rows))]
    return [whole[start : start + r] for start, r in zip(starts, rows)]


def put_blocks(refs, blocks):
    if len(refs) == len(blocks):
        for ref, block in zip(refs, blocks):
            ref[...] = block.astype(bf16)
        return
    start = 0
    for block in blocks:
        refs[0][start : start + block.shape[0], :] = block.astype(bf16)
        start += block.shape[0]


def halve_kernel(masks, spot_ref, *refs):
    count = len(masks)
    keeps = [ref[...].astype(f32) for ref in refs[:count]]
    rows = [keep.shape[0] for keep in keeps]
    ours = next(k for k in range(count, len(refs)) if refs[k].shape[0] == rows[0] // 2)
    totals = [a + b for a, b in zip(keeps, split_blocks(refs[count:ours], rows))]
    pairs = [
        ordered(bit_of(spot_ref, mask), total[: r // 2], total[r // 2 :])
        for mask, total, r in zip(masks, totals, rows)
    ]
    put_blocks(refs[ours : ours + count], [pair[0] for pair in pairs])
    put_blocks(refs[ours + count :], [pair[1] for pair in pairs])


def sum_kernel(count, *refs):
    keeps = [ref[...].astype(f32) for ref in refs[:count]]
    rows = [keep.shape[0] for keep in keeps]
    ours = count + (count if refs[count].shape[0] == rows[0] else 1)
    totals = [a + b for a, b in zip(keeps, split_blocks(refs[count:ours], rows))]
    put_blocks(refs[ours:], totals)


def plain_add_kernel(own_ref, got_ref, out_ref):
    out_ref[...] = own_ref[...] + got_ref[...]


def double_kernel(joint_in, masks, spot_ref, *refs):
    count = len(masks)
    ins = 1 if joint_in else count
    rows = [refs[0].shape[0] // count] * count if joint_in else [ref.shape[0] for ref in refs[:count]]
    owns, gots = split_blocks(refs[:ins], rows), split_blocks(refs[ins : 2 * ins], rows)
    blocks = [
        jnp.concatenate(ordered(bit_of(spot_ref, mask), own, got), axis=0)
        for mask, own, got in zip(masks, owns, gots)
    ]
    put_blocks(refs[2 * ins :], blocks)


def join_kernel(keep_ref, got_ref, total_ref, low_ref):
    total = keep_ref[...].astype(f32) + got_ref[...].astype(f32)
    total_ref[...] = total
    low_ref[...] = total.astype(bf16)


def ordered(bit, own, other):
    return jnp.where(bit == 0, own, other), jnp.where(bit == 0, other, own)


def halves_of(bit, own_ref, other_ref):
    return ordered(bit, own_ref[...].astype(f32), other_ref[...].astype(f32))


def put_halves(bit, first, second, keep_ref, send_ref):
    keep, send = ordered(bit, first, second)
    keep_ref[...] = keep.astype(bf16)
    send_ref[...] = send.astype(bf16)


def project_kernel(
    spot_ref, x_hbm, gain_hbm, bias_hbm, w_hbm, wb_hbm, act_ref, q_ref, k_ref, v_ref,
    x_ref, gain_ref, bias_ref, w_ref, wb_ref, sems,
):
    pairs = ((x_hbm, x_ref), (gain_hbm, gain_ref), (bias_hbm, bias_ref), (w_hbm, w_ref), (wb_hbm, wb_ref))
    copies = [pltpu.make_async_copy(a, b, sems.at[i]) for i, (a, b) in enumerate(pairs)]
    for copy in copies:
        copy.start()
    for copy in copies[:3]:
        copy.wait()
    slots, rows, _ = x_ref.shape
    gain, bias = row(gain_ref), row(bias_ref)
    acts = []
    for s in range(slots):
        centred, root = centred_rows(x_ref[s].astype(f32))
        acts.append((centred * root * gain + bias).astype(bf16))
        act_ref[s * rows : (s + 1) * rows, :] = acts[s]
    for copy in copies[3:]:
        copy.wait()
    kept = [
        jnp.concatenate([contract(a, w_ref[j], 1, 1) + wb_ref[j : j + 1, :] for a in acts], axis=-1)
        for j in range(3)
    ]
    q_ref[...] = kept[0]
    k_ref[...] = kept[1].astype(bf16)
    v_ref[...] = kept[2]


def masked_kernel(spot_ref, lengths_ref, cotangent_ref, low_ref, sum_ref):
    slots, rows, model = cotangent_ref.shape
    spot = spot_ref[0] * rows + lax.broadcasted_iota(jnp.int32, (rows, model), 0)
    total = 0.0
    for s in range(slots):
        grads = jnp.where(spot < lengths_ref[s], cotangent_ref[s], 0.0)
        low_ref[s * rows : (s + 1) * rows, :] = grads.astype(bf16)
        total = total + jnp.sum(grads, axis=0, keepdims=True)
    sum_ref[...] = total


def mix_kernel(
    edge_ref, k_ref, v_ref, taps_ref, skip_ref, decay_ref,
    shifted_ref, u_ref, end_ref, low_ref, ext_ref, wide_ref,
):
    taps, width = edge_ref.shape
    rows = k_ref.shape[0]
    slots = width // taps_ref.shape[1]
    ext_ref[0:taps, :] = edge_ref[...].astype(f32)
    ext_ref[taps : taps + rows, :] = k_ref[...].astype(f32)
    wide_ref[0:taps, :] = wide(taps_ref[...], slots)
    wide_ref[taps : taps + 1, :] = wide(row(skip_ref), slots)
    for lanes in lane_tiles(width):
        total = wide_ref[taps : taps + 1, lanes] * ext_ref[taps : taps + rows, lanes]
        for r in range(SUBS):
            if r:
                block = ext_ref[SUBS - r : taps + rows - r, lanes]
            else:
                block = ext_ref[0 : taps + rows - SUBS, lanes]
            for q in range(taps // SUBS):
                i = SUBS * q + (r if r else SUBS)
                start = taps - SUBS - SUBS * q
                total = total + wide_ref[i - 1 : i, lanes] * block[start : start + rows, :]
        shifted_ref[:, lanes] = total
        u_ref[:, lanes] = total * v_ref[:, lanes]
    run_scan(u_ref, decay_ref, end_ref, False)
    low_ref[...] = end_ref[...].astype(bf16)


def attend_kernel(
    mask, spot_ref, u_ref, decay_ref, weight_ref, whole_ref, got_ref, carry_ref, skip_ref,
    q_ref, w_ref, ssm_ref, gated_ref, start_ref, keep_ref, send_ref, part_ref,
):
    rows, width = u_ref.shape
    chans = w_ref.shape[0]
    slots = width // chans
    blocks = rows // SUBS
    skip = wide(row(skip_ref), slots)
    start_ref[...], _, _ = merged(
        mask, False, spot_ref[0], whole_ref[...], got_ref[...].astype(f32), carry_ref[...]
    )
    for lanes in lane_tiles(width):
        decay = decay_ref[:, lanes]
        weight = weight_ref[:, lanes]

        def one(lap, state, lanes=lanes, decay=decay, weight=weight):
            tile = u_ref[rows_at(lap * SUBS, SUBS), lanes]
            for r in range(SUBS):
                state = decay * state + tile[r : r + 1, :]
                part_ref[rows_at(lap * SUBS * SUBS + r * SUBS, SUBS), :] = folded(weight * state)
            return state

        lax.fori_loop(0, blocks, one, start_ref[:, lanes])
        ssm_ref[:, lanes] = part_total(part_ref, rows) + skip[:, lanes] * u_ref[:, lanes]
    mixture = q_ref[...] * ssm_ref[...]
    terms = []
    for s in range(slots):
        gated = slot_of(mixture, s, chans).astype(bf16)
        gated_ref[s * rows : (s + 1) * rows, :] = gated
        terms.append(contract(gated, w_ref[...], 1, 0))
    half = slots // 2
    put_halves(
        spot_ref[1],
        jnp.concatenate(terms[:half], axis=0),
        jnp.concatenate(terms[half:], axis=0),
        keep_ref,
        send_ref,
    )


def gelu_parts(x):
    root = 0.7978845608028654
    square = x * x
    bend = jnp.tanh(root * (x + 0.044715 * (square * x)))
    value = 0.5 * x * (1.0 + bend)
    slope = 0.5 * (1.0 + bend) + 0.5 * x * (1.0 - bend * bend) * root * (1.0 + 0.134145 * square)
    return value, slope


def feed_kernel(
    mask_one, mask_two, spot_ref, own_ref, other_ref, x_ref, b_out_ref, gain_ref, bias_ref, up_ref, up_bias_ref, down_ref,
    gout_ref, mid_ref, keep_ref, send_ref, out_keep_ref, out_send_ref,
    bias_sum_ref, w_up_ref, w_up_send_ref, w_down_ref, w_down_send_ref, act_ref, hidden_ref, grad_ref,
):
    bias_sum = 0.0
    backs, outs = [], []
    rows = own_ref.shape[0]
    for half, attended in enumerate(halves_of(spot_ref[1], own_ref, other_ref)):
        at = slice(half * rows, (half + 1) * rows)
        middle = x_ref[at, :].astype(f32) + attended + row(b_out_ref)
        mid_ref[at, :] = middle
        centred, root = centred_rows(middle)
        act = (centred * root * row(gain_ref) + row(bias_ref)).astype(bf16)
        act_ref[at, :] = act
        value, slope = gelu_parts(contract(act, up_ref[...], 1, 0) + row(up_bias_ref))
        hidden = value.astype(bf16)
        hidden_ref[at, :] = hidden
        grads = (contract(gout_ref[at, :], down_ref[...], 1, 1) * slope).astype(bf16)
        grad_ref[at, :] = grads
        bias_sum = bias_sum + jnp.sum(grads.astype(f32), axis=0, keepdims=True)
        backs.append(contract(grads, up_ref[...], 1, 1))
        outs.append(contract(hidden, down_ref[...], 1, 0))
    bias_sum_ref[...] = bias_sum
    put_halves(spot_ref[1], backs[0], backs[1], keep_ref, send_ref)
    put_halves(spot_ref[1], outs[0], outs[1], out_keep_ref, out_send_ref)
    sums = contract(act_ref[...], grad_ref[...], 0, 0)
    half = sums.shape[0] // 2
    put_halves(bit_of(spot_ref, mask_one), sums[:half], sums[half:], w_up_ref, w_up_send_ref)
    sums = contract(hidden_ref[...], gout_ref[...], 0, 0)
    half = sums.shape[0] // 2
    put_halves(bit_of(spot_ref, mask_two), sums[:half], sums[half:], w_down_ref, w_down_send_ref)


def norm_grad(grad, hat, root, gain):
    scaled = grad * gain
    inner = jnp.mean(scaled * hat, axis=-1, keepdims=True)
    return root * (scaled - jnp.mean(scaled, axis=-1, keepdims=True) - hat * inner)


def entry_kernel(
    spot_ref, lengths_ref, own_ref, other_ref, x_ref, gain_ref, gmid_ref, mid_ref, b_down_ref,
    out_ref, rows_ref, layer_ref,
):
    slots, rows, model = layer_ref.shape
    half = own_ref.shape[0] // 2
    first, second = halves_of(spot_ref[1], own_ref, other_ref)
    gain_rows = bias_rows = 0.0
    spot = spot_ref[0] * rows + lax.broadcasted_iota(jnp.int32, (rows, model), 0)
    for s in range(slots):
        at = slice(s * rows, (s + 1) * rows)
        held = first if s * rows < half else second
        inside = s * rows % half
        grad = held[inside : inside + rows]
        feed = held[half + inside : half + inside + rows]
        centred, root = centred_rows(x_ref[at, :].astype(f32))
        hat = centred * root
        out_ref[at, :] = gmid_ref[at, :] + norm_grad(grad, hat, root, row(gain_ref))
        gain_rows = gain_rows + jnp.sum(grad * hat, axis=0, keepdims=True)
        bias_rows = bias_rows + jnp.sum(grad, axis=0, keepdims=True)
        total = mid_ref[at, :] + feed + row(b_down_ref)
        layer_ref[s] = jnp.where(spot < lengths_ref[s], total, 0.0)
    rows_ref[...] = jnp.concatenate(
        [gain_rows, bias_rows, jnp.zeros((SUBS - 2, model), f32)], axis=0
    )


def middle_kernel(
    spot_ref, lengths_ref, own_ref, other_ref, mid_ref, cotangent_ref, gain_ref, w_ref, ssm_ref, q_ref, decay_ref,
    gmid_ref, low_ref, gq_ref, gs_ref, front_ref, front_low_ref, rows_ref,
):
    rows, width = ssm_ref.shape
    chans = w_ref.shape[0]
    gain = row(gain_ref)
    gain_rows = bias_rows = mid_rows = 0.0
    kept = []
    half = own_ref.shape[0]
    first, second = halves_of(spot_ref[1], own_ref, other_ref)
    for s in range(width // chans):
        at = slice(s * rows, (s + 1) * rows)
        inside = slice(s * rows % half, s * rows % half + rows)
        grad = (first if s * rows < half else second)[inside, :]
        centred, root = centred_rows(mid_ref[at, :])
        hat = centred * root
        spot = spot_ref[0] * rows + lax.broadcasted_iota(jnp.int32, hat.shape, 0)
        held = jnp.where(spot < lengths_ref[s], cotangent_ref[s], 0.0)
        grad_mid = held + norm_grad(grad, hat, root, gain)
        gmid_ref[at, :] = grad_mid
        low = grad_mid.astype(bf16)
        low_ref[at, :] = low
        gain_rows = gain_rows + jnp.sum(grad * hat, axis=0, keepdims=True)
        bias_rows = bias_rows + jnp.sum(grad, axis=0, keepdims=True)
        mid_rows = mid_rows + jnp.sum(grad_mid, axis=0, keepdims=True)
        kept.append(contract(low, w_ref[...], 1, 1))
    gated = jnp.concatenate(kept, axis=-1)
    gq_ref[...] = (gated * ssm_ref[...]).astype(bf16)
    gs_ref[...] = gated * q_ref[...]
    rows_ref[...] = jnp.zeros_like(rows_ref)
    rows_ref[0:1, :] = gain_rows
    rows_ref[1:2, :] = bias_rows
    rows_ref[2:3, :] = mid_rows
    run_scan(gs_ref, decay_ref, front_ref, True)
    front_low_ref[...] = front_ref[...].astype(bf16)


def local_kernel(
    u_ref, gs_ref, decay_ref, weight_ref, start_ref,
    out_ref, gain_ref, power_ref, reach_ref, part_ref, past_ref,
):
    rows = u_ref.shape[0]
    blocks = rows // SUBS
    states = decay_ref.shape[0]
    for lanes in lane_tiles(u_ref.shape[1]):
        decay = decay_ref[:, lanes]
        weight = weight_ref[:, lanes]

        def rise(lap, carry, lanes=lanes, decay=decay):
            state, reach = carry
            tile = u_ref[rows_at(lap * SUBS, SUBS), lanes]
            for r in range(SUBS):
                past_ref[rows_at(lap * SUBS * states + r * states, states), :] = state
                reach = decay * (reach + state)
                state = decay * state + tile[r : r + 1, :]
            return state, reach

        zero = jnp.zeros_like(decay)
        _, reach = lax.fori_loop(0, blocks, rise, (start_ref[:, lanes], zero))
        reach_ref[:, lanes] = reach

        def fall(lap, carry, lanes=lanes, decay=decay, weight=weight):
            adjoint, gain, power = carry
            place = blocks - 1 - lap
            tile = u_ref[rows_at(place * SUBS, SUBS), lanes]
            grads = gs_ref[rows_at(place * SUBS, SUBS), lanes]
            for r in range(SUBS - 1, -1, -1):
                adjoint = decay * adjoint + grads[r : r + 1, :]
                part_ref[rows_at(place * SUBS * SUBS + r * SUBS, SUBS), :] = folded(weight * adjoint)
                gain = gain + adjoint * tile[r : r + 1, :]
                power = power + adjoint * past_ref[
                    rows_at(place * SUBS * states + r * states, states), :
                ]
            return adjoint, gain, power

        _, gain, power = lax.fori_loop(0, blocks, fall, (zero, zero, zero))
        gain_ref[:, lanes] = gain
        power_ref[:, lanes] = power
        out_ref[:, lanes] = part_total(part_ref, rows)


def unmix_kernel(
    mask, spot_ref, gloc_ref, gs_ref, u_ref, decay_ref, weight_ref, whole_ref, got_ref, carry_ref, gain_ref, power_ref, reach_ref,
    end_ref, v_ref, shifted_ref, edge_ref, k_ref, taps_ref, shift_skip_ref, ssm_skip_ref,
    in_ref, out_ref, root_ref, slope_ref, fall_ref, a_ref, step_ref,
    gk_ref, halo_ref, gv_ref, small_ref, misc_ref,
    part_ref, ext_ref, pad_ref, wide_ref, sums_ref, tap_ref, behind_ref,
):
    rows, width = u_ref.shape
    blocks = rows // SUBS
    taps, chans = taps_ref.shape
    states = decay_ref.shape[0]
    slots = width // chans
    skip = wide(row(ssm_skip_ref), slots)
    behind_ref[...], _, _ = merged(
        mask, True, spot_ref[0], whole_ref[...], got_ref[...].astype(f32), carry_ref[...]
    )
    ext_ref[0:taps, :] = edge_ref[...].astype(f32)
    ext_ref[taps : taps + rows, :] = k_ref[...].astype(f32)
    pad_ref[0:taps, :] = jnp.zeros((taps, width), f32)
    pad_ref[taps + rows : 2 * taps + rows, :] = jnp.zeros((taps, width), f32)
    wide_ref[0:taps, :] = wide(taps_ref[...], slots)
    wide_ref[taps : taps + 1, :] = wide(row(shift_skip_ref), slots)
    tiles = lane_tiles(width)
    decays = [decay_ref[:, lanes] for lanes in tiles]

    def one(lap, carried):
        place = blocks - 1 - lap
        for r in range(SUBS - 1, -1, -1):
            carried = [d * c for d, c in zip(decays, carried)]
            for k, c in enumerate(carried):
                part_ref[rows_at((k * rows + place * SUBS + r) * SUBS, SUBS), :] = folded(c)
        return carried

    lax.fori_loop(
        0, blocks, one, [weight_ref[:, lanes] * behind_ref[:, lanes] for lanes in tiles]
    )
    for k, lanes in enumerate(tiles):
        grad_u = (
            gloc_ref[:, lanes] + part_total(part_ref, rows, k * rows * SUBS) + skip[:, lanes] * gs_ref[:, lanes]
        )
        gv_ref[:, lanes] = (grad_u * shifted_ref[:, lanes]).astype(bf16)
        pad_ref[taps : taps + rows, lanes] = grad_u * v_ref[:, lanes]
        total = wide_ref[taps : taps + 1, lanes] * pad_ref[taps : taps + rows, lanes]
        borrowed = jnp.zeros((taps, LANES), f32)
        for r in range(SUBS):
            block = pad_ref[r : 2 * taps + rows - SUBS + r, lanes]
            for q in range(taps // SUBS + 1):
                i = SUBS * q + r
                if i < 1 or i > taps:
                    continue
                tap = wide_ref[i - 1 : i, lanes]
                live = min(rows, -(-(rows - i) // SUBS) * SUBS)
                start = taps + SUBS * q
                live = min(live, block.shape[0] - start)
                fresh = total[:live] + tap * block[start : start + live, :]
                total = fresh if live == rows else jnp.concatenate([fresh, total[live:]], axis=0)
                idle = (taps - i) // SUBS * SUBS
                start = SUBS * q + idle
                fresh = borrowed[idle:] + tap * block[start : start + taps - idle, :]
                borrowed = fresh if not idle else jnp.concatenate([borrowed[:idle], fresh], axis=0)
        gk_ref[:, lanes] = total
        halo_ref[:, lanes] = borrowed.astype(bf16)
        grad_shifted = pad_ref[taps : taps + rows, lanes]
        for r in range(SUBS):
            block = ext_ref[r : taps + rows - SUBS + r, lanes] if r else ext_ref[:, lanes]
            for q in range(taps // SUBS + 1):
                start = SUBS * q
                i = taps - start - r
                if i < 0:
                    continue
                product = grad_shifted * block[start : start + rows, :]
                sums_ref[SUBS * i : SUBS * (i + 1), :] = folded(product)
        tap_ref[0 : taps + 1, lanes] = part_total(sums_ref, taps + 1)
    gain = gain_ref[...] + behind_ref[...] * decay_ref[...] * end_ref[...]
    power = power_ref[...] + behind_ref[...] * reach_ref[...]

    def slots_total(array):
        total = slot_of(array, 0, chans)
        for s in range(1, slots):
            total = total + slot_of(array, s, chans)
        return total

    gain, power = slots_total(gain), slots_total(power)
    grad_in = out_ref[...] * gain
    grad_rate = grad_in * slope_ref[...] - fall_ref[...] * power
    tap_sums = slots_total(tap_ref[0 : taps + 1, :])
    small_ref[...] = jnp.concatenate(
        [
            tap_sums[1 : taps + 1, :],
            grad_rate * row(step_ref),
            grad_in * root_ref[...],
            in_ref[...] * gain,
        ],
        axis=-1,
    )
    misc_ref[...] = jnp.zeros_like(misc_ref)
    skip_sums = slots_total(jnp.sum(gs_ref[...] * u_ref[...], axis=0, keepdims=True))
    step_sums = jnp.sum(grad_rate * a_ref[...], axis=0, keepdims=True)
    misc_ref[0:1, :] = jnp.concatenate(
        [tap_sums[0:1, :], skip_sums, step_sums, jnp.zeros_like(skip_sums)], axis=-1
    )


def weights_kernel(gq_ref, act_ref, gated_ref, low_ref, out_ref):
    rows, width = gq_ref.shape
    chans = gated_ref.shape[1]
    query = 0.0
    for s in range(width // chans):
        grads = slot_of(gq_ref[...].astype(f32), s, chans).astype(bf16)
        query = query + contract(grads, act_ref[s * rows : (s + 1) * rows, :], 0, 0)
    out_ref[0:chans, :] = query.astype(bf16)
    out_ref[chans : 2 * chans, :] = contract(gated_ref[...], low_ref[...], 0, 0).astype(bf16)


def last_kernel(
    mask_one, mask_two, spot_ref, out_keep_ref, out_send_ref, gq_ref, gk_ref, received_ref, gv_ref, act_ref, w_ref, early_ref, small_ref, misc_ref,
    rows_ref, up_ref, down_ref, keep_ref, send_ref, one_ref, one_send_ref, two_ref,
    two_send_ref, all_ref,
):
    rows, width = gk_ref.shape
    taps = received_ref.shape[0]
    chans = w_ref.shape[1]
    slots = width // chans
    grad_k = jnp.concatenate(
        [
            gk_ref[0 : rows - taps, :],
            gk_ref[rows - taps : rows, :] + received_ref[...].astype(f32),
        ],
        axis=0,
    ).astype(bf16)
    parts = [gq_ref[...].astype(f32), grad_k.astype(f32), gv_ref[...].astype(f32)]
    sums = [0.0, 0.0, 0.0]
    terms, biases = [], []
    for s in range(slots):
        act = act_ref[s * rows : (s + 1) * rows, :]
        term = 0.0
        for j in range(3):
            grads = slot_of(parts[j], s, chans).astype(bf16)
            term = term + contract(grads, w_ref[j], 1, 0)
            if j:
                sums[j] = sums[j] + contract(grads, act, 0, 0)
        terms.append(term)
    half = slots // 2
    count = out_keep_ref.shape[0]
    put_halves(
        spot_ref[1],
        jnp.concatenate(terms[:half], axis=0),
        jnp.concatenate(terms[half:], axis=0),
        keep_ref.at[0:count, :],
        send_ref.at[0:count, :],
    )
    keep_ref[count:, :] = out_keep_ref[...]
    send_ref[count:, :] = out_send_ref[...]
    for j in range(3):
        total = jnp.sum(parts[j], axis=0, keepdims=True)
        bias = slot_of(total, 0, chans)
        for s in range(1, slots):
            bias = bias + slot_of(total, s, chans)
        biases.append(bias)
    place = 0

    def put(block):
        nonlocal place
        all_ref[place : place + block.shape[0], :] = block.astype(f32)
        place += block.shape[0]

    put(early_ref[...])
    put(sums[1])
    put(sums[2])
    put(small_ref[...])
    put(
        jnp.concatenate(
            [
                misc_ref[0:1, :],
                jnp.concatenate(biases + [jnp.zeros_like(biases[0])], axis=-1),
                rows_ref[0:3, :],
                up_ref[...],
                down_ref[...],
                jnp.zeros((2 * SUBS - 7, misc_ref.shape[1]), f32),
            ],
            axis=0,
        )
    )
    put(jnp.zeros((all_ref.shape[0] - place, misc_ref.shape[1]), f32))
    count = all_ref.shape[0] // 4
    quarters = [all_ref[k * count : (k + 1) * count, :] for k in range(4)]
    put_halves(bit_of(spot_ref, mask_one), quarters[0], quarters[1], one_ref, one_send_ref)
    put_halves(bit_of(spot_ref, mask_two), quarters[2], quarters[3], two_ref, two_send_ref)


def widen_kernel(mask_one, mask_two, spot_ref, up_ref, up_got_ref, down_ref, down_got_ref, one_ref, two_ref):
    for mask, own_ref, got_ref, out_ref in (
        (mask_one, up_ref, up_got_ref, one_ref),
        (mask_two, down_ref, down_got_ref, two_ref),
    ):
        half = own_ref.shape[0]
        first, second = halves_of(bit_of(spot_ref, mask), own_ref, got_ref)
        out_ref[0:half, :] = first
        out_ref[half:, :] = second


def spread_kernel(
    chans, taps, mask_one, mask_two, spot_ref, ln1_ref, ln1_got_ref, one_ref, one_got_ref, two_ref, two_got_ref,
    qkv_ref, bias_ref, tap_ref, shift_skip_ref, a_ref, b_ref, c_ref, ssm_skip_ref, step_ref, out_ref,
    gain_ref, norm_bias_ref, out_bias_ref, up_ref, down_ref, entry_gain_ref, entry_bias_ref, all_ref,
):
    entry = ln1_ref[...] + ln1_got_ref[...]
    entry_gain_ref[...] = entry[0:1, :].reshape(entry.shape[1])
    entry_bias_ref[...] = entry[1:2, :].reshape(entry.shape[1])
    quarter = one_ref.shape[0]
    pieces = halves_of(bit_of(spot_ref, mask_one), one_ref, one_got_ref)
    pieces += halves_of(bit_of(spot_ref, mask_two), two_ref, two_got_ref)
    for place, piece in enumerate(pieces):
        all_ref[place * quarter : (place + 1) * quarter, :] = piece
    for j, place in enumerate((0, 2, 3)):
        qkv_ref[j] = all_ref[place * chans : (place + 1) * chans, :]
    out_ref[...] = all_ref[chans : 2 * chans, :]
    base = 4 * chans
    small = all_ref[base : base + taps, :]
    for slot, ref in enumerate((tap_ref, a_ref, b_ref, c_ref)):
        ref[...] = slot_of(small, slot, chans)
    base = base + taps
    misc = all_ref[base : base + SUBS, :]
    for slot, ref in enumerate((shift_skip_ref, ssm_skip_ref, step_ref)):
        ref[...] = slot_of(misc[0:1, :], slot, chans).reshape(chans)
    bias_ref[...] = jnp.concatenate([slot_of(misc[1:2, :], j, chans) for j in range(3)], axis=0)
    for place, ref in enumerate((gain_ref, norm_bias_ref, out_bias_ref, up_ref, down_ref)):
        ref[...] = misc[2 + place : 3 + place, :].reshape(misc.shape[1])


def ordered_calls():
    held = [jnp.zeros((SUBS, LANES), f32)]

    def call(kernel, outs, args, scratch=(), us=0.5, limit=24, scalars=0, place=pltpu.VMEM):
        inputs = len(args)

        def body(*refs):
            given, rest = refs[:inputs], refs[inputs + 1 :]
            rest[len(outs)][...] = refs[inputs][...]
            kernel(*given, *rest[: len(outs)], *rest[len(outs) + 1 :])

        size = sum(a.size * a.dtype.itemsize for a in list(args) + list(outs))
        specs = [pl.BlockSpec(memory_space=pltpu.SMEM)] * scalars
        specs += [pl.BlockSpec(memory_space=place)] * (inputs - scalars)
        specs += [pl.BlockSpec(memory_space=pltpu.VMEM)]
        results = pl.pallas_call(
            body,
            in_specs=specs,
            out_shape=tuple(outs) + (like((SUBS, LANES)),),
            scratch_shapes=list(scratch),
            compiler_params=pltpu.CompilerParams(vmem_limit_bytes=limit << 20),
            cost_estimate=pl.CostEstimate(
                flops=int(us * FLOPS_PER_US), bytes_accessed=0, transcendentals=0
            ),
        )(*args, held[0])
        held[0] = results[-1]
        return results[:-1]

    return call


def like(shape, dtype=f32):
    return jax.ShapeDtypeStruct(shape, dtype)


def shards(
    inputs,
    cotangent,
    lengths,
    ln1_gain,
    ln1_bias,
    query_key_value_weight,
    b_qkv,
    shift_taps,
    shift_skip,
    ssm_a,
    ssm_b,
    ssm_c,
    ssm_skip,
    ssm_step,
    output_weight,
    b_out,
    ln2_gain,
    ln2_bias,
    up_weight,
    up_bias,
    down_weight,
    b_down,
):
    slots, rows, model = inputs.shape
    taps, chans = shift_taps.shape
    states = ssm_a.shape[1]
    width = slots * chans
    tokens = slots * rows
    spot = jnp.stack([lax.axis_index("seq"), lax.axis_index("head") % 2]).astype(jnp.int32)
    peers = lax.axis_size("seq")
    last_mask = peers // 2
    half_tokens = tokens // 2
    half_like = like((half_tokens, model), bf16)
    projections = jnp.swapaxes(query_key_value_weight, 1, 2)
    flat_inputs = inputs.reshape(tokens, model)
    hidden_count = up_bias.shape[0]
    masks = [2**k for k in range(peers.bit_length() - 1)]
    orders = (masks, masks[1::-1] + masks[2:])
    ends = tuple(order[0] for order in orders)
    call = ordered_calls()

    rate = (ssm_step[:, None] * ssm_a).T
    decay = jnp.exp(-rate)
    gain_root = jnp.sqrt(-jnp.expm1(-2.0 * rate))
    turned_b, turned_c = ssm_b.T, ssm_c.T
    in_weight = gain_root * turned_b
    decay_wide = wide(decay, slots)
    whole_wide = wide(jnp.exp(-rate * rows), slots)
    weight_wide = wide(turned_c * in_weight, slots)
    slope = turned_b * jnp.exp(-2.0 * rate) / gain_root
    fall = decay * turned_c * in_weight

    act_one, queries, keys, values = call(
        project_kernel,
        [like((tokens, model), bf16), like((rows, width)), like((rows, width), bf16), like((rows, width))],
        [spot] + [
            pltpu.with_memory_space_constraint(a, pltpu.HBM)
            for a in (inputs, ln1_gain, ln1_bias, projections, b_qkv)
        ],
        [
            pltpu.VMEM(inputs.shape, inputs.dtype),
            pltpu.VMEM(ln1_gain.shape, f32),
            pltpu.VMEM(ln1_bias.shape, f32),
            pltpu.VMEM(projections.shape, projections.dtype),
            pltpu.VMEM(b_qkv.shape, f32),
            pltpu.SemaphoreType.DMA((5,)),
        ],
        us=2.0,
        scalars=1,
        place=pltpu.HBM,
        limit=24,
    )
    edge = shifted(keys[rows - taps :, :], "seq", 1)
    shifted_keys, series, end_local, end_low = call(
        mix_kernel,
        [like((rows, width)), like((rows, width)), like((states, width)), like((states, width), bf16)],
        [edge, keys, values, shift_taps, shift_skip, decay_wide],
        [pltpu.VMEM((taps + rows, width), f32), pltpu.VMEM((taps + SUBS, width), f32)],
        us=2.9,
    )
    steps = carry_steps(call, end_local, end_low, whole_wide, spot, "seq", False)
    next(steps)
    low_out, grad_b_down = call(
        masked_kernel,
        [like((tokens, model), bf16), like((1, model))],
        [spot, lengths, cotangent],
        us=0.8,
        scalars=2,
    )
    carry, got = ran(steps)
    ssm_out, gated, start_state, keep, send = call(
        functools.partial(attend_kernel, last_mask),
        [like((rows, width)), like((tokens, chans), bf16), like((states, width)), half_like, half_like],
        [
            spot, series, decay_wide, weight_wide, whole_wide, got, carry, ssm_skip, queries,
            output_weight,
        ],
        [pltpu.VMEM((rows * SUBS, LANES), f32)],
        us=2.9,
        scalars=1,
    )
    own, other = ran(head_steps(call, keep, send))
    middle, back_keep, back_send, out_keep, out_send, grad_b_up, up_keep, up_send, down_keep, down_send = call(
        functools.partial(feed_kernel, *ends),
        [
            like((tokens, model)),
            half_like,
            half_like,
            half_like,
            half_like,
            like((1, hidden_count)),
            like((model // 2, hidden_count), bf16),
            like((model // 2, hidden_count), bf16),
            like((hidden_count // 2, model), bf16),
            like((hidden_count // 2, model), bf16),
        ],
        [
            spot, own, other, flat_inputs, b_out, ln2_gain, ln2_bias, up_weight, up_bias, down_weight,
            low_out,
        ],
        [
            pltpu.VMEM((tokens, model), bf16),
            pltpu.VMEM((tokens, hidden_count), bf16),
            pltpu.VMEM((tokens, hidden_count), bf16),
        ],
        us=5.0,
        scalars=1,
        limit=32,
    )
    low_middle = early = last_parts = entry_parts = grad_inputs = layer_out = None
    sum_up = sum_down = last_rows = grad_queries = None

    def feed_work():
        nonlocal sum_up, sum_down
        feed_joined = yield from halving_steps(
            call, [(up_keep, up_send), (down_keep, down_send)], orders, spot, "seq"
        )
        sum_up, sum_down = call(
            functools.partial(widen_kernel, *ends),
            [like((model, hidden_count)), like((hidden_count, model))],
            [spot, *feed_joined],
            scalars=1,
            us=2.5,
        )

    def early_work():
        nonlocal early
        while low_middle is None:
            yield
        (early,) = call(
            weights_kernel,
            [like((2 * chans, model), bf16)],
            [grad_queries, act_one, gated, low_middle],
            us=0.5,
        )

    def last_work():
        while last_parts is None:
            yield
        one, one_send, two, two_send = last_parts
        return (
            yield from halving_steps(call, [(one, one_send), (two, two_send)], orders, spot, "seq")
        )

    def entry_work():
        while entry_parts is None:
            yield
        return (yield from sum_steps(call, entry_parts, "seq"))

    def main_work():
        nonlocal low_middle, grad_queries, last_parts, entry_parts, grad_inputs, layer_out, last_rows
        own, other = yield from head_steps(call, back_keep, back_send)
        grad_middle, low_middle, grad_queries, grad_ssm, front_local, front_low, norm_rows = call(
            middle_kernel,
            [
                like((tokens, model)),
                like((tokens, model), bf16),
                like((rows, width), bf16),
                like((rows, width)),
                like((states, width)),
                like((states, width), bf16),
                like((SUBS, model)),
            ],
            [
                spot, lengths, own, other, middle, cotangent, ln2_gain, output_weight, ssm_out, queries,
                decay_wide,
            ],
            us=2.5,
            scalars=2,
        )
        yield
        steps = carry_steps(call, front_local, front_low, whole_wide, spot, "seq", True)
        carry, got = yield from steps
        grad_local, gain_local, power_local, reach = call(
            local_kernel,
            [like((rows, width)), like((states, width)), like((states, width)), like((states, width))],
            [series, grad_ssm, decay_wide, weight_wide, start_state],
            [pltpu.VMEM((rows * SUBS, LANES), f32), pltpu.VMEM((rows * states, LANES), f32)],
            us=5.8,
        )
        yield
        grad_keys, halo, grad_values, small, misc = call(
            functools.partial(unmix_kernel, last_mask),
            [
                like((rows, width)),
                like((taps, width), bf16),
                like((rows, width), bf16),
                like((states, 4 * chans)),
                like((SUBS, 4 * chans)),
            ],
            [
                spot, grad_local, grad_ssm, series, decay_wide, weight_wide, whole_wide, got, carry,
                gain_local, power_local, reach, end_local, values, shifted_keys, edge, keys, shift_taps,
                shift_skip, ssm_skip, in_weight, turned_c, gain_root, slope, fall, ssm_a.T, ssm_step,
            ],
            [
                pltpu.VMEM((width * rows * SUBS // LANES, LANES), f32),
                pltpu.VMEM((taps + rows, width), f32),
                pltpu.VMEM((2 * taps + rows, width), f32),
                pltpu.VMEM((taps + SUBS, width), f32),
                pltpu.VMEM(((taps + 1) * SUBS, LANES), f32),
                pltpu.VMEM((taps + SUBS, width), f32),
                pltpu.VMEM((states, width), f32),
            ],
            us=6.0,
            scalars=1,
        )
        received = shifted(halo, "seq", -1)
        yield
        while early is None:
            step("E")
        unit = 2 * peers * SUBS
        last_rows = -(-(4 * chans + states + 2 * SUBS) // unit) * unit
        quarter = like((last_rows // 4, model), bf16)
        keep, send, one, one_send, two, two_send = call(
            functools.partial(last_kernel, *ends),
            [like((tokens, model), bf16)] * 2 + [quarter, quarter, quarter, quarter],
            [
                spot, out_keep, out_send, grad_queries, grad_keys, received, grad_values, act_one, projections, early, small,
                misc, norm_rows, grad_b_up, grad_b_down,
            ],
            [pltpu.VMEM((last_rows, model), f32)],
            us=1.5,
            scalars=1,
        )
        last_parts = (one, one_send, two, two_send)
        step("L")
        own, other = yield from head_steps(call, keep, send)
        yield
        grad_inputs, rows_sum, layer_out = call(
            entry_kernel,
            [like((tokens, model)), like((SUBS, model)), like(inputs.shape)],
            [spot, lengths, own, other, flat_inputs, ln1_gain, grad_middle, middle, b_down],
            scalars=2,
            us=3.0,
        )
        entry_parts = rows_sum
        step("N")

    works = {"m": main_work(), "M": feed_work(), "E": early_work(), "L": last_work(), "N": entry_work()}
    ended = {}

    def step(name):
        if name not in ended:
            try:
                next(works[name])
            except StopIteration as end:
                ended[name] = end.value

    step("M")
    for name in ORDER:
        step(name)
    for name in "mMLN":
        while name not in ended:
            step(name)
    joined, ln1_parts = ended["L"], ended["N"]
    spread = call(
        functools.partial(spread_kernel, chans, taps, *ends),
        [
            like((3, chans, model)),
            like((3, chans)),
            like((taps, chans)),
            like((chans,)),
            like((states, chans)),
            like((states, chans)),
            like((states, chans)),
            like((chans,)),
            like((chans,)),
            like((chans, model)),
            like((model,)),
            like((model,)),
            like((model,)),
            like(up_bias.shape),
            like((model,)),
            like((model,)),
            like((model,)),
        ],
        [spot, *ln1_parts, *joined],
        [pltpu.VMEM((last_rows, model), f32)],
        scalars=1,
        us=2.0,
    )
    (
        sum_qkv, sum_b_qkv, sum_taps, sum_shift_skip, sum_a, sum_b, sum_c, sum_ssm_skip, sum_step,
        sum_out, sum_ln2_gain, sum_ln2_bias, sum_b_out, sum_b_up, sum_b_down,
        sum_ln1_gain, sum_ln1_bias,
    ) = spread
    return (
        layer_out,
        grad_inputs.reshape(inputs.shape),
        sum_ln1_gain,
        sum_ln1_bias,
        jnp.swapaxes(sum_qkv, 1, 2),
        sum_b_qkv,
        sum_taps,
        sum_shift_skip,
        sum_a.T,
        sum_b.T,
        sum_c.T,
        sum_ssm_skip,
        sum_step,
        sum_out,
        sum_b_out,
        sum_ln2_gain,
        sum_ln2_bias,
        sum_up,
        sum_b_up,
        sum_down,
        sum_b_down,
    )


def solution(mesh):
    in_specs = (
        P(None, "seq", None),
        P(None, "seq", None),
        P(),
        P(),
        P(),
        P(None, None, "head"),
        P(None, "head"),
        P(None, "head"),
        P("head"),
        P("head", None),
        P("head", None),
        P("head", None),
        P("head"),
        P("head"),
        P("head", None),
        P(),
        P(),
        P(),
        P(None, "head"),
        P("head"),
        P("head", None),
        P(),
    )
    out_specs = (
        P(None, "seq", None),
        P(None, "seq", None),
        P(),
        P(),
        P(None, None, "head"),
        P(None, "head"),
        P(None, "head"),
        P("head"),
        P("head", None),
        P("head", None),
        P("head", None),
        P("head"),
        P("head"),
        P("head", None),
        P(),
        P(),
        P(),
        P(None, "head"),
        P("head"),
        P("head", None),
        P(),
    )
    return jax.shard_map(shards, mesh=mesh, in_specs=in_specs, out_specs=out_specs, check_vma=False)
```

```python
import functools

import jax
import jax.numpy as jnp
from jax import lax
from jax.experimental import pallas as pl
from jax.experimental.pallas import tpu as pltpu
from jax.sharding import PartitionSpec as P

norm_epsilon = 1e-05
f32 = jnp.float32
bf16 = jnp.bfloat16
LANES = 128
ORDER = "mmmmEmMmMmMmmMmLmLNMLLNLN"
FLOPS_PER_US = 0.54e9
SUBS = 8


def shifted(shard, axis, by):
    peers = lax.axis_size(axis)
    return lax.ppermute(shard, axis, [(i, i + by) for i in range(peers) if 0 <= i + by < peers])


def swapped(shard, axis, mask):
    return lax.ppermute(shard, axis, [(i, i ^ mask) for i in range(lax.axis_size(axis))])


def halving_steps(call, groups, orders, spot, axis):
    keeps, sends = [g[0] for g in groups], [g[1] for g in groups]
    count = len(orders[0])
    joint = [k > 0 and len({order[k] for order in orders}) == 1 for k in range(count)]

    def shapes(rows, stage):
        rows = [sum(rows)] if joint[stage] else rows
        return [like((r, keeps[0].shape[1]), bf16) for r in rows]

    def trade(blocks, stage):
        return [swapped(block, axis, order[stage]) for block, order in zip(blocks, orders)]

    for stage in range(count):
        gots = trade(sends, stage)
        yield
        rows = [k.shape[0] for k in keeps]
        if stage + 1 < count:
            half = [r // 2 for r in rows]
            masks = tuple(order[stage + 1] for order in orders)
            results = call(
                functools.partial(halve_kernel, masks),
                [like((r, keeps[0].shape[1]), bf16) for r in half] + shapes(half, stage + 1),
                [spot, *keeps, *gots], limit=8, scalars=1,
            )
            keeps, sends = results[: len(half)], results[len(half) :]
        else:
            owns = call(
                functools.partial(sum_kernel, len(keeps)), shapes(rows, stage), [*keeps, *gots], limit=8
            )
    for stage in range(count - 1, -1, -1):
        gots = trade(owns, stage)
        yield
        if not stage:
            return [a for pair in zip(owns, gots) for a in pair]
        masks = tuple(order[stage] for order in orders)
        owns = call(
            functools.partial(double_kernel, joint[stage], masks),
            shapes([2 * r for r in rows], stage - 1),
            [spot, *owns, *gots], limit=8, scalars=1,
        )
        rows = [2 * r for r in rows]


def head_steps(call, keep, send, axis="head"):
    got = swapped(send, axis, 1)
    mask = 2
    while True:
        yield
        if mask >= lax.axis_size(axis):
            (low,) = call(
                functools.partial(sum_kernel, 1), [like(keep.shape, bf16)], [keep, got], limit=8
            )
            return low, swapped(low, axis, 1)
        keep, low = call(
            join_kernel, [like(keep.shape), like(keep.shape, bf16)], [keep, got], limit=8
        )
        got = swapped(low, axis, mask)
        mask *= 2


def carry_steps(call, total, low, whole, spot, axis, ahead):
    carry = jnp.zeros_like(total)
    mask = 1
    while True:
        got = swapped(low, axis, mask)
        if 2 * mask >= lax.axis_size(axis):
            return carry, got
        yield
        more = 4 * mask < lax.axis_size(axis)
        low, carry, *kept = call(
            functools.partial(merge_kernel, mask, ahead),
            [like(total.shape, bf16), like(total.shape)] + [like(total.shape)] * more,
            [spot, whole, total, got, carry],
            limit=8,
            scalars=1,
        )
        total = kept[0] if kept else total
        mask *= 2


def plain_head_total(keep, send, axis="head"):
    total = keep.astype(f32) + swapped(send, axis, 1).astype(f32)
    mask = 2
    while mask < lax.axis_size(axis):
        total = total + swapped(total.astype(bf16), axis, mask).astype(f32)
        mask *= 2
    low = total.astype(bf16)
    return low, swapped(low, axis, 1)


def plain_carry(total, low, whole, place, axis):
    carry = jnp.zeros_like(total)
    mask, step = 1, whole
    while True:
        got = swapped(low, axis, mask)
        if 2 * mask >= lax.axis_size(axis):
            return carry, got
        far = (place & mask) > 0
        power, bit, base = jnp.ones_like(whole), 1, whole
        while bit < mask:
            power = jnp.where((place & bit) > 0, power * base, power)
            base = base * base
            bit *= 2
        got = got.astype(f32)
        carry = carry + jnp.where(far, power, 0.0) * got
        total = jnp.where(far, step, 1.0) * got + jnp.where(far, 1.0, step) * total
        low = total.astype(bf16)
        step = step * step
        mask *= 2


def sum_steps(call, rows, masks, axis):
    for mask in masks[:-1]:
        got = swapped(rows, axis, mask)
        yield
        (rows,) = call(plain_add_kernel, [like(rows.shape)], [rows, got], limit=4)
    got = swapped(rows, axis, masks[-1])
    yield
    return rows, got


def ran(steps):
    while True:
        try:
            next(steps)
        except StopIteration as end:
            return end.value


def lane_tiles(width):
    return [slice(i, i + LANES) for i in range(0, width, LANES)]


def folded(product):
    states, lanes = product.shape
    return jnp.sum(product.reshape(states // SUBS, SUBS, lanes), axis=0)


def rows_at(start, size):
    return pl.ds(pl.multiple_of(start, SUBS), size)


def centred_rows(rows):
    centred = rows - jnp.mean(rows, axis=-1, keepdims=True)
    spread = jnp.mean(centred * centred, axis=-1, keepdims=True)
    return centred, lax.rsqrt(spread + norm_epsilon)


def row(vector_ref):
    return vector_ref[...].reshape(1, vector_ref.shape[0])


def wide(array, slots):
    return jnp.concatenate([array] * slots, axis=-1)


def slot_of(array, slot, width):
    return array[:, slot * width : (slot + 1) * width]


def contract(left, right, left_dim, right_dim):
    return lax.dot_general(
        left, right, (((left_dim,), (right_dim,)), ((), ())), preferred_element_type=f32
    )


def run_scan(series_ref, decay_ref, out_ref, reverse):
    blocks = series_ref.shape[0] // SUBS
    tiles = lane_tiles(series_ref.shape[1])
    decays = [decay_ref[:, lanes] for lanes in tiles]

    def one(lap, states):
        place = blocks - 1 - lap if reverse else lap
        at = rows_at(place * SUBS, SUBS)
        blocks_in = [series_ref[at, lanes] for lanes in tiles]
        for r in range(SUBS):
            r = SUBS - 1 - r if reverse else r
            states = [d * s + b[r : r + 1, :] for d, s, b in zip(decays, states, blocks_in)]
        return states

    states = lax.fori_loop(0, blocks, one, [jnp.zeros_like(d) for d in decays])
    for lanes, state in zip(tiles, states):
        out_ref[:, lanes] = state


def part_total(part_ref, rows, base=0):
    total = part_ref[pl.ds(base, rows, stride=SUBS), :]
    for r in range(1, SUBS):
        total = total + part_ref[pl.ds(base + r, rows, stride=SUBS), :]
    return total


def power_of(whole, exponent, mask):
    power, bit = jnp.ones_like(whole), 1
    while bit < mask:
        power = jnp.where((exponent // bit) % 2 == 1, power * whole, power)
        whole = whole * whole
        bit *= 2
    return power, whole


def merged(mask, ahead, place, whole, got, carry):
    inner = place % mask
    far = (place // mask) % 2
    if ahead:
        inner, far = mask - 1 - inner, 1 - far
    power, step = power_of(whole, inner, mask)
    return jnp.where(far == 1, carry + power * got, carry), far, step


def merge_kernel(mask, ahead, spot_ref, whole_ref, total_ref, got_ref, carry_ref, low_ref, out_ref, *sums):
    got = got_ref[...].astype(f32)
    total = total_ref[...]
    out_ref[...], far, step = merged(
        mask, ahead, spot_ref[0], whole_ref[...], got, carry_ref[...]
    )
    total = jnp.where(far == 1, step * got + total, step * total + got)
    for sum_ref in sums:
        sum_ref[...] = total
    low_ref[...] = total.astype(bf16)


def bit_of(spot, mask):
    return (spot[0] // mask) % 2


def split_blocks(refs, rows):
    if len(refs) == len(rows):
        return [ref[...].astype(f32) for ref in refs]
    whole, starts = refs[0][...].astype(f32), [sum(rows[:k]) for k in range(len(rows))]
    return [whole[start : start + r] for start, r in zip(starts, rows)]


def put_blocks(refs, blocks):
    if len(refs) == len(blocks):
        for ref, block in zip(refs, blocks):
            ref[...] = block.astype(bf16)
        return
    start = 0
    for block in blocks:
        refs[0][start : start + block.shape[0], :] = block.astype(bf16)
        start += block.shape[0]


def halve_kernel(masks, spot_ref, *refs):
    count = len(masks)
    keeps = [ref[...].astype(f32) for ref in refs[:count]]
    rows = [keep.shape[0] for keep in keeps]
    ours = next(k for k in range(count, len(refs)) if refs[k].shape[0] == rows[0] // 2)
    totals = [a + b for a, b in zip(keeps, split_blocks(refs[count:ours], rows))]
    pairs = [
        ordered(bit_of(spot_ref, mask), total[: r // 2], total[r // 2 :])
        for mask, total, r in zip(masks, totals, rows)
    ]
    put_blocks(refs[ours : ours + count], [pair[0] for pair in pairs])
    put_blocks(refs[ours + count :], [pair[1] for pair in pairs])


def sum_kernel(count, *refs):
    keeps = [ref[...].astype(f32) for ref in refs[:count]]
    rows = [keep.shape[0] for keep in keeps]
    ours = count + (count if refs[count].shape[0] == rows[0] else 1)
    totals = [a + b for a, b in zip(keeps, split_blocks(refs[count:ours], rows))]
    put_blocks(refs[ours:], totals)


def plain_add_kernel(own_ref, got_ref, out_ref):
    out_ref[...] = own_ref[...] + got_ref[...]


def double_kernel(joint_in, masks, spot_ref, *refs):
    count = len(masks)
    ins = 1 if joint_in else count
    rows = [refs[0].shape[0] // count] * count if joint_in else [ref.shape[0] for ref in refs[:count]]
    owns, gots = split_blocks(refs[:ins], rows), split_blocks(refs[ins : 2 * ins], rows)
    blocks = [
        jnp.concatenate(ordered(bit_of(spot_ref, mask), own, got), axis=0)
        for mask, own, got in zip(masks, owns, gots)
    ]
    put_blocks(refs[2 * ins :], blocks)


def join_kernel(keep_ref, got_ref, total_ref, low_ref):
    total = keep_ref[...].astype(f32) + got_ref[...].astype(f32)
    total_ref[...] = total
    low_ref[...] = total.astype(bf16)


def ordered(bit, own, other):
    return jnp.where(bit == 0, own, other), jnp.where(bit == 0, other, own)


def halves_of(bit, own_ref, other_ref):
    return ordered(bit, own_ref[...].astype(f32), other_ref[...].astype(f32))


def put_halves(bit, first, second, keep_ref, send_ref):
    keep, send = ordered(bit, first, second)
    keep_ref[...] = keep.astype(bf16)
    send_ref[...] = send.astype(bf16)


def project_kernel(
    spot_ref, x_hbm, gain_hbm, bias_hbm, w_hbm, wb_hbm, act_ref, q_ref, k_ref, v_ref,
    x_ref, gain_ref, bias_ref, w_ref, wb_ref, sems,
):
    pairs = ((x_hbm, x_ref), (gain_hbm, gain_ref), (bias_hbm, bias_ref), (w_hbm, w_ref), (wb_hbm, wb_ref))
    copies = [pltpu.make_async_copy(a, b, sems.at[i]) for i, (a, b) in enumerate(pairs)]
    for copy in copies:
        copy.start()
    for copy in copies[:3]:
        copy.wait()
    slots, rows, _ = x_ref.shape
    gain, bias = row(gain_ref), row(bias_ref)
    acts = []
    for s in range(slots):
        centred, root = centred_rows(x_ref[s].astype(f32))
        acts.append((centred * root * gain + bias).astype(bf16))
        act_ref[s * rows : (s + 1) * rows, :] = acts[s]
    for copy in copies[3:]:
        copy.wait()
    kept = [
        jnp.concatenate([contract(a, w_ref[j], 1, 1) + wb_ref[j : j + 1, :] for a in acts], axis=-1)
        for j in range(3)
    ]
    q_ref[...] = kept[0]
    k_ref[...] = kept[1].astype(bf16)
    v_ref[...] = kept[2]


def masked_kernel(spot_ref, lengths_ref, cotangent_ref, low_ref, sum_ref):
    slots, rows, model = cotangent_ref.shape
    spot = spot_ref[0] * rows + lax.broadcasted_iota(jnp.int32, (rows, model), 0)
    total = 0.0
    for s in range(slots):
        grads = jnp.where(spot < lengths_ref[s], cotangent_ref[s], 0.0)
        low_ref[s * rows : (s + 1) * rows, :] = grads.astype(bf16)
        total = total + jnp.sum(grads, axis=0, keepdims=True)
    sum_ref[...] = total


def mix_kernel(
    edge_ref, k_ref, v_ref, taps_ref, skip_ref, decay_ref,
    shifted_ref, u_ref, end_ref, low_ref, ext_ref, wide_ref,
):
    taps, width = edge_ref.shape
    rows = k_ref.shape[0]
    slots = width // taps_ref.shape[1]
    ext_ref[0:taps, :] = edge_ref[...].astype(f32)
    ext_ref[taps : taps + rows, :] = k_ref[...].astype(f32)
    wide_ref[0:taps, :] = wide(taps_ref[...], slots)
    wide_ref[taps : taps + 1, :] = wide(row(skip_ref), slots)
    for lanes in lane_tiles(width):
        total = wide_ref[taps : taps + 1, lanes] * ext_ref[taps : taps + rows, lanes]
        for r in range(SUBS):
            if r:
                block = ext_ref[SUBS - r : taps + rows - r, lanes]
            else:
                block = ext_ref[0 : taps + rows - SUBS, lanes]
            for q in range(taps // SUBS):
                i = SUBS * q + (r if r else SUBS)
                start = taps - SUBS - SUBS * q
                total = total + wide_ref[i - 1 : i, lanes] * block[start : start + rows, :]
        shifted_ref[:, lanes] = total
        u_ref[:, lanes] = total * v_ref[:, lanes]
    run_scan(u_ref, decay_ref, end_ref, False)
    low_ref[...] = end_ref[...].astype(bf16)


def attend_kernel(
    mask, spot_ref, u_ref, decay_ref, weight_ref, whole_ref, got_ref, carry_ref, skip_ref,
    q_ref, w_ref, ssm_ref, gated_ref, start_ref, keep_ref, send_ref, part_ref,
):
    rows, width = u_ref.shape
    chans = w_ref.shape[0]
    slots = width // chans
    blocks = rows // SUBS
    skip = wide(row(skip_ref), slots)
    start_ref[...], _, _ = merged(
        mask, False, spot_ref[0], whole_ref[...], got_ref[...].astype(f32), carry_ref[...]
    )
    for lanes in lane_tiles(width):
        decay = decay_ref[:, lanes]
        weight = weight_ref[:, lanes]

        def one(lap, state, lanes=lanes, decay=decay, weight=weight):
            tile = u_ref[rows_at(lap * SUBS, SUBS), lanes]
            for r in range(SUBS):
                state = decay * state + tile[r : r + 1, :]
                part_ref[rows_at(lap * SUBS * SUBS + r * SUBS, SUBS), :] = folded(weight * state)
            return state

        lax.fori_loop(0, blocks, one, start_ref[:, lanes])
        ssm_ref[:, lanes] = part_total(part_ref, rows) + skip[:, lanes] * u_ref[:, lanes]
    mixture = q_ref[...] * ssm_ref[...]
    terms = []
    for s in range(slots):
        gated = slot_of(mixture, s, chans).astype(bf16)
        gated_ref[s * rows : (s + 1) * rows, :] = gated
        terms.append(contract(gated, w_ref[...], 1, 0))
    half = slots // 2
    put_halves(
        spot_ref[1],
        jnp.concatenate(terms[:half], axis=0),
        jnp.concatenate(terms[half:], axis=0),
        keep_ref,
        send_ref,
    )


def gelu_parts(x):
    root = 0.7978845608028654
    square = x * x
    bend = jnp.tanh(root * (x + 0.044715 * (square * x)))
    value = 0.5 * x * (1.0 + bend)
    slope = 0.5 * (1.0 + bend) + 0.5 * x * (1.0 - bend * bend) * root * (1.0 + 0.134145 * square)
    return value, slope


def feed_kernel(
    mask_one, mask_two, spot_ref, own_ref, other_ref, x_ref, b_out_ref, gain_ref, bias_ref, up_ref, up_bias_ref, down_ref,
    gout_ref, mid_ref, keep_ref, send_ref, out_keep_ref, out_send_ref,
    bias_sum_ref, w_up_ref, w_up_send_ref, w_down_ref, w_down_send_ref, act_ref, hidden_ref, grad_ref,
):
    bias_sum = 0.0
    backs, outs = [], []
    rows = own_ref.shape[0]
    for half, attended in enumerate(halves_of(spot_ref[1], own_ref, other_ref)):
        at = slice(half * rows, (half + 1) * rows)
        middle = x_ref[at, :].astype(f32) + attended + row(b_out_ref)
        mid_ref[at, :] = middle
        centred, root = centred_rows(middle)
        act = (centred * root * row(gain_ref) + row(bias_ref)).astype(bf16)
        act_ref[at, :] = act
        value, slope = gelu_parts(contract(act, up_ref[...], 1, 0) + row(up_bias_ref))
        hidden = value.astype(bf16)
        hidden_ref[at, :] = hidden
        grads = (contract(gout_ref[at, :], down_ref[...], 1, 1) * slope).astype(bf16)
        grad_ref[at, :] = grads
        bias_sum = bias_sum + jnp.sum(grads.astype(f32), axis=0, keepdims=True)
        backs.append(contract(grads, up_ref[...], 1, 1))
        outs.append(contract(hidden, down_ref[...], 1, 0))
    bias_sum_ref[...] = bias_sum
    put_halves(spot_ref[1], backs[0], backs[1], keep_ref, send_ref)
    put_halves(spot_ref[1], outs[0], outs[1], out_keep_ref, out_send_ref)
    sums = contract(act_ref[...], grad_ref[...], 0, 0)
    half = sums.shape[0] // 2
    put_halves(bit_of(spot_ref, mask_one), sums[:half], sums[half:], w_up_ref, w_up_send_ref)
    sums = contract(hidden_ref[...], gout_ref[...], 0, 0)
    half = sums.shape[0] // 2
    put_halves(bit_of(spot_ref, mask_two), sums[:half], sums[half:], w_down_ref, w_down_send_ref)


def norm_grad(grad, hat, root, gain):
    scaled = grad * gain
    inner = jnp.mean(scaled * hat, axis=-1, keepdims=True)
    return root * (scaled - jnp.mean(scaled, axis=-1, keepdims=True) - hat * inner)


def entry_kernel(
    spot_ref, lengths_ref, own_ref, other_ref, x_ref, gain_ref, gmid_ref, mid_ref, b_down_ref,
    out_ref, rows_ref, layer_ref,
):
    slots, rows, model = layer_ref.shape
    half = own_ref.shape[0] // 2
    first, second = halves_of(spot_ref[1], own_ref, other_ref)
    gain_rows = bias_rows = 0.0
    spot = spot_ref[0] * rows + lax.broadcasted_iota(jnp.int32, (rows, model), 0)
    for s in range(slots):
        at = slice(s * rows, (s + 1) * rows)
        held = first if s * rows < half else second
        inside = s * rows % half
        grad = held[inside : inside + rows]
        feed = held[half + inside : half + inside + rows]
        centred, root = centred_rows(x_ref[at, :].astype(f32))
        hat = centred * root
        out_ref[at, :] = gmid_ref[at, :] + norm_grad(grad, hat, root, row(gain_ref))
        gain_rows = gain_rows + jnp.sum(grad * hat, axis=0, keepdims=True)
        bias_rows = bias_rows + jnp.sum(grad, axis=0, keepdims=True)
        total = mid_ref[at, :] + feed + row(b_down_ref)
        layer_ref[s] = jnp.where(spot < lengths_ref[s], total, 0.0)
    rows_ref[...] = jnp.concatenate(
        [gain_rows, bias_rows, jnp.zeros((SUBS - 2, model), f32)], axis=0
    )


def middle_kernel(
    spot_ref, lengths_ref, own_ref, other_ref, mid_ref, cotangent_ref, gain_ref, w_ref, ssm_ref, q_ref, decay_ref,
    gmid_ref, low_ref, gq_ref, gs_ref, front_ref, front_low_ref, rows_ref,
):
    rows, width = ssm_ref.shape
    chans = w_ref.shape[0]
    gain = row(gain_ref)
    gain_rows = bias_rows = mid_rows = 0.0
    kept = []
    half = own_ref.shape[0]
    first, second = halves_of(spot_ref[1], own_ref, other_ref)
    for s in range(width // chans):
        at = slice(s * rows, (s + 1) * rows)
        inside = slice(s * rows % half, s * rows % half + rows)
        grad = (first if s * rows < half else second)[inside, :]
        centred, root = centred_rows(mid_ref[at, :])
        hat = centred * root
        spot = spot_ref[0] * rows + lax.broadcasted_iota(jnp.int32, hat.shape, 0)
        held = jnp.where(spot < lengths_ref[s], cotangent_ref[s], 0.0)
        grad_mid = held + norm_grad(grad, hat, root, gain)
        gmid_ref[at, :] = grad_mid
        low = grad_mid.astype(bf16)
        low_ref[at, :] = low
        gain_rows = gain_rows + jnp.sum(grad * hat, axis=0, keepdims=True)
        bias_rows = bias_rows + jnp.sum(grad, axis=0, keepdims=True)
        mid_rows = mid_rows + jnp.sum(grad_mid, axis=0, keepdims=True)
        kept.append(contract(low, w_ref[...], 1, 1))
    gated = jnp.concatenate(kept, axis=-1)
    gq_ref[...] = (gated * ssm_ref[...]).astype(bf16)
    gs_ref[...] = gated * q_ref[...]
    rows_ref[...] = jnp.zeros_like(rows_ref)
    rows_ref[0:1, :] = gain_rows
    rows_ref[1:2, :] = bias_rows
    rows_ref[2:3, :] = mid_rows
    run_scan(gs_ref, decay_ref, front_ref, True)
    front_low_ref[...] = front_ref[...].astype(bf16)


def reach_kernel(u_ref, decay_ref, reach_ref):
    blocks = u_ref.shape[0] // SUBS
    for lanes in lane_tiles(u_ref.shape[1]):
        decay = decay_ref[:, lanes]

        def rise(lap, carry, lanes=lanes, decay=decay):
            state, reach = carry
            tile = u_ref[rows_at(lap * SUBS, SUBS), lanes]
            for r in range(SUBS):
                reach = decay * (reach + state)
                state = decay * state + tile[r : r + 1, :]
            return state, reach

        zero = jnp.zeros_like(decay)
        reach_ref[:, lanes] = lax.fori_loop(0, blocks, rise, (zero, zero))[1]


def local_kernel(
    u_ref, gs_ref, decay_ref, weight_ref, start_ref, out_ref, gain_ref, power_ref, part_ref
):
    rows = u_ref.shape[0]
    blocks = rows // SUBS
    for lanes in lane_tiles(u_ref.shape[1]):
        decay = decay_ref[:, lanes]
        weight = weight_ref[:, lanes]

        def fall(lap, carry, lanes=lanes, decay=decay, weight=weight):
            adjoint, slope, gain, power = carry
            place = blocks - 1 - lap
            tile = u_ref[rows_at(place * SUBS, SUBS), lanes]
            grads = gs_ref[rows_at(place * SUBS, SUBS), lanes]
            for r in range(SUBS - 1, -1, -1):
                slope = decay * slope + adjoint
                adjoint = decay * adjoint + grads[r : r + 1, :]
                part_ref[rows_at(place * SUBS * SUBS + r * SUBS, SUBS), :] = folded(weight * adjoint)
                gain = gain + adjoint * tile[r : r + 1, :]
                power = power + slope * tile[r : r + 1, :]
            return adjoint, slope, gain, power

        zero = jnp.zeros_like(decay)
        adjoint, slope, gain, power = lax.fori_loop(0, blocks, fall, (zero, zero, zero, zero))
        gain_ref[:, lanes] = gain
        power_ref[:, lanes] = power + start_ref[:, lanes] * (decay * slope + adjoint)
        out_ref[:, lanes] = part_total(part_ref, rows)


def unmix_kernel(
    mask, spot_ref, gloc_ref, gs_ref, u_ref, decay_ref, weight_ref, whole_ref, got_ref, carry_ref, gain_ref, power_ref, reach_ref, start_ref,
    end_ref, v_ref, shifted_ref, edge_ref, k_ref, taps_ref, shift_skip_ref, ssm_skip_ref,
    in_ref, out_ref, root_ref, slope_ref, fall_ref, a_ref, step_ref,
    gk_ref, halo_ref, gv_ref, small_ref, misc_ref,
    part_ref, ext_ref, pad_ref, wide_ref, sums_ref, tap_ref, behind_ref,
):
    rows, width = u_ref.shape
    blocks = rows // SUBS
    taps, chans = taps_ref.shape
    states = decay_ref.shape[0]
    slots = width // chans
    skip = wide(row(ssm_skip_ref), slots)
    behind_ref[...], _, _ = merged(
        mask, True, spot_ref[0], whole_ref[...], got_ref[...].astype(f32), carry_ref[...]
    )
    ext_ref[0:taps, :] = edge_ref[...].astype(f32)
    ext_ref[taps : taps + rows, :] = k_ref[...].astype(f32)
    pad_ref[0:taps, :] = jnp.zeros((taps, width), f32)
    pad_ref[taps + rows : 2 * taps + rows, :] = jnp.zeros((taps, width), f32)
    wide_ref[0:taps, :] = wide(taps_ref[...], slots)
    wide_ref[taps : taps + 1, :] = wide(row(shift_skip_ref), slots)
    tiles = lane_tiles(width)
    decays = [decay_ref[:, lanes] for lanes in tiles]

    def one(lap, carried):
        place = blocks - 1 - lap
        for r in range(SUBS - 1, -1, -1):
            carried = [d * c for d, c in zip(decays, carried)]
            for k, c in enumerate(carried):
                part_ref[rows_at((k * rows + place * SUBS + r) * SUBS, SUBS), :] = folded(c)
        return carried

    lax.fori_loop(
        0, blocks, one, [weight_ref[:, lanes] * behind_ref[:, lanes] for lanes in tiles]
    )
    for k, lanes in enumerate(tiles):
        grad_u = (
            gloc_ref[:, lanes] + part_total(part_ref, rows, k * rows * SUBS) + skip[:, lanes] * gs_ref[:, lanes]
        )
        gv_ref[:, lanes] = (grad_u * shifted_ref[:, lanes]).astype(bf16)
        pad_ref[taps : taps + rows, lanes] = grad_u * v_ref[:, lanes]
        total = wide_ref[taps : taps + 1, lanes] * pad_ref[taps : taps + rows, lanes]
        borrowed = jnp.zeros((taps, LANES), f32)
        for r in range(SUBS):
            block = pad_ref[r : 2 * taps + rows - SUBS + r, lanes]
            for q in range(taps // SUBS + 1):
                i = SUBS * q + r
                if i < 1 or i > taps:
                    continue
                tap = wide_ref[i - 1 : i, lanes]
                live = min(rows, -(-(rows - i) // SUBS) * SUBS)
                start = taps + SUBS * q
                live = min(live, block.shape[0] - start)
                fresh = total[:live] + tap * block[start : start + live, :]
                total = fresh if live == rows else jnp.concatenate([fresh, total[live:]], axis=0)
                idle = (taps - i) // SUBS * SUBS
                start = SUBS * q + idle
                fresh = borrowed[idle:] + tap * block[start : start + taps - idle, :]
                borrowed = fresh if not idle else jnp.concatenate([borrowed[:idle], fresh], axis=0)
        gk_ref[:, lanes] = total
        halo_ref[:, lanes] = borrowed.astype(bf16)
        grad_shifted = pad_ref[taps : taps + rows, lanes]
        for r in range(SUBS):
            block = ext_ref[r : taps + rows - SUBS + r, lanes] if r else ext_ref[:, lanes]
            for q in range(taps // SUBS + 1):
                start = SUBS * q
                i = taps - start - r
                if i < 0:
                    continue
                product = grad_shifted * block[start : start + rows, :]
                sums_ref[SUBS * i : SUBS * (i + 1), :] = folded(product)
        tap_ref[0 : taps + 1, lanes] = part_total(sums_ref, taps + 1)
    gain = gain_ref[...] + behind_ref[...] * decay_ref[...] * end_ref[...]
    reach = reach_ref[...] + rows * whole_ref[...] * start_ref[...]
    power = power_ref[...] + behind_ref[...] * reach

    def slots_total(array):
        total = slot_of(array, 0, chans)
        for s in range(1, slots):
            total = total + slot_of(array, s, chans)
        return total

    gain, power = slots_total(gain), slots_total(power)
    grad_in = out_ref[...] * gain
    grad_rate = grad_in * slope_ref[...] - fall_ref[...] * power
    tap_sums = slots_total(tap_ref[0 : taps + 1, :])
    small_ref[...] = jnp.concatenate(
        [
            tap_sums[1 : taps + 1, :],
            grad_rate * row(step_ref),
            grad_in * root_ref[...],
            in_ref[...] * gain,
        ],
        axis=-1,
    )
    misc_ref[...] = jnp.zeros_like(misc_ref)
    skip_sums = slots_total(jnp.sum(gs_ref[...] * u_ref[...], axis=0, keepdims=True))
    step_sums = jnp.sum(grad_rate * a_ref[...], axis=0, keepdims=True)
    misc_ref[0:1, :] = jnp.concatenate(
        [tap_sums[0:1, :], skip_sums, step_sums, jnp.zeros_like(skip_sums)], axis=-1
    )


def weights_kernel(gq_ref, act_ref, gated_ref, low_ref, out_ref):
    rows, width = gq_ref.shape
    chans = gated_ref.shape[1]
    query = 0.0
    for s in range(width // chans):
        grads = slot_of(gq_ref[...].astype(f32), s, chans).astype(bf16)
        query = query + contract(grads, act_ref[s * rows : (s + 1) * rows, :], 0, 0)
    out_ref[0:chans, :] = query.astype(bf16)
    out_ref[chans : 2 * chans, :] = contract(gated_ref[...], low_ref[...], 0, 0).astype(bf16)


def last_kernel(
    mask_one, mask_two, spot_ref, out_keep_ref, out_send_ref, gq_ref, gk_ref, received_ref, gv_ref, act_ref, w_ref, early_ref, small_ref, misc_ref,
    rows_ref, up_ref, down_ref, keep_ref, send_ref, one_ref, one_send_ref, two_ref,
    two_send_ref, all_ref,
):
    rows, width = gk_ref.shape
    taps = received_ref.shape[0]
    chans = w_ref.shape[1]
    slots = width // chans
    grad_k = jnp.concatenate(
        [
            gk_ref[0 : rows - taps, :],
            gk_ref[rows - taps : rows, :] + received_ref[...].astype(f32),
        ],
        axis=0,
    ).astype(bf16)
    parts = [gq_ref[...].astype(f32), grad_k.astype(f32), gv_ref[...].astype(f32)]
    sums = [0.0, 0.0, 0.0]
    terms, biases = [], []
    for s in range(slots):
        act = act_ref[s * rows : (s + 1) * rows, :]
        term = 0.0
        for j in range(3):
            grads = slot_of(parts[j], s, chans).astype(bf16)
            term = term + contract(grads, w_ref[j], 1, 0)
            if j:
                sums[j] = sums[j] + contract(grads, act, 0, 0)
        terms.append(term)
    half = slots // 2
    count = out_keep_ref.shape[0]
    put_halves(
        spot_ref[1],
        jnp.concatenate(terms[:half], axis=0),
        jnp.concatenate(terms[half:], axis=0),
        keep_ref.at[0:count, :],
        send_ref.at[0:count, :],
    )
    keep_ref[count:, :] = out_keep_ref[...]
    send_ref[count:, :] = out_send_ref[...]
    for j in range(3):
        total = jnp.sum(parts[j], axis=0, keepdims=True)
        bias = slot_of(total, 0, chans)
        for s in range(1, slots):
            bias = bias + slot_of(total, s, chans)
        biases.append(bias)
    place = 0

    def put(block):
        nonlocal place
        all_ref[place : place + block.shape[0], :] = block.astype(f32)
        place += block.shape[0]

    put(early_ref[...])
    put(sums[1])
    put(sums[2])
    put(small_ref[...])
    put(
        jnp.concatenate(
            [
                misc_ref[0:1, :],
                jnp.concatenate(biases + [jnp.zeros_like(biases[0])], axis=-1),
                rows_ref[0:3, :],
                up_ref[...],
                down_ref[...],
                jnp.zeros((2 * SUBS - 7, misc_ref.shape[1]), f32),
            ],
            axis=0,
        )
    )
    put(jnp.zeros((all_ref.shape[0] - place, misc_ref.shape[1]), f32))
    count = all_ref.shape[0] // 4
    quarters = [all_ref[k * count : (k + 1) * count, :] for k in range(4)]
    put_halves(bit_of(spot_ref, mask_one), quarters[0], quarters[1], one_ref, one_send_ref)
    put_halves(bit_of(spot_ref, mask_two), quarters[2], quarters[3], two_ref, two_send_ref)


def widen_kernel(mask_one, mask_two, spot_ref, up_ref, up_got_ref, down_ref, down_got_ref, one_ref, two_ref):
    for mask, own_ref, got_ref, out_ref in (
        (mask_one, up_ref, up_got_ref, one_ref),
        (mask_two, down_ref, down_got_ref, two_ref),
    ):
        half = own_ref.shape[0]
        first, second = halves_of(bit_of(spot_ref, mask), own_ref, got_ref)
        out_ref[0:half, :] = first
        out_ref[half:, :] = second


def spread_kernel(
    chans, taps, mask_one, mask_two, spot_ref, ln1_ref, ln1_got_ref, one_ref, one_got_ref, two_ref, two_got_ref,
    qkv_ref, bias_ref, tap_ref, shift_skip_ref, a_ref, b_ref, c_ref, ssm_skip_ref, step_ref, out_ref,
    gain_ref, norm_bias_ref, out_bias_ref, up_ref, down_ref, entry_gain_ref, entry_bias_ref, all_ref,
):
    entry = ln1_ref[...] + ln1_got_ref[...]
    entry_gain_ref[...] = entry[0:1, :].reshape(entry.shape[1])
    entry_bias_ref[...] = entry[1:2, :].reshape(entry.shape[1])
    quarter = one_ref.shape[0]
    pieces = halves_of(bit_of(spot_ref, mask_one), one_ref, one_got_ref)
    pieces += halves_of(bit_of(spot_ref, mask_two), two_ref, two_got_ref)
    for place, piece in enumerate(pieces):
        all_ref[place * quarter : (place + 1) * quarter, :] = piece
    for j, place in enumerate((0, 2, 3)):
        qkv_ref[j] = all_ref[place * chans : (place + 1) * chans, :]
    out_ref[...] = all_ref[chans : 2 * chans, :]
    base = 4 * chans
    small = all_ref[base : base + taps, :]
    for slot, ref in enumerate((tap_ref, a_ref, b_ref, c_ref)):
        ref[...] = slot_of(small, slot, chans)
    base = base + taps
    misc = all_ref[base : base + SUBS, :]
    for slot, ref in enumerate((shift_skip_ref, ssm_skip_ref, step_ref)):
        ref[...] = slot_of(misc[0:1, :], slot, chans).reshape(chans)
    bias_ref[...] = jnp.concatenate([slot_of(misc[1:2, :], j, chans) for j in range(3)], axis=0)
    for place, ref in enumerate((gain_ref, norm_bias_ref, out_bias_ref, up_ref, down_ref)):
        ref[...] = misc[2 + place : 3 + place, :].reshape(misc.shape[1])


def ordered_calls():
    held = [jnp.zeros((SUBS, LANES), f32)]

    def call(kernel, outs, args, scratch=(), us=0.5, limit=24, scalars=0, place=pltpu.VMEM):
        inputs = len(args)

        def body(*refs):
            given, rest = refs[:inputs], refs[inputs + 1 :]
            rest[len(outs)][...] = refs[inputs][...]
            kernel(*given, *rest[: len(outs)], *rest[len(outs) + 1 :])

        size = sum(a.size * a.dtype.itemsize for a in list(args) + list(outs))
        specs = [pl.BlockSpec(memory_space=pltpu.SMEM)] * scalars
        specs += [pl.BlockSpec(memory_space=place)] * (inputs - scalars)
        specs += [pl.BlockSpec(memory_space=pltpu.VMEM)]
        results = pl.pallas_call(
            body,
            in_specs=specs,
            out_shape=tuple(outs) + (like((SUBS, LANES)),),
            scratch_shapes=list(scratch),
            compiler_params=pltpu.CompilerParams(vmem_limit_bytes=limit << 20),
            cost_estimate=pl.CostEstimate(
                flops=int(us * FLOPS_PER_US), bytes_accessed=0, transcendentals=0
            ),
        )(*args, held[0])
        held[0] = results[-1]
        return results[:-1]

    return call


def like(shape, dtype=f32):
    return jax.ShapeDtypeStruct(shape, dtype)


def shards(
    inputs,
    cotangent,
    lengths,
    ln1_gain,
    ln1_bias,
    query_key_value_weight,
    b_qkv,
    shift_taps,
    shift_skip,
    ssm_a,
    ssm_b,
    ssm_c,
    ssm_skip,
    ssm_step,
    output_weight,
    b_out,
    ln2_gain,
    ln2_bias,
    up_weight,
    up_bias,
    down_weight,
    b_down,
):
    slots, rows, model = inputs.shape
    taps, chans = shift_taps.shape
    states = ssm_a.shape[1]
    width = slots * chans
    tokens = slots * rows
    spot = jnp.stack([lax.axis_index("seq"), lax.axis_index("head") % 2]).astype(jnp.int32)
    peers = lax.axis_size("seq")
    last_mask = peers // 2
    half_tokens = tokens // 2
    half_like = like((half_tokens, model), bf16)
    projections = jnp.swapaxes(query_key_value_weight, 1, 2)
    flat_inputs = inputs.reshape(tokens, model)
    hidden_count = up_bias.shape[0]
    masks = [2**k for k in range(peers.bit_length() - 1)]
    orders = (masks, masks[1::-1] + masks[2:])
    ends = tuple(order[0] for order in orders)
    call = ordered_calls()

    rate = (ssm_step[:, None] * ssm_a).T
    decay = jnp.exp(-rate)
    gain_root = jnp.sqrt(-jnp.expm1(-2.0 * rate))
    turned_b, turned_c = ssm_b.T, ssm_c.T
    in_weight = gain_root * turned_b
    decay_wide = wide(decay, slots)
    whole_wide = wide(jnp.exp(-rate * rows), slots)
    weight_wide = wide(turned_c * in_weight, slots)
    slope = turned_b * jnp.exp(-2.0 * rate) / gain_root
    fall = decay * turned_c * in_weight

    act_one, queries, keys, values = call(
        project_kernel,
        [like((tokens, model), bf16), like((rows, width)), like((rows, width), bf16), like((rows, width))],
        [spot] + [
            pltpu.with_memory_space_constraint(a, pltpu.HBM)
            for a in (inputs, ln1_gain, ln1_bias, projections, b_qkv)
        ],
        [
            pltpu.VMEM(inputs.shape, inputs.dtype),
            pltpu.VMEM(ln1_gain.shape, f32),
            pltpu.VMEM(ln1_bias.shape, f32),
            pltpu.VMEM(projections.shape, projections.dtype),
            pltpu.VMEM(b_qkv.shape, f32),
            pltpu.SemaphoreType.DMA((5,)),
        ],
        us=2.0,
        scalars=1,
        place=pltpu.HBM,
        limit=24,
    )
    edge = shifted(keys[rows - taps :, :], "seq", 1)
    shifted_keys, series, end_local, end_low = call(
        mix_kernel,
        [like((rows, width)), like((rows, width)), like((states, width)), like((states, width), bf16)],
        [edge, keys, values, shift_taps, shift_skip, decay_wide],
        [pltpu.VMEM((taps + rows, width), f32), pltpu.VMEM((taps + SUBS, width), f32)],
        us=2.9,
    )
    low_out, grad_b_down = call(
        masked_kernel,
        [like((tokens, model), bf16), like((1, model))],
        [spot, lengths, cotangent],
        us=0.8,
        scalars=2,
    )
    carry, got = plain_carry(end_local, end_low, whole_wide, spot[:1].reshape(1, 1), "seq")
    ssm_out, gated, start_state, keep, send = call(
        functools.partial(attend_kernel, last_mask),
        [like((rows, width)), like((tokens, chans), bf16), like((states, width)), half_like, half_like],
        [
            spot, series, decay_wide, weight_wide, whole_wide, got, carry, ssm_skip, queries,
            output_weight,
        ],
        [pltpu.VMEM((rows * SUBS, LANES), f32)],
        us=2.9,
        scalars=1,
    )
    own, other = plain_head_total(keep, send)
    middle, back_keep, back_send, out_keep, out_send, grad_b_up, up_keep, up_send, down_keep, down_send = call(
        functools.partial(feed_kernel, *ends),
        [
            like((tokens, model)),
            half_like,
            half_like,
            half_like,
            half_like,
            like((1, hidden_count)),
            like((model // 2, hidden_count), bf16),
            like((model // 2, hidden_count), bf16),
            like((hidden_count // 2, model), bf16),
            like((hidden_count // 2, model), bf16),
        ],
        [
            spot, own, other, flat_inputs, b_out, ln2_gain, ln2_bias, up_weight, up_bias, down_weight,
            low_out,
        ],
        [
            pltpu.VMEM((tokens, model), bf16),
            pltpu.VMEM((tokens, hidden_count), bf16),
            pltpu.VMEM((tokens, hidden_count), bf16),
        ],
        us=5.0,
        scalars=1,
        limit=32,
    )
    low_middle = early = last_parts = entry_parts = grad_inputs = layer_out = None
    sum_up = sum_down = last_rows = grad_queries = None

    def feed_work():
        nonlocal sum_up, sum_down
        feed_joined = yield from halving_steps(
            call, [(up_keep, up_send), (down_keep, down_send)], orders, spot, "seq"
        )
        sum_up, sum_down = call(
            functools.partial(widen_kernel, *ends),
            [like((model, hidden_count)), like((hidden_count, model))],
            [spot, *feed_joined],
            scalars=1,
            us=2.5,
        )

    def early_work():
        nonlocal early
        while low_middle is None:
            yield
        (early,) = call(
            weights_kernel,
            [like((2 * chans, model), bf16)],
            [grad_queries, act_one, gated, low_middle],
            us=0.5,
        )

    def last_work():
        while last_parts is None:
            yield
        one, one_send, two, two_send = last_parts
        return (
            yield from halving_steps(call, [(one, one_send), (two, two_send)], orders, spot, "seq")
        )

    def entry_work():
        while entry_parts is None:
            yield
        return (yield from sum_steps(call, entry_parts, masks[:1] + masks[:0:-1], "seq"))

    def main_work():
        nonlocal low_middle, grad_queries, last_parts, entry_parts, grad_inputs, layer_out, last_rows
        joins = head_steps(call, back_keep, back_send)
        next(joins)
        yield
        next(joins)
        (reach,) = call(
            reach_kernel, [like((states, width))], [series, decay_wide], us=2.0
        )
        yield
        own, other = ran(joins)
        grad_middle, low_middle, grad_queries, grad_ssm, front_local, front_low, norm_rows = call(
            middle_kernel,
            [
                like((tokens, model)),
                like((tokens, model), bf16),
                like((rows, width), bf16),
                like((rows, width)),
                like((states, width)),
                like((states, width), bf16),
                like((SUBS, model)),
            ],
            [
                spot, lengths, own, other, middle, cotangent, ln2_gain, output_weight, ssm_out, queries,
                decay_wide,
            ],
            us=3.00,
            scalars=2,
        )
        yield
        steps = carry_steps(call, front_local, front_low, whole_wide, spot, "seq", True)
        carry, got = yield from steps
        grad_local, gain_local, power_local = call(
            local_kernel,
            [like((rows, width)), like((states, width)), like((states, width))],
            [series, grad_ssm, decay_wide, weight_wide, start_state],
            [pltpu.VMEM((rows * SUBS, LANES), f32)],
            us=4.8,
        )
        yield
        grad_keys, halo, grad_values, small, misc = call(
            functools.partial(unmix_kernel, last_mask),
            [
                like((rows, width)),
                like((taps, width), bf16),
                like((rows, width), bf16),
                like((states, 4 * chans)),
                like((SUBS, 4 * chans)),
            ],
            [
                spot, grad_local, grad_ssm, series, decay_wide, weight_wide, whole_wide, got, carry,
                gain_local, power_local, reach, start_state, end_local, values, shifted_keys, edge, keys, shift_taps,
                shift_skip, ssm_skip, in_weight, turned_c, gain_root, slope, fall, ssm_a.T, ssm_step,
            ],
            [
                pltpu.VMEM((width * rows * SUBS // LANES, LANES), f32),
                pltpu.VMEM((taps + rows, width), f32),
                pltpu.VMEM((2 * taps + rows, width), f32),
                pltpu.VMEM((taps + SUBS, width), f32),
                pltpu.VMEM(((taps + 1) * SUBS, LANES), f32),
                pltpu.VMEM((taps + SUBS, width), f32),
                pltpu.VMEM((states, width), f32),
            ],
            us=6.0,
            scalars=1,
        )
        received = shifted(halo, "seq", -1)
        yield
        while early is None:
            step("E")
        unit = 2 * peers * SUBS
        last_rows = -(-(4 * chans + states + 2 * SUBS) // unit) * unit
        quarter = like((last_rows // 4, model), bf16)
        keep, send, one, one_send, two, two_send = call(
            functools.partial(last_kernel, *ends),
            [like((tokens, model), bf16)] * 2 + [quarter, quarter, quarter, quarter],
            [
                spot, out_keep, out_send, grad_queries, grad_keys, received, grad_values, act_one, projections, early, small,
                misc, norm_rows, grad_b_up, grad_b_down,
            ],
            [pltpu.VMEM((last_rows, model), f32)],
            us=0.45,
            scalars=1,
        )
        last_parts = (one, one_send, two, two_send)
        step("L")
        own, other = yield from head_steps(call, keep, send)
        yield
        grad_inputs, rows_sum, layer_out = call(
            entry_kernel,
            [like((tokens, model)), like((SUBS, model)), like(inputs.shape)],
            [spot, lengths, own, other, flat_inputs, ln1_gain, grad_middle, middle, b_down],
            scalars=2,
            us=0.90,
        )
        entry_parts = rows_sum
        step("N")

    works = {"m": main_work(), "M": feed_work(), "E": early_work(), "L": last_work(), "N": entry_work()}
    ended = {}

    def step(name):
        if name not in ended:
            try:
                next(works[name])
            except StopIteration as end:
                ended[name] = end.value

    step("M")
    for name in ORDER:
        step(name)
    for name in "mMLN":
        while name not in ended:
            step(name)
    joined, ln1_parts = ended["L"], ended["N"]
    spread = call(
        functools.partial(spread_kernel, chans, taps, *ends),
        [
            like((3, chans, model)),
            like((3, chans)),
            like((taps, chans)),
            like((chans,)),
            like((states, chans)),
            like((states, chans)),
            like((states, chans)),
            like((chans,)),
            like((chans,)),
            like((chans, model)),
            like((model,)),
            like((model,)),
            like((model,)),
            like(up_bias.shape),
            like((model,)),
            like((model,)),
            like((model,)),
        ],
        [spot, *ln1_parts, *joined],
        [pltpu.VMEM((last_rows, model), f32)],
        scalars=1,
        us=2.0,
    )
    (
        sum_qkv, sum_b_qkv, sum_taps, sum_shift_skip, sum_a, sum_b, sum_c, sum_ssm_skip, sum_step,
        sum_out, sum_ln2_gain, sum_ln2_bias, sum_b_out, sum_b_up, sum_b_down,
        sum_ln1_gain, sum_ln1_bias,
    ) = spread
    return (
        layer_out,
        grad_inputs.reshape(inputs.shape),
        sum_ln1_gain,
        sum_ln1_bias,
        jnp.swapaxes(sum_qkv, 1, 2),
        sum_b_qkv,
        sum_taps,
        sum_shift_skip,
        sum_a.T,
        sum_b.T,
        sum_c.T,
        sum_ssm_skip,
        sum_step,
        sum_out,
        sum_b_out,
        sum_ln2_gain,
        sum_ln2_bias,
        sum_up,
        sum_b_up,
        sum_down,
        sum_b_down,
    )


def solution(mesh):
    in_specs = (
        P(None, "seq", None),
        P(None, "seq", None),
        P(),
        P(),
        P(),
        P(None, None, "head"),
        P(None, "head"),
        P(None, "head"),
        P("head"),
        P("head", None),
        P("head", None),
        P("head", None),
        P("head"),
        P("head"),
        P("head", None),
        P(),
        P(),
        P(),
        P(None, "head"),
        P("head"),
        P("head", None),
        P(),
    )
    out_specs = (
        P(None, "seq", None),
        P(None, "seq", None),
        P(),
        P(),
        P(None, None, "head"),
        P(None, "head"),
        P(None, "head"),
        P("head"),
        P("head", None),
        P("head", None),
        P("head", None),
        P("head"),
        P("head"),
        P("head", None),
        P(),
        P(),
        P(),
        P(None, "head"),
        P("head"),
        P("head", None),
        P(),
    )
    return jax.shard_map(shards, mesh=mesh, in_specs=in_specs, out_specs=out_specs, check_vma=False)
```

```python
import functools

import jax
import jax.numpy as jnp
from jax import lax
from jax.experimental import pallas as pl
from jax.experimental.pallas import tpu as pltpu
from jax.sharding import PartitionSpec as P

norm_epsilon = 1e-05
f32 = jnp.float32
bf16 = jnp.bfloat16
LANES = 128
ORDER = "mmmmEmMmMmMmmMmLmLLMLLM"
FLOPS_PER_US = 0.5e9
SUBS = 8


def shifted(shard, axis, by):
    peers = lax.axis_size(axis)
    return lax.ppermute(shard, axis, [(i, i + by) for i in range(peers) if 0 <= i + by < peers])


def swapped(shard, axis, mask):
    return lax.ppermute(shard, axis, [(i, i ^ mask) for i in range(lax.axis_size(axis))])


def halving_steps(call, groups, orders, spot, axis, extra=None):
    keeps, sends = [g[0] for g in groups], [g[1] for g in groups]
    count, groups_count, model = len(orders[0]), len(groups), keeps[0].shape[1]
    joint = [k > 0 and len({order[k] for order in orders}) == 1 for k in range(count)]
    rows = [k.shape[0] for k in keeps]
    tail = 0

    def shapes(rows, stage):
        sizes = [sum(rows) + tail] if joint[stage] else [rows[0] + tail] + rows[1:]
        return [like((size, model), bf16) for size in sizes]

    def trade(blocks, stage):
        return [swapped(block, axis, order[stage]) for block, order in zip(blocks, orders)]

    def masks_at(stage):
        return tuple(order[stage] for order in orders)

    for stage in range(count):
        gots = trade(sends, stage)
        yield
        if stage + 1 < count:
            half = [r // 2 for r in rows]
            held = []
            if extra and stage + 2 == count:
                held, tail = [extra()], SUBS
            results = call(
                functools.partial(halve_kernel, masks_at(stage + 1), len(gots), len(held)),
                [like((r, model), bf16) for r in half] + shapes(half, stage + 1),
                [spot, *keeps, *gots, *held], limit=8, scalars=1,
            )
            keeps, sends, rows = results[:groups_count], results[groups_count:], half
        else:
            kept = tail
            tail = 0
            owns = call(
                functools.partial(sum_kernel, groups_count, len(gots), kept),
                shapes(rows, stage) + [like((SUBS, model))] * len(held),
                [*keeps, *gots, *held], limit=8,
            )
            owns, held = (owns[:-1], [owns[-1]]) if held else (owns, [])
    for stage in range(count - 1, -1, -1):
        gots = trade(owns, stage)
        yield
        if not stage:
            return [a for pair in zip(owns, gots) for a in pair]
        before = tail
        tail = SUBS if held or tail else 0
        double = [2 * r for r in rows]
        owns = call(
            functools.partial(double_kernel, masks_at(stage), tuple(rows), len(gots), before, len(held)),
            shapes(double, stage - 1), [spot, *owns, *gots, *held], limit=8, scalars=1,
        )
        rows, held = double, []


def head_steps(call, keep, send, axis="head"):
    got = swapped(send, axis, 1)
    mask = 2
    while True:
        yield
        if mask >= lax.axis_size(axis):
            (low,) = call(
                functools.partial(sum_kernel, 1, 1, 0), [like(keep.shape, bf16)], [keep, got], limit=8
            )
            return low, swapped(low, axis, 1)
        keep, low = call(
            join_kernel, [like(keep.shape), like(keep.shape, bf16)], [keep, got], limit=8
        )
        got = swapped(low, axis, mask)
        mask *= 2


def carry_steps(call, total, low, whole, spot, axis, ahead):
    carry = jnp.zeros_like(total)
    mask = 1
    while True:
        got = swapped(low, axis, mask)
        if 2 * mask >= lax.axis_size(axis):
            return carry, got
        yield
        more = 4 * mask < lax.axis_size(axis)
        low, carry, *kept = call(
            functools.partial(merge_kernel, mask, ahead),
            [like(total.shape, bf16), like(total.shape)] + [like(total.shape)] * more,
            [spot, whole, total, got, carry],
            limit=8,
            scalars=1,
        )
        total = kept[0] if kept else total
        mask *= 2


def plain_head_total(keep, send, axis="head"):
    total = keep.astype(f32) + swapped(send, axis, 1).astype(f32)
    mask = 2
    while mask < lax.axis_size(axis):
        total = total + swapped(total.astype(bf16), axis, mask).astype(f32)
        mask *= 2
    low = total.astype(bf16)
    return low, swapped(low, axis, 1)


def plain_carry(total, low, whole, place, axis):
    carry = jnp.zeros_like(total)
    mask, step = 1, whole
    while True:
        got = swapped(low, axis, mask)
        if 2 * mask >= lax.axis_size(axis):
            return carry, got
        far = (place & mask) > 0
        power, bit, base = jnp.ones_like(whole), 1, whole
        while bit < mask:
            power = jnp.where((place & bit) > 0, power * base, power)
            base = base * base
            bit *= 2
        got = got.astype(f32)
        carry = carry + jnp.where(far, power, 0.0) * got
        total = jnp.where(far, step, 1.0) * got + jnp.where(far, 1.0, step) * total
        low = total.astype(bf16)
        step = step * step
        mask *= 2


def ran(steps):
    while True:
        try:
            next(steps)
        except StopIteration as end:
            return end.value


def lane_tiles(width):
    return [slice(i, i + LANES) for i in range(0, width, LANES)]


def folded(product):
    states, lanes = product.shape
    return jnp.sum(product.reshape(states // SUBS, SUBS, lanes), axis=0)


def rows_at(start, size):
    return pl.ds(pl.multiple_of(start, SUBS), size)


def centred_rows(rows):
    centred = rows - jnp.mean(rows, axis=-1, keepdims=True)
    spread = jnp.mean(centred * centred, axis=-1, keepdims=True)
    return centred, lax.rsqrt(spread + norm_epsilon)


def row(vector_ref):
    return vector_ref[...].reshape(1, vector_ref.shape[0])


def wide(array, slots):
    return jnp.concatenate([array] * slots, axis=-1)


def slot_of(array, slot, width):
    return array[:, slot * width : (slot + 1) * width]


def contract(left, right, left_dim, right_dim):
    return lax.dot_general(
        left, right, (((left_dim,), (right_dim,)), ((), ())), preferred_element_type=f32
    )


def run_scan(series_ref, decay_ref, out_ref, reverse):
    blocks = series_ref.shape[0] // SUBS
    tiles = lane_tiles(series_ref.shape[1])
    decays = [decay_ref[:, lanes] for lanes in tiles]

    def one(lap, states):
        place = blocks - 1 - lap if reverse else lap
        at = rows_at(place * SUBS, SUBS)
        blocks_in = [series_ref[at, lanes] for lanes in tiles]
        for r in range(SUBS):
            r = SUBS - 1 - r if reverse else r
            states = [d * s + b[r : r + 1, :] for d, s, b in zip(decays, states, blocks_in)]
        return states

    states = lax.fori_loop(0, blocks, one, [jnp.zeros_like(d) for d in decays])
    for lanes, state in zip(tiles, states):
        out_ref[:, lanes] = state


def part_total(part_ref, rows, base=0):
    total = part_ref[pl.ds(base, rows, stride=SUBS), :]
    for r in range(1, SUBS):
        total = total + part_ref[pl.ds(base + r, rows, stride=SUBS), :]
    return total


def power_of(whole, exponent, mask):
    power, bit = jnp.ones_like(whole), 1
    while bit < mask:
        power = jnp.where((exponent // bit) % 2 == 1, power * whole, power)
        whole = whole * whole
        bit *= 2
    return power, whole


def merged(mask, ahead, place, whole, got, carry):
    inner = place % mask
    far = (place // mask) % 2
    if ahead:
        inner, far = mask - 1 - inner, 1 - far
    power, step = power_of(whole, inner, mask)
    return jnp.where(far == 1, carry + power * got, carry), far, step


def merge_kernel(mask, ahead, spot_ref, whole_ref, total_ref, got_ref, carry_ref, low_ref, out_ref, *sums):
    got = got_ref[...].astype(f32)
    total = total_ref[...]
    out_ref[...], far, step = merged(
        mask, ahead, spot_ref[0], whole_ref[...], got, carry_ref[...]
    )
    total = jnp.where(far == 1, step * got + total, step * total + got)
    for sum_ref in sums:
        sum_ref[...] = total
    low_ref[...] = total.astype(bf16)


def bit_of(spot, mask):
    return (spot[0] // mask) % 2


def split_blocks(refs, rows, tail=0):
    if len(refs) == 1:
        sizes, whole = list(rows) + [tail], refs[0][...].astype(f32)
        blocks = [whole[sum(sizes[:k]) : sum(sizes[: k + 1])] for k in range(len(rows))]
        return blocks, whole[sum(rows) :] if tail else None
    blocks = [ref[0:r, :].astype(f32) for ref, r in zip(refs, rows)]
    return blocks, refs[0][rows[0] :, :].astype(f32) if tail else None


def put_blocks(refs, blocks, riding=None):
    blocks = list(blocks)
    rider = [] if riding is None else [riding]
    parts = [blocks + rider] if len(refs) == 1 else [blocks[:1] + rider] + [[b] for b in blocks[1:]]
    for ref, pieces in zip(refs, parts):
        start = 0
        for piece in pieces:
            ref[start : start + piece.shape[0], :] = piece.astype(bf16)
            start += piece.shape[0]


def halve_kernel(masks, got_count, held, spot_ref, *refs):
    count = len(masks)
    keeps = [ref[...].astype(f32) for ref in refs[:count]]
    rows = [keep.shape[0] for keep in keeps]
    ins = count + got_count
    totals = [a + b for a, b in zip(keeps, split_blocks(refs[count:ins], rows)[0])]
    pairs = [
        ordered(bit_of(spot_ref, mask), total[: r // 2], total[r // 2 :])
        for mask, total, r in zip(masks, totals, rows)
    ]
    outs = refs[ins + held :]
    for ref, pair in zip(outs[:count], pairs):
        ref[...] = pair[0].astype(bf16)
    put_blocks(outs[count:], [pair[1] for pair in pairs], refs[ins][...] if held else None)


def sum_kernel(count, got_count, tail, *refs):
    keeps = [ref[...].astype(f32) for ref in refs[:count]]
    rows = [keep.shape[0] for keep in keeps]
    ins = count + got_count
    gots, riding = split_blocks(refs[count:ins], rows, tail)
    outs = refs[ins + (1 if tail else 0) :]
    if tail:
        outs[-1][...] = refs[ins][...].astype(bf16).astype(f32) + riding
        outs = outs[:-1]
    put_blocks(outs, [a + b for a, b in zip(keeps, gots)])


def double_kernel(masks, rows, ins, tail, held, spot_ref, *refs):
    owns, mine = split_blocks(refs[:ins], rows, tail)
    gots, theirs = split_blocks(refs[ins : 2 * ins], rows, tail)
    riding = mine + theirs if tail else refs[2 * ins][...] if held else None
    blocks = [
        jnp.concatenate(ordered(bit_of(spot_ref, mask), own, got), axis=0)
        for mask, own, got in zip(masks, owns, gots)
    ]
    put_blocks(refs[2 * ins + held :], blocks, riding)


def join_kernel(keep_ref, got_ref, total_ref, low_ref):
    total = keep_ref[...].astype(f32) + got_ref[...].astype(f32)
    total_ref[...] = total
    low_ref[...] = total.astype(bf16)


def ordered(bit, own, other):
    return jnp.where(bit == 0, own, other), jnp.where(bit == 0, other, own)


def halves_of(bit, own_ref, other_ref):
    return ordered(bit, own_ref[...].astype(f32), other_ref[...].astype(f32))


def put_halves(bit, first, second, keep_ref, send_ref):
    keep, send = ordered(bit, first, second)
    keep_ref[...] = keep.astype(bf16)
    send_ref[...] = send.astype(bf16)


def project_kernel(
    spot_ref, x_hbm, gain_hbm, bias_hbm, w_hbm, wb_hbm, act_ref, q_ref, k_ref, v_ref,
    x_ref, gain_ref, bias_ref, w_ref, wb_ref, sems,
):
    pairs = ((x_hbm, x_ref), (gain_hbm, gain_ref), (bias_hbm, bias_ref), (w_hbm, w_ref), (wb_hbm, wb_ref))
    copies = [pltpu.make_async_copy(a, b, sems.at[i]) for i, (a, b) in enumerate(pairs)]
    for copy in copies:
        copy.start()
    for copy in copies[:3]:
        copy.wait()
    slots, rows, _ = x_ref.shape
    gain, bias = row(gain_ref), row(bias_ref)
    acts = []
    for s in range(slots):
        centred, root = centred_rows(x_ref[s].astype(f32))
        acts.append((centred * root * gain + bias).astype(bf16))
        act_ref[s * rows : (s + 1) * rows, :] = acts[s]
    for copy in copies[3:]:
        copy.wait()
    kept = [
        jnp.concatenate([contract(a, w_ref[j], 1, 1) + wb_ref[j : j + 1, :] for a in acts], axis=-1)
        for j in range(3)
    ]
    q_ref[...] = kept[0]
    k_ref[...] = kept[1].astype(bf16)
    v_ref[...] = kept[2]


def masked_kernel(spot_ref, lengths_ref, cotangent_ref, low_ref, sum_ref):
    slots, rows, model = cotangent_ref.shape
    spot = spot_ref[0] * rows + lax.broadcasted_iota(jnp.int32, (rows, model), 0)
    total = 0.0
    for s in range(slots):
        grads = jnp.where(spot < lengths_ref[s], cotangent_ref[s], 0.0)
        low_ref[s * rows : (s + 1) * rows, :] = grads.astype(bf16)
        total = total + jnp.sum(grads, axis=0, keepdims=True)
    sum_ref[...] = total


def mix_kernel(
    edge_ref, k_ref, v_ref, taps_ref, skip_ref, decay_ref,
    shifted_ref, u_ref, end_ref, low_ref, ext_ref, wide_ref,
):
    taps, width = edge_ref.shape
    rows = k_ref.shape[0]
    slots = width // taps_ref.shape[1]
    ext_ref[0:taps, :] = edge_ref[...].astype(f32)
    ext_ref[taps : taps + rows, :] = k_ref[...].astype(f32)
    wide_ref[0:taps, :] = wide(taps_ref[...], slots)
    wide_ref[taps : taps + 1, :] = wide(row(skip_ref), slots)
    for lanes in lane_tiles(width):
        total = wide_ref[taps : taps + 1, lanes] * ext_ref[taps : taps + rows, lanes]
        for r in range(SUBS):
            if r:
                block = ext_ref[SUBS - r : taps + rows - r, lanes]
            else:
                block = ext_ref[0 : taps + rows - SUBS, lanes]
            for q in range(taps // SUBS):
                i = SUBS * q + (r if r else SUBS)
                start = taps - SUBS - SUBS * q
                total = total + wide_ref[i - 1 : i, lanes] * block[start : start + rows, :]
        shifted_ref[:, lanes] = total
        u_ref[:, lanes] = total * v_ref[:, lanes]
    run_scan(u_ref, decay_ref, end_ref, False)
    low_ref[...] = end_ref[...].astype(bf16)


def attend_kernel(
    mask, spot_ref, u_ref, decay_ref, weight_ref, whole_ref, got_ref, carry_ref, skip_ref,
    q_ref, w_ref, ssm_ref, gated_ref, start_ref, keep_ref, send_ref, part_ref,
):
    rows, width = u_ref.shape
    chans = w_ref.shape[0]
    slots = width // chans
    blocks = rows // SUBS
    skip = wide(row(skip_ref), slots)
    start_ref[...], _, _ = merged(
        mask, False, spot_ref[0], whole_ref[...], got_ref[...].astype(f32), carry_ref[...]
    )
    for lanes in lane_tiles(width):
        decay = decay_ref[:, lanes]
        weight = weight_ref[:, lanes]

        def one(lap, state, lanes=lanes, decay=decay, weight=weight):
            tile = u_ref[rows_at(lap * SUBS, SUBS), lanes]
            for r in range(SUBS):
                state = decay * state + tile[r : r + 1, :]
                part_ref[rows_at(lap * SUBS * SUBS + r * SUBS, SUBS), :] = folded(weight * state)
            return state

        lax.fori_loop(0, blocks, one, start_ref[:, lanes])
        ssm_ref[:, lanes] = part_total(part_ref, rows) + skip[:, lanes] * u_ref[:, lanes]
    mixture = q_ref[...] * ssm_ref[...]
    terms = []
    for s in range(slots):
        gated = slot_of(mixture, s, chans).astype(bf16)
        gated_ref[s * rows : (s + 1) * rows, :] = gated
        terms.append(contract(gated, w_ref[...], 1, 0))
    half = slots // 2
    put_halves(
        spot_ref[1],
        jnp.concatenate(terms[:half], axis=0),
        jnp.concatenate(terms[half:], axis=0),
        keep_ref,
        send_ref,
    )


def gelu_parts(x):
    root = 0.7978845608028654
    square = x * x
    bend = jnp.tanh(root * (x + 0.044715 * (square * x)))
    value = 0.5 * x * (1.0 + bend)
    slope = 0.5 * (1.0 + bend) + 0.5 * x * (1.0 - bend * bend) * root * (1.0 + 0.134145 * square)
    return value, slope


def feed_kernel(
    mask_one, mask_two, spot_ref, own_ref, other_ref, x_ref, b_out_ref, gain_ref, bias_ref, up_ref, up_bias_ref, down_ref,
    gout_ref, mid_ref, keep_ref, send_ref, out_keep_ref, out_send_ref,
    bias_sum_ref, w_up_ref, w_up_send_ref, w_down_ref, w_down_send_ref, act_ref, hidden_ref, grad_ref,
):
    bias_sum = 0.0
    backs, outs = [], []
    rows = own_ref.shape[0]
    for half, attended in enumerate(halves_of(spot_ref[1], own_ref, other_ref)):
        at = slice(half * rows, (half + 1) * rows)
        middle = x_ref[at, :].astype(f32) + attended + row(b_out_ref)
        mid_ref[at, :] = middle
        centred, root = centred_rows(middle)
        act = (centred * root * row(gain_ref) + row(bias_ref)).astype(bf16)
        act_ref[at, :] = act
        value, slope = gelu_parts(contract(act, up_ref[...], 1, 0) + row(up_bias_ref))
        hidden = value.astype(bf16)
        hidden_ref[at, :] = hidden
        grads = (contract(gout_ref[at, :], down_ref[...], 1, 1) * slope).astype(bf16)
        grad_ref[at, :] = grads
        bias_sum = bias_sum + jnp.sum(grads.astype(f32), axis=0, keepdims=True)
        backs.append(contract(grads, up_ref[...], 1, 1))
        outs.append(contract(hidden, down_ref[...], 1, 0))
    bias_sum_ref[...] = bias_sum
    put_halves(spot_ref[1], backs[0], backs[1], keep_ref, send_ref)
    put_halves(spot_ref[1], outs[0], outs[1], out_keep_ref, out_send_ref)
    sums = contract(act_ref[...], grad_ref[...], 0, 0)
    half = sums.shape[0] // 2
    put_halves(bit_of(spot_ref, mask_one), sums[:half], sums[half:], w_up_ref, w_up_send_ref)
    sums = contract(hidden_ref[...], gout_ref[...], 0, 0)
    half = sums.shape[0] // 2
    put_halves(bit_of(spot_ref, mask_two), sums[:half], sums[half:], w_down_ref, w_down_send_ref)


def norm_grad(grad, hat, root, gain):
    scaled = grad * gain
    inner = jnp.mean(scaled * hat, axis=-1, keepdims=True)
    return root * (scaled - jnp.mean(scaled, axis=-1, keepdims=True) - hat * inner)


def entry_kernel(
    spot_ref, lengths_ref, own_ref, other_ref, x_ref, gain_ref, gmid_ref, mid_ref, b_down_ref,
    out_ref, rows_ref, layer_ref,
):
    slots, rows, model = layer_ref.shape
    half = own_ref.shape[0] // 2
    first, second = halves_of(spot_ref[1], own_ref, other_ref)
    gain_rows = bias_rows = 0.0
    spot = spot_ref[0] * rows + lax.broadcasted_iota(jnp.int32, (rows, model), 0)
    for s in range(slots):
        at = slice(s * rows, (s + 1) * rows)
        held = first if s * rows < half else second
        inside = s * rows % half
        grad = held[inside : inside + rows]
        feed = held[half + inside : half + inside + rows]
        centred, root = centred_rows(x_ref[at, :].astype(f32))
        hat = centred * root
        out_ref[at, :] = gmid_ref[at, :] + norm_grad(grad, hat, root, row(gain_ref))
        gain_rows = gain_rows + jnp.sum(grad * hat, axis=0, keepdims=True)
        bias_rows = bias_rows + jnp.sum(grad, axis=0, keepdims=True)
        total = mid_ref[at, :] + feed + row(b_down_ref)
        layer_ref[s] = jnp.where(spot < lengths_ref[s], total, 0.0)
    rows_ref[...] = jnp.concatenate(
        [gain_rows, bias_rows, jnp.zeros((SUBS - 2, model), f32)], axis=0
    )


def middle_kernel(
    spot_ref, lengths_ref, own_ref, other_ref, mid_ref, cotangent_ref, gain_ref, w_ref, ssm_ref, q_ref, decay_ref,
    gmid_ref, low_ref, gq_ref, gs_ref, front_ref, front_low_ref, rows_ref,
):
    rows, width = ssm_ref.shape
    chans = w_ref.shape[0]
    gain = row(gain_ref)
    gain_rows = bias_rows = mid_rows = 0.0
    kept = []
    half = own_ref.shape[0]
    first, second = halves_of(spot_ref[1], own_ref, other_ref)
    for s in range(width // chans):
        at = slice(s * rows, (s + 1) * rows)
        inside = slice(s * rows % half, s * rows % half + rows)
        grad = (first if s * rows < half else second)[inside, :]
        centred, root = centred_rows(mid_ref[at, :])
        hat = centred * root
        spot = spot_ref[0] * rows + lax.broadcasted_iota(jnp.int32, hat.shape, 0)
        held = jnp.where(spot < lengths_ref[s], cotangent_ref[s], 0.0)
        grad_mid = held + norm_grad(grad, hat, root, gain)
        gmid_ref[at, :] = grad_mid
        low = grad_mid.astype(bf16)
        low_ref[at, :] = low
        gain_rows = gain_rows + jnp.sum(grad * hat, axis=0, keepdims=True)
        bias_rows = bias_rows + jnp.sum(grad, axis=0, keepdims=True)
        mid_rows = mid_rows + jnp.sum(grad_mid, axis=0, keepdims=True)
        kept.append(contract(low, w_ref[...], 1, 1))
    gated = jnp.concatenate(kept, axis=-1)
    gq_ref[...] = (gated * ssm_ref[...]).astype(bf16)
    gs_ref[...] = gated * q_ref[...]
    rows_ref[...] = jnp.zeros_like(rows_ref)
    rows_ref[0:1, :] = gain_rows
    rows_ref[1:2, :] = bias_rows
    rows_ref[2:3, :] = mid_rows
    run_scan(gs_ref, decay_ref, front_ref, True)
    front_low_ref[...] = front_ref[...].astype(bf16)


def reach_kernel(u_ref, decay_ref, reach_ref):
    blocks = u_ref.shape[0] // SUBS
    for lanes in lane_tiles(u_ref.shape[1]):
        decay = decay_ref[:, lanes]

        def rise(lap, carry, lanes=lanes, decay=decay):
            state, reach = carry
            tile = u_ref[rows_at(lap * SUBS, SUBS), lanes]
            for r in range(SUBS):
                reach = decay * (reach + state)
                state = decay * state + tile[r : r + 1, :]
            return state, reach

        zero = jnp.zeros_like(decay)
        reach_ref[:, lanes] = lax.fori_loop(0, blocks, rise, (zero, zero))[1]


def local_kernel(
    u_ref, gs_ref, decay_ref, weight_ref, start_ref, out_ref, gain_ref, power_ref, part_ref
):
    rows = u_ref.shape[0]
    blocks = rows // SUBS
    for lanes in lane_tiles(u_ref.shape[1]):
        decay = decay_ref[:, lanes]
        weight = weight_ref[:, lanes]

        def fall(lap, carry, lanes=lanes, decay=decay, weight=weight):
            adjoint, slope, gain, power = carry
            place = blocks - 1 - lap
            tile = u_ref[rows_at(place * SUBS, SUBS), lanes]
            grads = gs_ref[rows_at(place * SUBS, SUBS), lanes]
            for r in range(SUBS - 1, -1, -1):
                slope = decay * slope + adjoint
                adjoint = decay * adjoint + grads[r : r + 1, :]
                part_ref[rows_at(place * SUBS * SUBS + r * SUBS, SUBS), :] = folded(weight * adjoint)
                gain = gain + adjoint * tile[r : r + 1, :]
                power = power + slope * tile[r : r + 1, :]
            return adjoint, slope, gain, power

        zero = jnp.zeros_like(decay)
        adjoint, slope, gain, power = lax.fori_loop(0, blocks, fall, (zero, zero, zero, zero))
        gain_ref[:, lanes] = gain
        power_ref[:, lanes] = power + start_ref[:, lanes] * (decay * slope + adjoint)
        out_ref[:, lanes] = part_total(part_ref, rows)


def unmix_kernel(
    mask, spot_ref, gloc_ref, gs_ref, u_ref, decay_ref, weight_ref, whole_ref, got_ref, carry_ref, gain_ref, power_ref, reach_ref, start_ref,
    end_ref, v_ref, shifted_ref, edge_ref, k_ref, taps_ref, shift_skip_ref, ssm_skip_ref,
    in_ref, out_ref, root_ref, slope_ref, fall_ref, a_ref, step_ref,
    gk_ref, halo_ref, gv_ref, small_ref, misc_ref,
    part_ref, ext_ref, pad_ref, wide_ref, sums_ref, tap_ref, behind_ref,
):
    rows, width = u_ref.shape
    blocks = rows // SUBS
    taps, chans = taps_ref.shape
    states = decay_ref.shape[0]
    slots = width // chans
    skip = wide(row(ssm_skip_ref), slots)
    behind_ref[...], _, _ = merged(
        mask, True, spot_ref[0], whole_ref[...], got_ref[...].astype(f32), carry_ref[...]
    )
    ext_ref[0:taps, :] = edge_ref[...].astype(f32)
    ext_ref[taps : taps + rows, :] = k_ref[...].astype(f32)
    pad_ref[0:taps, :] = jnp.zeros((taps, width), f32)
    pad_ref[taps + rows : 2 * taps + rows, :] = jnp.zeros((taps, width), f32)
    wide_ref[0:taps, :] = wide(taps_ref[...], slots)
    wide_ref[taps : taps + 1, :] = wide(row(shift_skip_ref), slots)
    tiles = lane_tiles(width)
    decays = [decay_ref[:, lanes] for lanes in tiles]

    def one(lap, carried):
        place = blocks - 1 - lap
        for r in range(SUBS - 1, -1, -1):
            carried = [d * c for d, c in zip(decays, carried)]
            for k, c in enumerate(carried):
                part_ref[rows_at((k * rows + place * SUBS + r) * SUBS, SUBS), :] = folded(c)
        return carried

    lax.fori_loop(
        0, blocks, one, [weight_ref[:, lanes] * behind_ref[:, lanes] for lanes in tiles]
    )
    for k, lanes in enumerate(tiles):
        grad_u = (
            gloc_ref[:, lanes] + part_total(part_ref, rows, k * rows * SUBS) + skip[:, lanes] * gs_ref[:, lanes]
        )
        gv_ref[:, lanes] = (grad_u * shifted_ref[:, lanes]).astype(bf16)
        pad_ref[taps : taps + rows, lanes] = grad_u * v_ref[:, lanes]
        total = wide_ref[taps : taps + 1, lanes] * pad_ref[taps : taps + rows, lanes]
        borrowed = jnp.zeros((taps, LANES), f32)
        for r in range(SUBS):
            block = pad_ref[r : 2 * taps + rows - SUBS + r, lanes]
            for q in range(taps // SUBS + 1):
                i = SUBS * q + r
                if i < 1 or i > taps:
                    continue
                tap = wide_ref[i - 1 : i, lanes]
                live = min(rows, -(-(rows - i) // SUBS) * SUBS)
                start = taps + SUBS * q
                live = min(live, block.shape[0] - start)
                fresh = total[:live] + tap * block[start : start + live, :]
                total = fresh if live == rows else jnp.concatenate([fresh, total[live:]], axis=0)
                idle = (taps - i) // SUBS * SUBS
                start = SUBS * q + idle
                fresh = borrowed[idle:] + tap * block[start : start + taps - idle, :]
                borrowed = fresh if not idle else jnp.concatenate([borrowed[:idle], fresh], axis=0)
        gk_ref[:, lanes] = total
        halo_ref[:, lanes] = borrowed.astype(bf16)
        grad_shifted = pad_ref[taps : taps + rows, lanes]
        for r in range(SUBS):
            block = ext_ref[r : taps + rows - SUBS + r, lanes] if r else ext_ref[:, lanes]
            for q in range(taps // SUBS + 1):
                start = SUBS * q
                i = taps - start - r
                if i < 0:
                    continue
                product = grad_shifted * block[start : start + rows, :]
                sums_ref[SUBS * i : SUBS * (i + 1), :] = folded(product)
        tap_ref[0 : taps + 1, lanes] = part_total(sums_ref, taps + 1)
    gain = gain_ref[...] + behind_ref[...] * decay_ref[...] * end_ref[...]
    reach = reach_ref[...] + rows * whole_ref[...] * start_ref[...]
    power = power_ref[...] + behind_ref[...] * reach

    def slots_total(array):
        total = slot_of(array, 0, chans)
        for s in range(1, slots):
            total = total + slot_of(array, s, chans)
        return total

    gain, power = slots_total(gain), slots_total(power)
    grad_in = out_ref[...] * gain
    grad_rate = grad_in * slope_ref[...] - fall_ref[...] * power
    tap_sums = slots_total(tap_ref[0 : taps + 1, :])
    small_ref[...] = jnp.concatenate(
        [
            tap_sums[1 : taps + 1, :],
            grad_rate * row(step_ref),
            grad_in * root_ref[...],
            in_ref[...] * gain,
        ],
        axis=-1,
    )
    misc_ref[...] = jnp.zeros_like(misc_ref)
    skip_sums = slots_total(jnp.sum(gs_ref[...] * u_ref[...], axis=0, keepdims=True))
    step_sums = jnp.sum(grad_rate * a_ref[...], axis=0, keepdims=True)
    misc_ref[0:1, :] = jnp.concatenate(
        [tap_sums[0:1, :], skip_sums, step_sums, jnp.zeros_like(skip_sums)], axis=-1
    )


def weights_kernel(gq_ref, act_ref, gated_ref, low_ref, out_ref):
    rows, width = gq_ref.shape
    chans = gated_ref.shape[1]
    query = 0.0
    for s in range(width // chans):
        grads = slot_of(gq_ref[...].astype(f32), s, chans).astype(bf16)
        query = query + contract(grads, act_ref[s * rows : (s + 1) * rows, :], 0, 0)
    out_ref[0:chans, :] = query.astype(bf16)
    out_ref[chans : 2 * chans, :] = contract(gated_ref[...], low_ref[...], 0, 0).astype(bf16)


def last_kernel(
    mask_one, mask_two, spot_ref, out_keep_ref, out_send_ref, gq_ref, gk_ref, received_ref, gv_ref, act_ref, w_ref, early_ref, small_ref, misc_ref,
    rows_ref, up_ref, down_ref, keep_ref, send_ref, one_ref, one_send_ref, two_ref,
    two_send_ref, all_ref,
):
    rows, width = gk_ref.shape
    taps = received_ref.shape[0]
    chans = w_ref.shape[1]
    slots = width // chans
    grad_k = jnp.concatenate(
        [
            gk_ref[0 : rows - taps, :],
            gk_ref[rows - taps : rows, :] + received_ref[...].astype(f32),
        ],
        axis=0,
    ).astype(bf16)
    parts = [gq_ref[...].astype(f32), grad_k.astype(f32), gv_ref[...].astype(f32)]
    sums = [0.0, 0.0, 0.0]
    terms, biases = [], []
    for s in range(slots):
        act = act_ref[s * rows : (s + 1) * rows, :]
        term = 0.0
        for j in range(3):
            grads = slot_of(parts[j], s, chans).astype(bf16)
            term = term + contract(grads, w_ref[j], 1, 0)
            if j:
                sums[j] = sums[j] + contract(grads, act, 0, 0)
        terms.append(term)
    half = slots // 2
    count = out_keep_ref.shape[0]
    put_halves(
        spot_ref[1],
        jnp.concatenate(terms[:half], axis=0),
        jnp.concatenate(terms[half:], axis=0),
        keep_ref.at[0:count, :],
        send_ref.at[0:count, :],
    )
    keep_ref[count:, :] = out_keep_ref[...]
    send_ref[count:, :] = out_send_ref[...]
    for j in range(3):
        total = jnp.sum(parts[j], axis=0, keepdims=True)
        bias = slot_of(total, 0, chans)
        for s in range(1, slots):
            bias = bias + slot_of(total, s, chans)
        biases.append(bias)
    place = 0

    def put(block):
        nonlocal place
        all_ref[place : place + block.shape[0], :] = block.astype(f32)
        place += block.shape[0]

    put(early_ref[...])
    put(sums[1])
    put(sums[2])
    put(small_ref[...])
    put(
        jnp.concatenate(
            [
                misc_ref[0:1, :],
                jnp.concatenate(biases + [jnp.zeros_like(biases[0])], axis=-1),
                rows_ref[0:3, :],
                up_ref[...],
                down_ref[...],
                jnp.zeros((2 * SUBS - 7, misc_ref.shape[1]), f32),
            ],
            axis=0,
        )
    )
    put(jnp.zeros((all_ref.shape[0] - place, misc_ref.shape[1]), f32))
    count = all_ref.shape[0] // 4
    quarters = [all_ref[k * count : (k + 1) * count, :] for k in range(4)]
    put_halves(bit_of(spot_ref, mask_one), quarters[0], quarters[1], one_ref, one_send_ref)
    put_halves(bit_of(spot_ref, mask_two), quarters[2], quarters[3], two_ref, two_send_ref)


def widen_kernel(mask_one, mask_two, spot_ref, up_ref, up_got_ref, down_ref, down_got_ref, one_ref, two_ref):
    for mask, own_ref, got_ref, out_ref in (
        (mask_one, up_ref, up_got_ref, one_ref),
        (mask_two, down_ref, down_got_ref, two_ref),
    ):
        half = own_ref.shape[0]
        first, second = halves_of(bit_of(spot_ref, mask), own_ref, got_ref)
        out_ref[0:half, :] = first
        out_ref[half:, :] = second


def spread_kernel(
    chans, taps, mask_one, mask_two, spot_ref, one_ref, one_got_ref, two_ref, two_got_ref,
    qkv_ref, bias_ref, tap_ref, shift_skip_ref, a_ref, b_ref, c_ref, ssm_skip_ref, step_ref, out_ref,
    gain_ref, norm_bias_ref, out_bias_ref, up_ref, down_ref, entry_gain_ref, entry_bias_ref, all_ref,
):
    quarter = two_ref.shape[0]
    entry = one_ref[quarter:, :].astype(f32) + one_got_ref[quarter:, :].astype(f32)
    entry_gain_ref[...] = entry[0:1, :].reshape(entry.shape[1])
    entry_bias_ref[...] = entry[1:2, :].reshape(entry.shape[1])
    pieces = halves_of(bit_of(spot_ref, mask_one), one_ref.at[0:quarter, :], one_got_ref.at[0:quarter, :])
    pieces += halves_of(bit_of(spot_ref, mask_two), two_ref, two_got_ref)
    for place, piece in enumerate(pieces):
        all_ref[place * quarter : (place + 1) * quarter, :] = piece
    for j, place in enumerate((0, 2, 3)):
        qkv_ref[j] = all_ref[place * chans : (place + 1) * chans, :]
    out_ref[...] = all_ref[chans : 2 * chans, :]
    base = 4 * chans
    small = all_ref[base : base + taps, :]
    for slot, ref in enumerate((tap_ref, a_ref, b_ref, c_ref)):
        ref[...] = slot_of(small, slot, chans)
    base = base + taps
    misc = all_ref[base : base + SUBS, :]
    for slot, ref in enumerate((shift_skip_ref, ssm_skip_ref, step_ref)):
        ref[...] = slot_of(misc[0:1, :], slot, chans).reshape(chans)
    bias_ref[...] = jnp.concatenate([slot_of(misc[1:2, :], j, chans) for j in range(3)], axis=0)
    for place, ref in enumerate((gain_ref, norm_bias_ref, out_bias_ref, up_ref, down_ref)):
        ref[...] = misc[2 + place : 3 + place, :].reshape(misc.shape[1])


def ordered_calls():
    held = [jnp.zeros((SUBS, LANES), f32)]

    def call(kernel, outs, args, scratch=(), us=0.5, limit=24, scalars=0, place=pltpu.VMEM):
        inputs = len(args)

        def body(*refs):
            given, rest = refs[:inputs], refs[inputs + 1 :]
            rest[len(outs)][...] = refs[inputs][...]
            kernel(*given, *rest[: len(outs)], *rest[len(outs) + 1 :])

        size = sum(a.size * a.dtype.itemsize for a in list(args) + list(outs))
        specs = [pl.BlockSpec(memory_space=pltpu.SMEM)] * scalars
        specs += [pl.BlockSpec(memory_space=place)] * (inputs - scalars)
        specs += [pl.BlockSpec(memory_space=pltpu.VMEM)]
        results = pl.pallas_call(
            body,
            in_specs=specs,
            out_shape=tuple(outs) + (like((SUBS, LANES)),),
            scratch_shapes=list(scratch),
            compiler_params=pltpu.CompilerParams(vmem_limit_bytes=limit << 20),
            cost_estimate=pl.CostEstimate(
                flops=int(us * FLOPS_PER_US), bytes_accessed=0, transcendentals=0
            ),
        )(*args, held[0])
        held[0] = results[-1]
        return results[:-1]

    return call


def like(shape, dtype=f32):
    return jax.ShapeDtypeStruct(shape, dtype)


def shards(
    inputs,
    cotangent,
    lengths,
    ln1_gain,
    ln1_bias,
    query_key_value_weight,
    b_qkv,
    shift_taps,
    shift_skip,
    ssm_a,
    ssm_b,
    ssm_c,
    ssm_skip,
    ssm_step,
    output_weight,
    b_out,
    ln2_gain,
    ln2_bias,
    up_weight,
    up_bias,
    down_weight,
    b_down,
):
    slots, rows, model = inputs.shape
    taps, chans = shift_taps.shape
    states = ssm_a.shape[1]
    width = slots * chans
    tokens = slots * rows
    spot = jnp.stack([lax.axis_index("seq"), lax.axis_index("head") % 2]).astype(jnp.int32)
    peers = lax.axis_size("seq")
    last_mask = peers // 2
    half_tokens = tokens // 2
    half_like = like((half_tokens, model), bf16)
    projections = jnp.swapaxes(query_key_value_weight, 1, 2)
    flat_inputs = inputs.reshape(tokens, model)
    hidden_count = up_bias.shape[0]
    masks = [2**k for k in range(peers.bit_length() - 1)]
    orders = (masks, masks[1::-1] + masks[2:])
    ends = tuple(order[0] for order in orders)
    call = ordered_calls()

    rate = (ssm_step[:, None] * ssm_a).T
    decay = jnp.exp(-rate)
    gain_root = jnp.sqrt(-jnp.expm1(-2.0 * rate))
    turned_b, turned_c = ssm_b.T, ssm_c.T
    in_weight = gain_root * turned_b
    decay_wide = wide(decay, slots)
    whole_wide = wide(jnp.exp(-rate * rows), slots)
    weight_wide = wide(turned_c * in_weight, slots)
    slope = turned_b * jnp.exp(-2.0 * rate) / gain_root
    fall = decay * turned_c * in_weight

    act_one, queries, keys, values = call(
        project_kernel,
        [like((tokens, model), bf16), like((rows, width)), like((rows, width), bf16), like((rows, width))],
        [spot] + [
            pltpu.with_memory_space_constraint(a, pltpu.HBM)
            for a in (inputs, ln1_gain, ln1_bias, projections, b_qkv)
        ],
        [
            pltpu.VMEM(inputs.shape, inputs.dtype),
            pltpu.VMEM(ln1_gain.shape, f32),
            pltpu.VMEM(ln1_bias.shape, f32),
            pltpu.VMEM(projections.shape, projections.dtype),
            pltpu.VMEM(b_qkv.shape, f32),
            pltpu.SemaphoreType.DMA((5,)),
        ],
        us=2.0,
        scalars=1,
        place=pltpu.HBM,
        limit=24,
    )
    edge = shifted(keys[rows - taps :, :], "seq", 1)
    shifted_keys, series, end_local, end_low = call(
        mix_kernel,
        [like((rows, width)), like((rows, width)), like((states, width)), like((states, width), bf16)],
        [edge, keys, values, shift_taps, shift_skip, decay_wide],
        [pltpu.VMEM((taps + rows, width), f32), pltpu.VMEM((taps + SUBS, width), f32)],
        us=2.9,
    )
    low_out, grad_b_down = call(
        masked_kernel,
        [like((tokens, model), bf16), like((1, model))],
        [spot, lengths, cotangent],
        us=0.8,
        scalars=2,
    )
    carry, got = plain_carry(end_local, end_low, whole_wide, spot[:1].reshape(1, 1), "seq")
    ssm_out, gated, start_state, keep, send = call(
        functools.partial(attend_kernel, last_mask),
        [like((rows, width)), like((tokens, chans), bf16), like((states, width)), half_like, half_like],
        [
            spot, series, decay_wide, weight_wide, whole_wide, got, carry, ssm_skip, queries,
            output_weight,
        ],
        [pltpu.VMEM((rows * SUBS, LANES), f32)],
        us=2.9,
        scalars=1,
    )
    own, other = plain_head_total(keep, send)
    middle, back_keep, back_send, out_keep, out_send, grad_b_up, up_keep, up_send, down_keep, down_send = call(
        functools.partial(feed_kernel, *ends),
        [
            like((tokens, model)),
            half_like,
            half_like,
            half_like,
            half_like,
            like((1, hidden_count)),
            like((model // 2, hidden_count), bf16),
            like((model // 2, hidden_count), bf16),
            like((hidden_count // 2, model), bf16),
            like((hidden_count // 2, model), bf16),
        ],
        [
            spot, own, other, flat_inputs, b_out, ln2_gain, ln2_bias, up_weight, up_bias, down_weight,
            low_out,
        ],
        [
            pltpu.VMEM((tokens, model), bf16),
            pltpu.VMEM((tokens, hidden_count), bf16),
            pltpu.VMEM((tokens, hidden_count), bf16),
        ],
        us=5.0,
        scalars=1,
        limit=32,
    )
    low_middle = early = last_parts = entry_parts = grad_inputs = layer_out = None
    sum_up = sum_down = last_rows = grad_queries = None

    def feed_work():
        nonlocal sum_up, sum_down
        feed_joined = yield from halving_steps(
            call, [(up_keep, up_send), (down_keep, down_send)], orders, spot, "seq"
        )
        sum_up, sum_down = call(
            functools.partial(widen_kernel, *ends),
            [like((model, hidden_count)), like((hidden_count, model))],
            [spot, *feed_joined],
            scalars=1,
            us=2.5,
        )

    def early_work():
        nonlocal early
        while low_middle is None:
            yield
        (early,) = call(
            weights_kernel,
            [like((2 * chans, model), bf16)],
            [grad_queries, act_one, gated, low_middle],
            us=0.5,
        )

    def last_work():
        while last_parts is None:
            yield
        one, one_send, two, two_send = last_parts

        def extra():
            while entry_parts is None:
                step("m")
            return entry_parts

        return (
            yield from halving_steps(
                call, [(one, one_send), (two, two_send)], orders, spot, "seq", extra
            )
        )

    def main_work():
        nonlocal low_middle, grad_queries, last_parts, entry_parts, grad_inputs, layer_out, last_rows
        joins = head_steps(call, back_keep, back_send)
        next(joins)
        yield
        next(joins)
        (reach,) = call(
            reach_kernel, [like((states, width))], [series, decay_wide], us=2.0
        )
        yield
        own, other = ran(joins)
        grad_middle, low_middle, grad_queries, grad_ssm, front_local, front_low, norm_rows = call(
            middle_kernel,
            [
                like((tokens, model)),
                like((tokens, model), bf16),
                like((rows, width), bf16),
                like((rows, width)),
                like((states, width)),
                like((states, width), bf16),
                like((SUBS, model)),
            ],
            [
                spot, lengths, own, other, middle, cotangent, ln2_gain, output_weight, ssm_out, queries,
                decay_wide,
            ],
            us=3.00,
            scalars=2,
        )
        yield
        steps = carry_steps(call, front_local, front_low, whole_wide, spot, "seq", True)
        carry, got = yield from steps
        grad_local, gain_local, power_local = call(
            local_kernel,
            [like((rows, width)), like((states, width)), like((states, width))],
            [series, grad_ssm, decay_wide, weight_wide, start_state],
            [pltpu.VMEM((rows * SUBS, LANES), f32)],
            us=4.8,
        )
        yield
        grad_keys, halo, grad_values, small, misc = call(
            functools.partial(unmix_kernel, last_mask),
            [
                like((rows, width)),
                like((taps, width), bf16),
                like((rows, width), bf16),
                like((states, 4 * chans)),
                like((SUBS, 4 * chans)),
            ],
            [
                spot, grad_local, grad_ssm, series, decay_wide, weight_wide, whole_wide, got, carry,
                gain_local, power_local, reach, start_state, end_local, values, shifted_keys, edge, keys, shift_taps,
                shift_skip, ssm_skip, in_weight, turned_c, gain_root, slope, fall, ssm_a.T, ssm_step,
            ],
            [
                pltpu.VMEM((width * rows * SUBS // LANES, LANES), f32),
                pltpu.VMEM((taps + rows, width), f32),
                pltpu.VMEM((2 * taps + rows, width), f32),
                pltpu.VMEM((taps + SUBS, width), f32),
                pltpu.VMEM(((taps + 1) * SUBS, LANES), f32),
                pltpu.VMEM((taps + SUBS, width), f32),
                pltpu.VMEM((states, width), f32),
            ],
            us=6.0,
            scalars=1,
        )
        received = shifted(halo, "seq", -1)
        yield
        while early is None:
            step("E")
        unit = 2 * peers * SUBS
        last_rows = -(-(4 * chans + states + 2 * SUBS) // unit) * unit
        quarter = like((last_rows // 4, model), bf16)
        keep, send, one, one_send, two, two_send = call(
            functools.partial(last_kernel, *ends),
            [like((tokens, model), bf16)] * 2 + [quarter, quarter, quarter, quarter],
            [
                spot, out_keep, out_send, grad_queries, grad_keys, received, grad_values, act_one, projections, early, small,
                misc, norm_rows, grad_b_up, grad_b_down,
            ],
            [pltpu.VMEM((last_rows, model), f32)],
            us=4.50,
            scalars=1,
        )
        last_parts = (one, one_send, two, two_send)
        step("L")
        own, other = yield from head_steps(call, keep, send)
        yield
        grad_inputs, rows_sum, layer_out = call(
            entry_kernel,
            [like((tokens, model)), like((SUBS, model)), like(inputs.shape)],
            [spot, lengths, own, other, flat_inputs, ln1_gain, grad_middle, middle, b_down],
            scalars=2,
            us=3.0,
        )
        entry_parts = rows_sum

    works = {"m": main_work(), "M": feed_work(), "E": early_work(), "L": last_work()}
    ended = {}

    def step(name):
        if name not in ended:
            try:
                next(works[name])
            except StopIteration as end:
                ended[name] = end.value

    step("M")
    for name in ORDER:
        step(name)
    for name in "mML":
        while name not in ended:
            step(name)
    joined = ended["L"]
    spread = call(
        functools.partial(spread_kernel, chans, taps, *ends),
        [
            like((3, chans, model)),
            like((3, chans)),
            like((taps, chans)),
            like((chans,)),
            like((states, chans)),
            like((states, chans)),
            like((states, chans)),
            like((chans,)),
            like((chans,)),
            like((chans, model)),
            like((model,)),
            like((model,)),
            like((model,)),
            like(up_bias.shape),
            like((model,)),
            like((model,)),
            like((model,)),
        ],
        [spot, *joined],
        [pltpu.VMEM((last_rows, model), f32)],
        scalars=1,
        us=2.0,
    )
    (
        sum_qkv, sum_b_qkv, sum_taps, sum_shift_skip, sum_a, sum_b, sum_c, sum_ssm_skip, sum_step,
        sum_out, sum_ln2_gain, sum_ln2_bias, sum_b_out, sum_b_up, sum_b_down,
        sum_ln1_gain, sum_ln1_bias,
    ) = spread
    return (
        layer_out,
        grad_inputs.reshape(inputs.shape),
        sum_ln1_gain,
        sum_ln1_bias,
        jnp.swapaxes(sum_qkv, 1, 2),
        sum_b_qkv,
        sum_taps,
        sum_shift_skip,
        sum_a.T,
        sum_b.T,
        sum_c.T,
        sum_ssm_skip,
        sum_step,
        sum_out,
        sum_b_out,
        sum_ln2_gain,
        sum_ln2_bias,
        sum_up,
        sum_b_up,
        sum_down,
        sum_b_down,
    )


def solution(mesh):
    in_specs = (
        P(None, "seq", None),
        P(None, "seq", None),
        P(),
        P(),
        P(),
        P(None, None, "head"),
        P(None, "head"),
        P(None, "head"),
        P("head"),
        P("head", None),
        P("head", None),
        P("head", None),
        P("head"),
        P("head"),
        P("head", None),
        P(),
        P(),
        P(),
        P(None, "head"),
        P("head"),
        P("head", None),
        P(),
    )
    out_specs = (
        P(None, "seq", None),
        P(None, "seq", None),
        P(),
        P(),
        P(None, None, "head"),
        P(None, "head"),
        P(None, "head"),
        P("head"),
        P("head", None),
        P("head", None),
        P("head", None),
        P("head"),
        P("head"),
        P("head", None),
        P(),
        P(),
        P(),
        P(None, "head"),
        P("head"),
        P("head", None),
        P(),
    )
    return jax.shard_map(shards, mesh=mesh, in_specs=in_specs, out_specs=out_specs, check_vma=False)
```
